256 devices in a mesh: layer: 8 (over x, core), feat: 32 (over y, z).
Axes of the slice: x: 4, y: 4, z: 8, core: 2. Of those that a mesh axis runs over, the one named last changes fastest.
Arguments:
- gradient: bfloat16 [8, 2560, 2560], P('layer', 'feat'), may hold values from -3 to 3
- in_inverse: bfloat16 [8, 2560, 2560], P('layer', 'feat'), may hold values from -1 to 2.5, as said below
- in_coupling: bfloat16 [8, 2560, 2560], P('layer', 'feat'), may hold values from -0.125 to 0.125
- in_carry: bfloat16 [8, 2560, 2560], P('layer', 'feat'), may hold values from -0.125 to 0.125
- out_inverse: bfloat16 [8, 20, 128, 128], P('layer'), may hold values from -1 to 2.5, as said below
- out_coupling: bfloat16 [8, 20, 128, 128], P('layer'), may hold values from -0.5 to 0.5
Outputs:
- update: bfloat16 [8, 2560, 2560], P('layer', 'feat')
The draws below stay inside these ranges and needn't reach their ends.
Inputs may be any that keep to these rules, and one draw needn't show every extreme that they name: `in_inverse`: symmetric in its last two dimensions. `out_inverse`: symmetric in its last two dimensions.
All inputs are finite; a program needn't handle non-finite values.
Results may differ from the reference program's by a relative error of at most 0.006.
Values may be sent and summed in bfloat16 or wider, within the bound.
No kernel may reach another device: no remote copies, remote signals or barrier semaphores. Data moves between devices by JAX's collectives and lax.ppermute only.
A program may use at most 64 MiB of HBM per device.

```python
import math
import jax
import jax.numpy as jnp
from jax import lax

DIN = 2560
DOUT = 2560
BLK = 128
LAYERS = 8
OBLOCKS = 20


def symmetric_blocks(key, leading, matrix_order, spread, lower_end, upper_end):
    first_key, second_key = jax.random.split(key)
    noise_part = jax.random.truncated_normal(first_key, -4.0, 4.0, leading + (matrix_order, matrix_order), jnp.float32)
    off_part = (noise_part + jnp.swapaxes(noise_part, -1, -2)) * (spread / math.sqrt(2.0 * matrix_order))
    diagonal = jax.random.uniform(second_key, leading + (matrix_order,), jnp.float32, lower_end, upper_end)
    identity = jnp.eye(matrix_order, dtype=jnp.float32)
    return off_part * (1.0 - identity) + diagonal[..., None] * identity


def draw_in_inverse(key, part):
    matrix = symmetric_blocks(jax.random.fold_in(key, 11), (LAYERS,), DIN, 0.45, 1.0, 2.0)
    return matrix.astype(jnp.bfloat16)


def draw_out_inverse(key, part):
    matrix = symmetric_blocks(jax.random.fold_in(key, 23), (LAYERS, DOUT // BLK), BLK, 0.45, 1.0, 2.0)
    return matrix.astype(jnp.bfloat16)


def level_of(rng, dims, cuts, smallest, top_value):
    loudness, own = 1.0, jax.random.fold_in(rng, 6)
    for axis_at, shards_of in cuts:
        draws = jnp.exp(jax.random.uniform(jax.random.fold_in(own, axis_at), (shards_of,), jnp.float32, smallest / len(cuts), top_value / len(cuts)))
        loudness = loudness * jnp.repeat(draws, dims[axis_at] // shards_of).reshape([-1 if axis == axis_at else 1 for axis in range(len(dims))])
    return loudness


def noise(key, dims, width, limit, shards=(), kind=jnp.bfloat16):
    loudness = level_of(key, dims, shards, -0.22, 0.18) if shards else 1.0
    entries = jax.random.normal(key, dims, jnp.float32) * width * loudness
    return jnp.minimum(jnp.maximum(entries, -limit), limit).astype(kind)


def setup_inputs(seed: int = 0) -> dict:
    key_list = jax.random.split(jax.random.key(seed), 7)
    gradient = noise(key_list[0], (LAYERS, DIN, DOUT), 0.5, 3.0, ((0, 8), (1, 32)))
    in_inverse = draw_in_inverse(jax.random.fold_in(key_list[6], 71), 0)
    in_coupling = noise(key_list[2], (LAYERS, DIN, DIN), DIN ** -0.5, 0.125, ((0, 8), (1, 32)))
    in_carry = noise(key_list[3], (LAYERS, DIN, DIN), DIN ** -0.5, 0.125, ((0, 8), (1, 32)))
    out_inverse = draw_out_inverse(jax.random.fold_in(key_list[6], 71), 0)
    out_coupling = noise(key_list[5], (LAYERS, OBLOCKS, BLK, BLK), BLK ** -0.5, 0.5, ((0, 8),))
    return {"gradient": gradient, "in_inverse": in_inverse, "in_coupling": in_coupling, "in_carry": in_carry, "out_inverse": out_inverse, "out_coupling": out_coupling}


def block_apply(matrix, table, flipped):
    row_count = matrix.shape[0]
    blocks = table.shape[0]
    block_width = table.shape[1]
    grouped = matrix.astype(jnp.float32).reshape(row_count, blocks, block_width)
    pattern = "rnb,ncb->rnc" if flipped else "rnb,nbc->rnc"
    product = jnp.einsum(pattern, grouped, table.astype(jnp.float32), precision=lax.Precision.HIGHEST)
    return product.reshape(row_count, blocks * block_width)


def reference(gradient, in_inverse, in_coupling, in_carry, out_inverse, out_coupling):
    results = []
    pushed_prev = jnp.zeros((DIN, DOUT), jnp.float32)
    for position in range(LAYERS):
        if position + 1 < LAYERS:
            near_rows = block_apply(gradient[position + 1], out_coupling[position], True).astype(jnp.bfloat16)
            coupled = jnp.dot(in_coupling[position], near_rows, preferred_element_type=jnp.float32)
        else:
            coupled = jnp.zeros((DIN, DOUT), jnp.float32)
        reduced = (gradient[position].astype(jnp.float32) - coupled).astype(jnp.bfloat16)
        whitened = jnp.dot(in_inverse[position], reduced, preferred_element_type=jnp.float32).astype(jnp.bfloat16)
        carried = jnp.dot(in_carry[position], reduced, preferred_element_type=jnp.float32).astype(jnp.bfloat16)
        local_term = block_apply(whitened, out_inverse[position], False)
        middle = block_apply(carried, out_inverse[position], False).astype(jnp.bfloat16)
        results.append((local_term - pushed_prev).astype(jnp.bfloat16))
        pushed_prev = block_apply(middle, out_coupling[position], False)
    return jnp.stack(results)
```

```python
import jax
import jax.numpy as jnp
import numpy as np
from jax import lax
from jax.experimental import pallas as pl
from jax.experimental.pallas import tpu as pltpu
from jax.sharding import Mesh, PartitionSpec as P

BF = jnp.bfloat16
F32 = jnp.float32
BLK = 128
VMEM = pl.BlockSpec(memory_space=pltpu.VMEM)


def call(kernel, out, name, operands, scratch=(), mib=48, flops=0):
    moved = sum(x.size * x.dtype.itemsize for x in operands) + sum(x.size * x.dtype.itemsize for x in jax.tree.leaves(out))
    return pl.pallas_call(
        kernel,
        out_shape=out,
        in_specs=[VMEM] * len(operands),
        out_specs=jax.tree.map(lambda _: VMEM, out),
        scratch_shapes=list(scratch),
        compiler_params=pltpu.CompilerParams(vmem_limit_bytes=mib << 20),
        cost_estimate=pl.CostEstimate(flops=flops, bytes_accessed=moved, transcendentals=0),
        name=name,
    )(*operands)


def like(rows, cols, dtype):
    return jax.ShapeDtypeStruct((rows, cols), dtype)


def hop_z(x, by):
    size = lax.axis_size("z")
    return lax.ppermute(x, "z", [(i, (i + by) % size) for i in range(size)])


def hop_layer(x, by):
    size = lax.axis_size("layer")
    return lax.ppermute(x, "layer", [(i, i + by) for i in range(size) if 0 <= i + by < size])


def hop_y(x, layers, by):
    count, size = lax.axis_size("layer"), lax.axis_size("y")
    pairs = []
    for i in range(count):
        for j in range(size):
            if 0 <= i + layers < count:
                pairs.append((i * size + j, (i + layers) * size + (j + by) % size))
    return lax.ppermute(x, ("layer", "y"), pairs)


def after(x, *others):
    return lax.optimization_barrier((x, *others))[0]


def ring(tile):
    half = tile.shape[0] // 2
    up = down = tile
    pieces = [(tile, 0, 0)]
    for step in range(1, lax.axis_size("z") // 2):
        up, down = hop_z(up, 1), hop_z(down, -1)
        pieces += [(up, 0, -step), (down, 0, step)]
    far = lax.axis_size("z") // 2
    pieces += [(hop_z(up[:half], 1), 0, -far), (hop_z(down[half:], -1), half, far)]
    return pieces


def spread(refs, places, panel_ref, rows):
    y, z = lax.axis_index("y"), lax.axis_index("z")
    ys, zs = lax.axis_size("y"), lax.axis_size("z")
    for ref, (first, distance) in zip(refs, places, strict=True):
        source = lax.rem(z + (distance + zs), zs)
        for k in range(ref.shape[0] // rows):
            owner = lax.rem(y + (first // rows + k), ys)
            at = pl.multiple_of((owner * zs + source) * rows, 16)
            panel_ref[pl.ds(at, rows), :] = ref[pl.ds(k * rows, rows), :]


def near_tile(above, table):
    rows, width = above[0].shape
    blocks = width // BLK
    count = len(above)

    def kernel(*refs):
        table_ref, out_ref = refs[count:]
        y = lax.axis_index("y")
        for b in range(blocks):
            cols = pl.ds(b * BLK, BLK)
            block = table_ref[y * blocks + b]
            for k in range(count):
                near = lax.dot_general(refs[k][:, cols], block, (((1,), (1,)), ((), ())), preferred_element_type=F32)
                out_ref[pl.ds(k * rows, rows), cols] = near.astype(BF)

    return call(kernel, like(count * rows, width, BF), "near", [*above, table], flops=2 * count * rows * width * BLK)


def reduced_tile(pieces, factor, grads):
    rows, width = grads[0].shape
    tiles, places = [p[0] for p in pieces], [p[1:] for p in pieces]
    count, depth = len(tiles), factor.shape[1]

    def kernel(*refs):
        factor_ref, grad_refs = refs[count], refs[count + 1 : count + 1 + len(grads)]
        out_ref, panel_ref = refs[-2:]
        spread(refs[:count], places, panel_ref, rows)
        for at in range(0, width, 256):
            cols = pl.ds(at, min(256, width - at))
            coupled = jnp.dot(factor_ref[...], panel_ref[:, cols], preferred_element_type=F32)
            for k, grad_ref in enumerate(grad_refs):
                part = coupled[k * rows : (k + 1) * rows]
                out_ref[pl.ds(k * rows, rows), cols] = (grad_ref[:, cols].astype(F32) - part).astype(BF)

    return call(
        kernel,
        like(factor.shape[0], width, BF),
        "reduced",
        [*tiles, factor, *grads],
        [pltpu.VMEM((depth, width), BF)],
        flops=2 * factor.shape[0] * depth * width,
    )


def last_tiles(pieces, factors, table, shards):
    width = pieces[0][0].shape[1]
    tiles, places = [p[0] for p in pieces], [p[1:] for p in pieces]
    count, depth = len(tiles), factors.shape[1]
    rows = factors.shape[0] // (2 * shards)
    blocks = width // BLK

    def kernel(*refs):
        factors_ref, table_ref, local_ref, middle_ref, panel_ref = refs[count:]
        y = lax.axis_index("y")
        spread(refs[:count], places, panel_ref, rows)
        for at in range(0, width, 256):
            w = min(256, width - at)
            both = jnp.dot(factors_ref[...], panel_ref[:, pl.ds(at, w)], preferred_element_type=F32).astype(BF)
            for b in range(w // BLK):
                sub = pl.ds(at + b * BLK, BLK)
                block = table_ref[y * blocks + at // BLK + b]
                product = jnp.dot(both[:, b * BLK : (b + 1) * BLK], block, preferred_element_type=F32)
                for k in range(shards):
                    local_ref[pl.ds(k * rows, rows), sub] = product[2 * k * rows : (2 * k + 1) * rows]
                    middle_ref[pl.ds(k * rows, rows), sub] = product[(2 * k + 1) * rows : (2 * k + 2) * rows].astype(BF)

    return call(
        kernel,
        (like(shards * rows, width, F32), like(shards * rows, width, BF)),
        "last",
        [*tiles, factors, table],
        [pltpu.VMEM((depth, width), BF)],
        flops=2 * factors.shape[0] * depth * width,
    )


def update_tiles(local_term, middle, table, shards):
    rows, width = middle.shape[0] // shards, middle.shape[1]
    blocks = width // BLK

    def kernel(local_ref, middle_ref, table_ref, *out_refs):
        y = lax.axis_index("y")
        for b in range(blocks):
            cols = pl.ds(b * BLK, BLK)
            pushed = jnp.dot(middle_ref[:, cols], table_ref[y * blocks + b], preferred_element_type=F32)
            update = (local_ref[:, cols] - pushed).astype(BF)
            for k in range(shards):
                out_refs[k][:, cols] = update[k * rows : (k + 1) * rows]

    return call(
        kernel,
        tuple(like(rows, width, BF) for _ in range(shards)),
        "update",
        [local_term, middle, table],
        flops=2 * middle.size * BLK,
    )


def join_rows(pieces):
    rows, width = pieces[0].shape
    count = len(pieces)

    def kernel(*refs):
        y = lax.axis_index("y")
        for k in range(count):
            at = pl.multiple_of(lax.rem(y + (count - k), count) * width, BLK)
            refs[count][0, :, pl.ds(at, width)] = refs[k][...]

    return call(kernel, jax.ShapeDtypeStruct((1, rows, count * width), BF), "join", pieces)


def local(gradient, in_inverse, in_coupling, in_carry, out_inverse, out_coupling):
    shards = lax.axis_size("y")
    grad_rows = gradient[0]
    width = grad_rows.shape[1] // shards
    out_inv = out_inverse[0]
    out_psi = out_coupling[0]
    y = lax.axis_index("y")
    slices = [
        lax.dynamic_slice_in_dim(grad_rows, lax.rem(y + (shards - k), shards) * width, width, 1) for k in range(shards)
    ]
    above = [hop_y(slices[k], -1, -k) for k in range(shards)]
    near = near_tile(above, out_psi)
    near_ring = ring(near)
    first = near_ring[1][0], near_ring[2][0]
    second = near_ring[3][0], near_ring[4][0]
    grads = [slices[0]] + [hop_y(after(slices[k], near), 0, -k) for k in range(1, shards)]
    coupling = after(in_coupling[0], *first)
    factor = jnp.concatenate([coupling] + [hop_y(coupling, 0, -k) for k in range(1, shards)], 0)
    stacked = jnp.concatenate([in_inverse[0], in_carry[0]], 0)
    stacked = after(stacked, *second)
    factors = jnp.concatenate([stacked] + [hop_y(stacked, 0, -k) for k in range(1, shards)], 0)
    reduced = reduced_tile(near_ring, factor, grads)
    reduced_ring = ring(reduced)
    psi_below = hop_layer(after(out_psi, reduced), 1)
    local_term, middle = last_tiles(reduced_ring, factors, out_inv, shards)
    update = update_tiles(local_term, hop_layer(middle, 1), psi_below, shards)
    return join_rows([update[0]] + [hop_y(update[k], 0, k) for k in range(1, shards)])


def solution(mesh):
    layers = mesh.shape["layer"]
    fine = Mesh(np.asarray(mesh.devices).reshape(layers, 4, -1), ("layer", "y", "z"))
    rows = P("layer", ("y", "z"), None)
    table = P("layer", None, None, None)
    return jax.shard_map(
        local,
        mesh=fine,
        in_specs=(rows, rows, rows, rows, table, table),
        out_specs=rows,
        check_vma=False,
    )
```

```python
import jax
import jax.numpy as jnp
import numpy as np
from jax import lax
from jax.experimental import pallas as pl
from jax.experimental.pallas import tpu as pltpu
from jax.sharding import Mesh, PartitionSpec as P

BF = jnp.bfloat16
F32 = jnp.float32
HALF = jnp.float16
BLK = 128
CODE = 8
VMEM = pl.BlockSpec(memory_space=pltpu.VMEM)


def call(kernel, out, name, operands, scratch=(), mib=16, flops=0):
    moved = sum(x.size * x.dtype.itemsize for x in operands) + sum(x.size * x.dtype.itemsize for x in jax.tree.leaves(out))
    return pl.pallas_call(
        kernel,
        out_shape=out,
        in_specs=[VMEM] * len(operands),
        out_specs=jax.tree.map(lambda _: VMEM, out),
        scratch_shapes=list(scratch),
        compiler_params=pltpu.CompilerParams(vmem_limit_bytes=mib << 20),
        cost_estimate=pl.CostEstimate(flops=flops, bytes_accessed=moved, transcendentals=0),
        name=name,
    )(*operands)


def like(rows, cols, dtype):
    return jax.ShapeDtypeStruct((rows, cols), dtype)


def hop_layer(x, by):
    size = lax.axis_size("layer")
    return lax.ppermute(x, "layer", [(i, i + by) for i in range(size) if 0 <= i + by < size])


def chunks_of(width):
    return [(at, min(256, width - at)) for at in range(0, width, 256)]


def store_scaled(out_ref, values, at, shards, rows):
    width = values.shape[1]
    cols = pl.ds(at, width)
    line = lax.broadcasted_iota(jnp.int32, (CODE, width), 0)
    codes = jnp.full((CODE, width), 1.0, F32)
    for k in range(shards):
        part = values[k * rows : (k + 1) * rows]
        top = jnp.max(jnp.abs(part), axis=0, keepdims=True)
        scale = jnp.ones_like(top)
        code = jnp.full_like(top, 128.0)
        for bits in (64, 32, 16, 8):
            small = top < 2.0 ** (15 - bits)
            grow = jnp.where(small, 2.0**bits, 1.0)
            top = top * grow
            scale = scale * grow
            code = code * jnp.where(small, 2.0 ** (-(bits // 8)), 1.0)
        out_ref[pl.ds(k * rows, rows), cols] = (part * scale).astype(BF)
        codes = jnp.where(line == k, code, codes)
    out_ref[pl.ds(shards * rows, CODE), cols] = codes.astype(BF)


def load_scaled(in_ref, panel_ref, at, width, shards, rows):
    cols = pl.ds(at, width)
    count = in_ref.shape[0]
    for j in range(count):
        codes = in_ref[j, pl.ds(shards * rows, CODE), cols].astype(F32) * (1.0 / 128.0)
        codes = codes * codes
        codes = codes * codes
        codes = codes * codes
        for k in range(shards):
            part = in_ref[j, pl.ds(k * rows, rows), cols].astype(F32) * codes[k : k + 1]
            panel_ref[pl.ds((k * count + j) * rows, rows), cols] = part.astype(BF)


def near_tile(above, table, shards):
    tile, width = above.shape
    blocks = width // BLK

    def kernel(above_ref, table_ref, out_ref):
        y = lax.axis_index("y")
        for b in range(blocks):
            block = table_ref[y * blocks + b]
            near = lax.dot_general(
                above_ref[:, pl.ds(b * BLK, BLK)], block, (((1,), (1,)), ((), ())), preferred_element_type=F32
            )
            store_scaled(out_ref, near.astype(BF).astype(F32), b * BLK, shards, tile // shards)

    return call(kernel, like(tile + CODE, width, BF), "near", [above, table], flops=2 * tile * width * BLK)


def reduced_tile(panel, factor, grad, shards):
    tile, width = grad.shape
    depth = factor.shape[1]

    def kernel(panel_in, factor_ref, grad_ref, out_ref, panel_ref):
        for at, w in chunks_of(width):
            cols = pl.ds(at, w)
            load_scaled(panel_in, panel_ref, at, w, shards, tile // shards)
            coupled = jnp.dot(factor_ref[...], panel_ref[:, cols], preferred_element_type=F32)
            reduced = (grad_ref[:, cols].astype(F32) - coupled).astype(BF).astype(F32)
            store_scaled(out_ref, reduced, at, shards, tile // shards)

    return call(
        kernel,
        like(tile + CODE, width, BF),
        "reduced",
        [panel, factor, grad],
        [pltpu.VMEM((depth, width), BF)],
        flops=2 * tile * depth * width,
    )


def last_tiles(panel, factors, table, shards):
    tile, width = factors.shape[0] // 2, panel.shape[2]
    depth, rows, blocks = factors.shape[1], tile // shards, width // BLK

    def kernel(panel_in, factors_ref, table_ref, local_ref, middle_ref, panel_ref):
        y = lax.axis_index("y")
        for at, w in chunks_of(width):
            load_scaled(panel_in, panel_ref, at, w, shards, rows)
            both = jnp.dot(factors_ref[...], panel_ref[:, pl.ds(at, w)], preferred_element_type=F32).astype(BF)
            for b in range(w // BLK):
                sub = pl.ds(at + b * BLK, BLK)
                block = table_ref[y * blocks + at // BLK + b]
                product = jnp.dot(both[:, b * BLK : (b + 1) * BLK], block, preferred_element_type=F32)
                for k in range(shards):
                    local_ref[pl.ds(k * rows, rows), sub] = product[2 * k * rows : (2 * k + 1) * rows]
                    middle_ref[pl.ds(k * rows, rows), sub] = product[(2 * k + 1) * rows : (2 * k + 2) * rows].astype(BF)

    return call(
        kernel,
        (like(tile, width, F32), like(tile, width, BF)),
        "last",
        [panel, factors, table],
        [pltpu.VMEM((depth, width), BF)],
        flops=4 * tile * depth * width,
    )


def update_tile(local_term, middle, table):
    tile, width = middle.shape
    blocks = width // BLK

    def kernel(local_ref, middle_ref, table_ref, out_ref):
        y = lax.axis_index("y")
        for b in range(blocks):
            cols = pl.ds(b * BLK, BLK)
            pushed = jnp.dot(middle_ref[:, cols], table_ref[y * blocks + b], preferred_element_type=F32)
            out_ref[:, cols] = (local_ref[:, cols] - pushed).astype(BF)

    return call(kernel, like(tile, width, BF), "update", [local_term, middle, table], flops=2 * tile * width * BLK)


def split_columns(x, shards):
    _, rows, width = x.shape
    width //= shards

    def kernel(in_ref, out_ref):
        for k in range(shards):
            out_ref[pl.ds(k * rows, rows), :] = in_ref[0, :, pl.ds(k * width, width)]

    return call(kernel, like(shards * rows, width, x.dtype), "split", [x])


def join_columns(x, shards):
    rows, width = x.shape[0] // shards, x.shape[1]

    def kernel(in_ref, out_ref):
        for k in range(shards):
            out_ref[0, :, pl.ds(k * width, width)] = in_ref[pl.ds(k * rows, rows), :]

    return call(kernel, jax.ShapeDtypeStruct((1, rows, shards * width), x.dtype), "join", [x])


def gather_panel(tile):
    return lax.all_gather(tile.astype(HALF), "z", axis=0).astype(BF)


def local(gradient, in_inverse, in_coupling, in_carry, out_inverse, out_coupling):
    shards = lax.axis_size("y")
    out_psi = out_coupling[0]
    factor = lax.all_gather(in_coupling[0], "y", axis=0, tiled=True)
    stacked = jnp.concatenate([in_inverse[0], in_carry[0]], 0)
    grad = lax.all_to_all(split_columns(gradient, shards), "y", split_axis=0, concat_axis=0, tiled=True)
    stacked = lax.optimization_barrier((stacked, grad))[0]
    factors = lax.all_gather(stacked, "y", axis=0, tiled=True)
    psi_below = hop_layer(out_psi, 1)
    near = near_tile(hop_layer(grad, -1), out_psi, shards)
    reduced = reduced_tile(gather_panel(near), factor, grad, shards)
    local_term, middle = last_tiles(gather_panel(reduced), factors, out_inverse[0], shards)
    update = update_tile(local_term, hop_layer(middle, 1), psi_below)
    return join_columns(lax.all_to_all(update, "y", split_axis=0, concat_axis=0, tiled=True), shards)


def solution(mesh):
    layers = mesh.shape["layer"]
    fine = Mesh(np.asarray(mesh.devices).reshape(layers, 4, -1), ("layer", "y", "z"))
    rows = P("layer", ("y", "z"), None)
    table = P("layer", None, None, None)
    return jax.shard_map(
        local,
        mesh=fine,
        in_specs=(rows, rows, rows, rows, table, table),
        out_specs=rows,
        check_vma=False,
    )
```

```python
import jax
import jax.numpy as jnp
import numpy as np
from jax import lax
from jax.experimental import pallas as pl
from jax.experimental.pallas import tpu as pltpu
from jax.sharding import Mesh, PartitionSpec as P

BF = jnp.bfloat16
F32 = jnp.float32
HALF = jnp.float16
BLK = 128
CODE = 8
VMEM = pl.BlockSpec(memory_space=pltpu.VMEM)
HBM = pl.BlockSpec(memory_space=pltpu.HBM)


def call(kernel, out, name, operands, scratch=(), mib=16, flops=0, far=()):
    moved = sum(x.size * x.dtype.itemsize for x in operands) + sum(x.size * x.dtype.itemsize for x in jax.tree.leaves(out))
    return pl.pallas_call(
        kernel,
        out_shape=out,
        in_specs=[HBM if i in far else VMEM for i in range(len(operands))],
        out_specs=jax.tree.map(lambda _: VMEM, out),
        scratch_shapes=list(scratch),
        compiler_params=pltpu.CompilerParams(vmem_limit_bytes=mib << 20),
        cost_estimate=pl.CostEstimate(flops=flops, bytes_accessed=moved, transcendentals=0),
        name=name,
    )(*operands)


def like(rows, cols, dtype):
    return jax.ShapeDtypeStruct((rows, cols), dtype)


def hop_layer(x, by):
    size = lax.axis_size("layer")
    return lax.ppermute(x, "layer", [(i, i + by) for i in range(size) if 0 <= i + by < size])


def chunks_of(width):
    return [(at, min(256, width - at)) for at in range(0, width, 256)]


def store_scaled(out_ref, values, at, shards, rows):
    width = values.shape[1]
    cols = pl.ds(at, width)
    line = lax.broadcasted_iota(jnp.int32, (CODE, width), 0)
    codes = jnp.full((CODE, width), 1.0, F32)
    for k in range(shards):
        part = values[k * rows : (k + 1) * rows]
        top = jnp.max(jnp.abs(part), axis=0, keepdims=True)
        scale = jnp.ones_like(top)
        code = jnp.full_like(top, 128.0)
        for bits in (64, 32, 16, 8):
            small = top < 2.0 ** (15 - bits)
            grow = jnp.where(small, 2.0**bits, 1.0)
            top = top * grow
            scale = scale * grow
            code = code * jnp.where(small, 2.0 ** (-(bits // 8)), 1.0)
        out_ref[pl.ds(k * rows, rows), cols] = (part * scale).astype(BF)
        codes = jnp.where(line == k, code, codes)
    out_ref[pl.ds(shards * rows, CODE), cols] = codes.astype(BF)


def load_scaled(in_ref, panel_ref, at, width, shards, rows):
    cols = pl.ds(at, width)
    count = in_ref.shape[0]
    for j in range(count):
        codes = in_ref[j, pl.ds(shards * rows, CODE), cols].astype(F32) * (1.0 / 128.0)
        codes = codes * codes
        codes = codes * codes
        codes = codes * codes
        for k in range(shards):
            part = in_ref[j, pl.ds(k * rows, rows), cols].astype(F32) * codes[k : k + 1]
            panel_ref[pl.ds((k * count + j) * rows, rows), cols] = part.astype(BF)


def near_tile(above, table, shards):
    tile, width = above.shape
    blocks = width // BLK

    def kernel(above_ref, table_ref, out_ref):
        for b in range(blocks):
            block = table_ref[b]
            near = lax.dot_general(
                above_ref[:, pl.ds(b * BLK, BLK)], block, (((1,), (1,)), ((), ())), preferred_element_type=F32
            )
            store_scaled(out_ref, near.astype(BF).astype(F32), b * BLK, shards, tile // shards)

    return call(kernel, like(tile + CODE, width, BF), "near", [above, table], flops=2 * tile * width * BLK)


def reduced_tile(panel, factor, grad, shards):
    tile, width = grad.shape
    depth, rows = factor[0].shape[1], tile // shards

    def kernel(panel_in, grad_ref, *refs):
        pieces, (out_ref, panel_ref, factor_ref) = refs[:shards], refs[shards:]
        y = lax.axis_index("y")
        for k in range(shards):
            at = pl.multiple_of(lax.rem(y + (shards - k), shards) * rows, 16)
            factor_ref[pl.ds(at, rows), :] = pieces[k][...]
        for at, w in chunks_of(width):
            cols = pl.ds(at, w)
            load_scaled(panel_in, panel_ref, at, w, shards, rows)
            coupled = jnp.dot(factor_ref[...], panel_ref[:, cols], preferred_element_type=F32)
            reduced = (grad_ref[:, cols].astype(F32) - coupled).astype(BF).astype(F32)
            store_scaled(out_ref, reduced, at, shards, rows)

    return call(
        kernel,
        like(tile + CODE, width, BF),
        "reduced",
        [panel, grad, *factor],
        [pltpu.VMEM((depth, width), BF), pltpu.VMEM((tile, depth), BF)],
        flops=2 * tile * depth * width,
    )


def last_tiles(panel, factors, table, shards):
    tile, width = factors.shape[0] // 2, panel.shape[2]
    depth, rows = factors.shape[1], tile // shards

    def kernel(panel_in, factors_in, table_ref, local_ref, middle_ref, panel_ref, factors_ref, sem):
        copy = pltpu.make_async_copy(factors_in, factors_ref, sem)
        copy.start()
        for at, w in chunks_of(width):
            load_scaled(panel_in, panel_ref, at, w, shards, rows)
            if at == 0:
                copy.wait()
            both = jnp.dot(factors_ref[...], panel_ref[:, pl.ds(at, w)], preferred_element_type=F32).astype(BF)
            for b in range(w // BLK):
                sub = pl.ds(at + b * BLK, BLK)
                block = table_ref[at // BLK + b]
                product = jnp.dot(both[:, b * BLK : (b + 1) * BLK], block, preferred_element_type=F32)
                for k in range(shards):
                    local_ref[pl.ds(k * rows, rows), sub] = product[2 * k * rows : (2 * k + 1) * rows]
                    middle_ref[pl.ds(k * rows, rows), sub] = product[(2 * k + 1) * rows : (2 * k + 2) * rows].astype(BF)

    return call(
        kernel,
        (like(tile, width, F32), like(tile, width, BF)),
        "last",
        [panel, factors, table],
        [pltpu.VMEM((depth, width), BF), pltpu.VMEM(factors.shape, BF), pltpu.SemaphoreType.DMA],
        far=(1,),
        flops=4 * tile * depth * width,
    )


def update_tile(local_term, middle, table):
    tile, width = middle.shape
    blocks = width // BLK

    def kernel(local_ref, middle_ref, table_ref, out_ref):
        for b in range(blocks):
            cols = pl.ds(b * BLK, BLK)
            pushed = jnp.dot(middle_ref[:, cols], table_ref[b], preferred_element_type=F32)
            out_ref[:, cols] = (local_ref[:, cols] - pushed).astype(BF)

    return call(kernel, like(tile, width, BF), "update", [local_term, middle, table], flops=2 * tile * width * BLK)


def copies(kernel, out, name, operands, count):
    def body(*refs):
        sems = refs[-1]
        started = []
        for i, (source, target) in enumerate(kernel(*refs[:-1])):
            copy = pltpu.make_async_copy(source, target, sems.at[i])
            copy.start()
            started.append(copy)
        for copy in started:
            copy.wait()

    moved = 2 * sum(x.size * x.dtype.itemsize for x in jax.tree.leaves(out))
    return pl.pallas_call(
        body,
        out_shape=out,
        in_specs=[HBM] * len(operands),
        out_specs=jax.tree.map(lambda _: VMEM, out),
        scratch_shapes=[pltpu.SemaphoreType.DMA((count,))],
        compiler_params=pltpu.CompilerParams(vmem_limit_bytes=16 << 20),
        cost_estimate=pl.CostEstimate(flops=0, bytes_accessed=moved, transcendentals=0),
        name=name,
    )(*[pltpu.with_memory_space_constraint(x, pltpu.HBM) for x in operands])


def prepare(gradient, out_inverse, out_coupling, shards):
    _, rows, width = gradient.shape
    width //= shards
    blocks = out_inverse.shape[1] // shards
    table = jax.ShapeDtypeStruct((blocks, BLK, BLK), BF)

    def kernel(grad_ref, inverse_ref, coupling_ref, split_ref, inv_ref, psi_ref):
        mine = pl.ds(lax.axis_index("y") * blocks, blocks)
        for k in range(shards):
            yield grad_ref.at[0, :, pl.ds(k * width, width)], split_ref.at[pl.ds(k * rows, rows), :]
        yield coupling_ref.at[0, mine], psi_ref
        yield inverse_ref.at[0, mine], inv_ref

    out = (like(shards * rows, width, BF), table, table)
    return copies(kernel, out, "prepare", [gradient, out_inverse, out_coupling], shards + 2)


def repeat_rows(parts, shards, name):
    rows, width = parts[0].shape[1:]
    count = len(parts)

    def kernel(*refs):
        for k in range(shards):
            for i in range(count):
                yield refs[i].at[0], refs[count].at[pl.ds((k * count + i) * rows, rows), :]

    return copies(kernel, like(shards * count * rows, width, BF), name, parts, shards * count)


def hop_y(x, by):
    size = lax.axis_size("y")
    return lax.ppermute(x, "y", [(i, (i + by) % size) for i in range(size)])


def exchange(x):
    return lax.all_to_all(x, "y", split_axis=0, concat_axis=0, tiled=True)


def after(x, *others):
    return lax.optimization_barrier((x, *others))[0]


def join_columns(x, shards):
    rows, width = x.shape[0] // shards, x.shape[1]

    def kernel(in_ref, out_ref):
        for k in range(shards):
            out_ref[0, :, pl.ds(k * width, width)] = in_ref[pl.ds(k * rows, rows), :]

    return call(kernel, jax.ShapeDtypeStruct((1, rows, shards * width), x.dtype), "join", [x])


def gather_panel(tile):
    return lax.all_gather(tile.astype(HALF), "z", axis=0).astype(BF)


def local(gradient, in_inverse, in_coupling, in_carry, out_inverse, out_coupling):
    shards = lax.axis_size("y")
    split, inv, psi = prepare(gradient, out_inverse, out_coupling, shards)
    psi_below = hop_layer(psi, 1)
    grad = exchange(split)
    above = hop_layer(grad, -1)
    coupling = after(in_coupling, grad)[0]
    factor = [coupling] + [hop_y(coupling, k) for k in range(1, shards)]
    near = near_tile(above, psi, shards)
    factors = exchange(after(repeat_rows([after(in_inverse, grad), in_carry], shards, "twice"), near))
    reduced = reduced_tile(gather_panel(near), factor, grad, shards)
    local_term, middle = last_tiles(gather_panel(reduced), factors, inv, shards)
    update = update_tile(local_term, hop_layer(middle, 1), psi_below)
    return join_columns(exchange(update), shards)


def solution(mesh):
    layers = mesh.shape["layer"]
    fine = Mesh(np.asarray(mesh.devices).reshape(layers, 4, -1), ("layer", "y", "z"))
    rows = P("layer", ("y", "z"), None)
    table = P("layer", None, None, None)
    return jax.shard_map(
        local,
        mesh=fine,
        in_specs=(rows, rows, rows, rows, table, table),
        out_specs=rows,
        check_vma=False,
    )
```

```python
import jax
import jax.numpy as jnp
import numpy as np
from jax import lax
from jax.experimental import pallas as pl
from jax.experimental.pallas import tpu as pltpu
from jax.sharding import Mesh, PartitionSpec as P

BF = jnp.bfloat16
F32 = jnp.float32
HALF = jnp.float16
BLK = 128
CODE = 8
VMEM = pl.BlockSpec(memory_space=pltpu.VMEM)
HBM = pl.BlockSpec(memory_space=pltpu.HBM)


def call(kernel, out, name, operands, scratch=(), mib=16, flops=0, far=()):
    moved = sum(x.size * x.dtype.itemsize for x in operands) + sum(x.size * x.dtype.itemsize for x in jax.tree.leaves(out))
    return pl.pallas_call(
        kernel,
        out_shape=out,
        in_specs=[HBM if i in far else VMEM for i in range(len(operands))],
        out_specs=jax.tree.map(lambda _: VMEM, out),
        scratch_shapes=list(scratch),
        compiler_params=pltpu.CompilerParams(vmem_limit_bytes=mib << 20),
        cost_estimate=pl.CostEstimate(flops=flops, bytes_accessed=moved, transcendentals=0),
        name=name,
    )(*operands)


def like(rows, cols, dtype):
    return jax.ShapeDtypeStruct((rows, cols), dtype)


def hop_layer(x, by):
    size = lax.axis_size("layer")
    return lax.ppermute(x, "layer", [(i, i + by) for i in range(size) if 0 <= i + by < size])


def chunks_of(width):
    return [(at, min(256, width - at)) for at in range(0, width, 256)]


def store_scaled(out_ref, values, at, shards, rows):
    width = values.shape[1]
    cols = pl.ds(at, width)
    line = lax.broadcasted_iota(jnp.int32, (CODE, width), 0)
    codes = jnp.full((CODE, width), 1.0, F32)
    for k in range(shards):
        part = values[k * rows : (k + 1) * rows]
        top = jnp.max(jnp.abs(part), axis=0, keepdims=True)
        scale = jnp.ones_like(top)
        code = jnp.full_like(top, 128.0)
        for bits in (64, 32, 16, 8):
            small = top < 2.0 ** (15 - bits)
            grow = jnp.where(small, 2.0**bits, 1.0)
            top = top * grow
            scale = scale * grow
            code = code * jnp.where(small, 2.0 ** (-(bits // 8)), 1.0)
        out_ref[pl.ds(k * rows, rows), cols] = (part * scale).astype(BF)
        codes = jnp.where(line == k, code, codes)
    out_ref[pl.ds(shards * rows, CODE), cols] = codes.astype(BF)


def load_scaled(in_ref, panel_ref, at, width, shards, rows):
    cols = pl.ds(at, width)
    count = in_ref.shape[0]
    for j in range(count):
        codes = in_ref[j, pl.ds(shards * rows, CODE), cols].astype(F32) * (1.0 / 128.0)
        codes = codes * codes
        codes = codes * codes
        codes = codes * codes
        for k in range(shards):
            part = in_ref[j, pl.ds(k * rows, rows), cols].astype(F32) * codes[k : k + 1]
            panel_ref[pl.ds((k * count + j) * rows, rows), cols] = part.astype(BF)


def near_tile(above, table, shards):
    tile, width = above.shape
    blocks = width // BLK

    def kernel(above_ref, table_ref, out_ref):
        for b in range(blocks):
            block = table_ref[b]
            near = lax.dot_general(
                above_ref[:, pl.ds(b * BLK, BLK)], block, (((1,), (1,)), ((), ())), preferred_element_type=F32
            )
            store_scaled(out_ref, near.astype(BF).astype(F32), b * BLK, shards, tile // shards)

    return call(kernel, like(tile + CODE, width, BF), "near", [above, table], flops=2 * tile * width * BLK)


def reduced_tile(panel, factor, grad, shards):
    tile, width = grad.shape
    depth, rows = factor[0].shape[1], tile // shards

    def kernel(panel_in, grad_ref, *refs):
        pieces, (out_ref, panel_ref, factor_ref) = refs[:shards], refs[shards:]
        gather_rows(pieces, factor_ref, rows)
        for at, w in chunks_of(width):
            cols = pl.ds(at, w)
            load_scaled(panel_in, panel_ref, at, w, shards, rows)
            coupled = jnp.dot(factor_ref[...], panel_ref[:, cols], preferred_element_type=F32)
            reduced = (grad_ref[:, cols].astype(F32) - coupled).astype(BF).astype(F32)
            store_scaled(out_ref, reduced, at, shards, rows)

    return call(
        kernel,
        like(tile + CODE, width, BF),
        "reduced",
        [panel, grad, *factor],
        [pltpu.VMEM((depth, width), BF), pltpu.VMEM((tile, depth), BF)],
        flops=2 * tile * depth * width,
    )


def gather_rows(pieces, factor_ref, rows, first=0):
    y, shards = lax.axis_index("y"), len(pieces)
    for k in range(shards):
        at = pl.multiple_of(lax.rem(y + (shards - k), shards) * rows, 16)
        factor_ref[pl.ds(at, rows), :] = pieces[k][pl.ds(first, rows), :]


def middle_tile(panel, factor, table, shards):
    rows, depth = factor[0].shape[0] // 2, factor[0].shape[1]
    tile, width = shards * rows, panel.shape[2]

    def kernel(panel_in, table_ref, *refs):
        pieces, (middle_ref, panel_ref, factor_ref) = refs[:shards], refs[shards:]
        gather_rows(pieces, factor_ref, rows, rows)
        for at, w in chunks_of(width):
            load_scaled(panel_in, panel_ref, at, w, shards, rows)
            carried = jnp.dot(factor_ref[...], panel_ref[:, pl.ds(at, w)], preferred_element_type=F32).astype(BF)
            for b in range(w // BLK):
                product = jnp.dot(
                    carried[:, b * BLK : (b + 1) * BLK], table_ref[at // BLK + b], preferred_element_type=F32
                )
                middle_ref[:, pl.ds(at + b * BLK, BLK)] = product.astype(BF)

    return call(
        kernel,
        (like(tile, width, BF), like(depth, width, BF)),
        "middle",
        [panel, table, *factor],
        [pltpu.VMEM((tile, depth), BF)],
        flops=2 * tile * depth * width,
    )


def local_tile(panel, factor, table, shards):
    rows, depth = factor[0].shape[0] // 2, factor[0].shape[1]
    tile, width = shards * rows, panel.shape[1]

    def kernel(panel_ref, table_ref, *refs):
        pieces, (local_ref, factor_ref) = refs[:shards], refs[shards:]
        gather_rows(pieces, factor_ref, rows)
        for at, w in chunks_of(width):
            whitened = jnp.dot(factor_ref[...], panel_ref[:, pl.ds(at, w)], preferred_element_type=F32).astype(BF)
            for b in range(w // BLK):
                local_ref[:, pl.ds(at + b * BLK, BLK)] = jnp.dot(
                    whitened[:, b * BLK : (b + 1) * BLK], table_ref[at // BLK + b], preferred_element_type=F32
                )

    return call(
        kernel,
        like(tile, width, F32),
        "local",
        [panel, table, *factor],
        [pltpu.VMEM((tile, depth), BF)],
        flops=2 * tile * depth * width,
    )


def update_tile(local_term, middle, table):
    tile, width = middle.shape
    blocks = width // BLK

    def kernel(local_ref, middle_ref, table_ref, out_ref):
        for b in range(blocks):
            cols = pl.ds(b * BLK, BLK)
            pushed = jnp.dot(middle_ref[:, cols], table_ref[b], preferred_element_type=F32)
            out_ref[:, cols] = (local_ref[:, cols] - pushed).astype(BF)

    return call(kernel, like(tile, width, BF), "update", [local_term, middle, table], flops=2 * tile * width * BLK)


def copies(kernel, out, name, operands, count):
    def body(*refs):
        sems = refs[-1]
        started = []
        for i, (source, target) in enumerate(kernel(*refs[:-1])):
            copy = pltpu.make_async_copy(source, target, sems.at[i])
            copy.start()
            started.append(copy)
        for copy in started:
            copy.wait()

    moved = 2 * sum(x.size * x.dtype.itemsize for x in jax.tree.leaves(out))
    return pl.pallas_call(
        body,
        out_shape=out,
        in_specs=[HBM] * len(operands),
        out_specs=jax.tree.map(lambda _: VMEM, out),
        scratch_shapes=[pltpu.SemaphoreType.DMA((count,))],
        compiler_params=pltpu.CompilerParams(vmem_limit_bytes=16 << 20),
        cost_estimate=pl.CostEstimate(flops=0, bytes_accessed=moved, transcendentals=0),
        name=name,
    )(*[pltpu.with_memory_space_constraint(x, pltpu.HBM) for x in operands])


def prepare(gradient, out_inverse, out_coupling, shards):
    _, rows, width = gradient.shape
    width //= shards
    blocks = out_inverse.shape[1] // shards
    table = jax.ShapeDtypeStruct((blocks, BLK, BLK), BF)

    def kernel(grad_ref, inverse_ref, coupling_ref, split_ref, inv_ref, psi_ref):
        mine = pl.ds(lax.axis_index("y") * blocks, blocks)
        for k in range(shards):
            yield grad_ref.at[0, :, pl.ds(k * width, width)], split_ref.at[pl.ds(k * rows, rows), :]
        yield coupling_ref.at[0, mine], psi_ref
        yield inverse_ref.at[0, mine], inv_ref

    out = (like(shards * rows, width, BF), table, table)
    return copies(kernel, out, "prepare", [gradient, out_inverse, out_coupling], shards + 2)


def stack(parts):
    rows, width = parts[0].shape[1:]
    count = len(parts)

    def kernel(*refs):
        for i in range(count):
            yield refs[i].at[0], refs[count].at[pl.ds(i * rows, rows), :]

    return copies(kernel, like(count * rows, width, BF), "stack", parts, count)


def hop_y(x, by):
    size = lax.axis_size("y")
    return lax.ppermute(x, "y", [(i, (i + by) % size) for i in range(size)])


def exchange(x):
    return lax.all_to_all(x, "y", split_axis=0, concat_axis=0, tiled=True)


def after(x, *others):
    return lax.optimization_barrier((x, *others))[0]


def join_columns(x, shards):
    rows, width = x.shape[0] // shards, x.shape[1]

    def kernel(in_ref, out_ref):
        for k in range(shards):
            out_ref[0, :, pl.ds(k * width, width)] = in_ref[pl.ds(k * rows, rows), :]

    return call(kernel, jax.ShapeDtypeStruct((1, rows, shards * width), x.dtype), "join", [x])


def gather_panel(tile):
    return lax.all_gather(tile.astype(HALF), "z", axis=0).astype(BF)


def from_peers(x, shards):
    return [x] + [hop_y(x, k) for k in range(1, shards)]


def local(gradient, in_inverse, in_coupling, in_carry, out_inverse, out_coupling):
    shards = lax.axis_size("y")
    split, inv, psi = prepare(gradient, out_inverse, out_coupling, shards)
    psi_below = hop_layer(psi, 1)
    grad = exchange(split)
    above = hop_layer(grad, -1)
    coupling = from_peers(after(in_coupling, grad)[0], shards)
    both = stack([after(in_inverse, grad), in_carry])
    near = near_tile(above, after(psi, psi_below), shards)
    factors = from_peers(after(both, near), shards)
    reduced = reduced_tile(gather_panel(near), coupling, grad, shards)
    middle, panel = middle_tile(gather_panel(reduced), factors, inv, shards)
    local_term = local_tile(panel, factors, inv, shards)
    update = update_tile(local_term, hop_layer(middle, 1), psi_below)
    return join_columns(exchange(update), shards)


def solution(mesh):
    layers = mesh.shape["layer"]
    fine = Mesh(np.asarray(mesh.devices).reshape(layers, 4, -1), ("layer", "y", "z"))
    rows = P("layer", ("y", "z"), None)
    table = P("layer", None, None, None)
    return jax.shard_map(
        local,
        mesh=fine,
        in_specs=(rows, rows, rows, rows, table, table),
        out_specs=rows,
        check_vma=False,
    )
```

```python
import jax
import jax.numpy as jnp
import numpy as np
from jax import lax
from jax.experimental import pallas as pl
from jax.experimental.pallas import tpu as pltpu
from jax.sharding import Mesh, PartitionSpec as P

BF = jnp.bfloat16
F32 = jnp.float32
HALF = jnp.float16
BLK = 128
CODE = 8
VMEM = pl.BlockSpec(memory_space=pltpu.VMEM)
HBM = pl.BlockSpec(memory_space=pltpu.HBM)


def call(kernel, out, name, operands, scratch=(), mib=16, flops=0, far=()):
    moved = sum(x.size * x.dtype.itemsize for x in operands) + sum(x.size * x.dtype.itemsize for x in jax.tree.leaves(out))
    return pl.pallas_call(
        kernel,
        out_shape=out,
        in_specs=[HBM if i in far else VMEM for i in range(len(operands))],
        out_specs=jax.tree.map(lambda _: VMEM, out),
        scratch_shapes=list(scratch),
        compiler_params=pltpu.CompilerParams(vmem_limit_bytes=mib << 20),
        cost_estimate=pl.CostEstimate(flops=flops, bytes_accessed=moved, transcendentals=0),
        name=name,
    )(*operands)


def like(rows, cols, dtype):
    return jax.ShapeDtypeStruct((rows, cols), dtype)


def hop_layer(x, by):
    size = lax.axis_size("layer")
    return lax.ppermute(x, "layer", [(i, i + by) for i in range(size) if 0 <= i + by < size])


def chunks_of(width):
    return [(at, min(256, width - at)) for at in range(0, width, 256)]


def store_scaled(out_ref, parts, owners, at):
    rows, width = parts[0].shape
    cols = pl.ds(at, width)
    line = lax.broadcasted_iota(jnp.int32, (CODE, width), 0)
    codes = jnp.full((CODE, width), 1.0, F32)
    for part, owner in zip(parts, owners, strict=True):
        top = jnp.max(jnp.abs(part), axis=0, keepdims=True)
        scale = jnp.ones_like(top)
        code = jnp.full_like(top, 128.0)
        for bits in (64, 32, 16, 8):
            small = top < 2.0 ** (15 - bits)
            grow = jnp.where(small, 2.0**bits, 1.0)
            top = top * grow
            scale = scale * grow
            code = code * jnp.where(small, 2.0 ** (-(bits // 8)), 1.0)
        out_ref[rows_of(owner, rows), cols] = (part * scale).astype(BF)
        codes = jnp.where(line == owner, code, codes)
    out_ref[pl.ds(len(parts) * rows, CODE), cols] = codes.astype(BF)


def rows_of(owner, rows):
    return pl.ds(owner * rows if isinstance(owner, int) else pl.multiple_of(owner * rows, 16), rows)


def blocks_of(values, count):
    rows = values.shape[0] // count
    return [values[k * rows : (k + 1) * rows] for k in range(count)]


def owners_of(shards):
    y = lax.axis_index("y")
    return [lax.rem(y + (shards - k), shards) for k in range(shards)]


def joined(pieces, rows, first=0):
    return jnp.concatenate([piece[pl.ds(first, rows), :] for piece in pieces], axis=0)


def load_scaled(in_ref, panel_ref, at, width, shards, rows):
    cols = pl.ds(at, width)
    count = in_ref.shape[0]
    for j in range(count):
        codes = in_ref[j, pl.ds(shards * rows, CODE), cols].astype(F32) * (1.0 / 128.0)
        codes = codes * codes
        codes = codes * codes
        codes = codes * codes
        for k in range(shards):
            part = in_ref[j, pl.ds(k * rows, rows), cols].astype(F32) * codes[k : k + 1]
            panel_ref[pl.ds((k * count + j) * rows, rows), cols] = part.astype(BF)


def near_tile(above, table, shards):
    tile, width = above.shape
    blocks = width // BLK

    def kernel(above_ref, table_ref, out_ref):
        for b in range(blocks):
            block = table_ref[b]
            near = lax.dot_general(
                above_ref[:, pl.ds(b * BLK, BLK)], block, (((1,), (1,)), ((), ())), preferred_element_type=F32
            )
            store_scaled(out_ref, blocks_of(near.astype(BF).astype(F32), shards), list(range(shards)), b * BLK)

    return call(kernel, like(tile + CODE, width, BF), "near", [above, table], flops=2 * tile * width * BLK)


def reduced_tile(panel, factor, grad, shards):
    tile, width = grad.shape
    depth, rows = factor[0].shape[1], tile // shards

    def kernel(panel_in, grad_ref, *refs):
        pieces, (out_ref, panel_ref) = refs[:shards], refs[shards:]
        owners = owners_of(shards)
        for at, w in chunks_of(width):
            cols = pl.ds(at, w)
            load_scaled(panel_in, panel_ref, at, w, shards, rows)
            coupled = jnp.dot(joined(pieces, rows), panel_ref[:, cols], preferred_element_type=F32)
            parts = [
                (grad_ref[rows_of(owner, rows), cols].astype(F32) - part).astype(BF).astype(F32)
                for owner, part in zip(owners, blocks_of(coupled, shards), strict=True)
            ]
            store_scaled(out_ref, parts, owners, at)

    return call(
        kernel,
        like(tile + CODE, width, BF),
        "reduced",
        [panel, grad, *factor],
        [pltpu.VMEM((depth, width), BF)],
        flops=2 * tile * depth * width,
    )


def pushed_tile(panel, factor, inverse, coupling, shards):
    rows, depth = factor[0].shape[0] // 2, factor[0].shape[1]
    tile, width = shards * rows, panel.shape[2]

    def kernel(panel_in, inverse_ref, coupling_ref, *refs):
        pieces, (pushed_ref, panel_ref) = refs[:shards], refs[shards:]
        owners = owners_of(shards)
        carried = []
        for at, w in chunks_of(width):
            load_scaled(panel_in, panel_ref, at, w, shards, rows)
            both = jnp.dot(joined(pieces, rows, rows), panel_ref[:, pl.ds(at, w)], preferred_element_type=F32)
            carried += [both[:, i : i + BLK].astype(BF) for i in range(0, w, BLK)]
        middle = [
            jnp.dot(x, inverse_ref[b], preferred_element_type=F32).astype(BF) for b, x in enumerate(carried)
        ]
        for b, x in enumerate(middle):
            pushed = jnp.dot(x, coupling_ref[b], preferred_element_type=F32).astype(BF)
            for owner, part in zip(owners, blocks_of(pushed, shards), strict=True):
                pushed_ref[rows_of(owner, rows), pl.ds(b * BLK, BLK)] = part

    return call(
        kernel,
        (like(tile, width, BF), like(depth, width, BF)),
        "pushed",
        [panel, inverse, coupling, *factor],
        flops=2 * tile * depth * width,
    )


def local_tile(panel, factor, inverse, shards):
    rows, depth = factor[0].shape[0] // 2, factor[0].shape[1]
    tile, width = shards * rows, panel.shape[1]

    def kernel(panel_ref, inverse_ref, *refs):
        pieces, (local_ref,) = refs[:shards], refs[shards:]
        owners = owners_of(shards)
        whitened = []
        for at, w in chunks_of(width):
            both = jnp.dot(joined(pieces, rows), panel_ref[:, pl.ds(at, w)], preferred_element_type=F32)
            whitened += [both[:, i : i + BLK].astype(BF) for i in range(0, w, BLK)]
        for b, x in enumerate(whitened):
            product = jnp.dot(x, inverse_ref[b], preferred_element_type=F32)
            for owner, part in zip(owners, blocks_of(product, shards), strict=True):
                local_ref[rows_of(owner, rows), pl.ds(b * BLK, BLK)] = part

    return call(
        kernel,
        like(tile, width, F32),
        "local",
        [panel, inverse, *factor],
        flops=2 * tile * depth * width,
    )


def update_tile(local_term, pushed):
    def kernel(local_ref, pushed_ref, out_ref):
        out_ref[...] = (local_ref[...] - pushed_ref[...].astype(F32)).astype(BF)

    return call(kernel, like(*pushed.shape, BF), "update", [local_term, pushed])


def copies(kernel, out, name, operands, count):
    def body(*refs):
        sems = refs[-1]
        started = []
        for i, (source, target) in enumerate(kernel(*refs[:-1])):
            copy = pltpu.make_async_copy(source, target, sems.at[i])
            copy.start()
            started.append(copy)
        for copy in started:
            copy.wait()

    moved = 2 * sum(x.size * x.dtype.itemsize for x in jax.tree.leaves(out))
    return pl.pallas_call(
        body,
        out_shape=out,
        in_specs=[HBM] * len(operands),
        out_specs=jax.tree.map(lambda _: VMEM, out),
        scratch_shapes=[pltpu.SemaphoreType.DMA((count,))],
        compiler_params=pltpu.CompilerParams(vmem_limit_bytes=16 << 20),
        cost_estimate=pl.CostEstimate(flops=0, bytes_accessed=moved, transcendentals=0),
        name=name,
    )(*[pltpu.with_memory_space_constraint(x, pltpu.HBM) for x in operands])


def prepare(gradient, out_inverse, out_coupling, shards):
    _, rows, width = gradient.shape
    width //= shards
    blocks = out_inverse.shape[1] // shards
    table = jax.ShapeDtypeStruct((blocks, BLK, BLK), BF)

    def kernel(grad_ref, inverse_ref, coupling_ref, split_ref, inv_ref, psi_ref):
        mine = pl.ds(lax.axis_index("y") * blocks, blocks)
        for k in range(shards):
            yield grad_ref.at[0, :, pl.ds(k * width, width)], split_ref.at[pl.ds(k * rows, rows), :]
        yield coupling_ref.at[0, mine], psi_ref
        yield inverse_ref.at[0, mine], inv_ref

    out = (like(shards * rows, width, BF), table, table)
    return copies(kernel, out, "prepare", [gradient, out_inverse, out_coupling], shards + 2)


def stack(parts):
    rows, width = parts[0].shape[1:]
    count = len(parts)

    def kernel(*refs):
        for i in range(count):
            yield refs[i].at[0], refs[count].at[pl.ds(i * rows, rows), :]

    return copies(kernel, like(count * rows, width, BF), "stack", parts, count)


def hop_y(x, by):
    size = lax.axis_size("y")
    return lax.ppermute(x, "y", [(i, (i + by) % size) for i in range(size)])


def exchange(x):
    return lax.all_to_all(x, "y", split_axis=0, concat_axis=0, tiled=True)


def after(x, *others):
    return lax.optimization_barrier((x, *others))[0]


def join_columns(x, shards):
    rows, width = x.shape[0] // shards, x.shape[1]

    def kernel(in_ref, out_ref):
        for k in range(shards):
            out_ref[0, :, pl.ds(k * width, width)] = in_ref[pl.ds(k * rows, rows), :]

    return call(kernel, jax.ShapeDtypeStruct((1, rows, shards * width), x.dtype), "join", [x])


def gather_panel(tile):
    return lax.all_gather(tile.astype(HALF), "z", axis=0).astype(BF)


def local(gradient, in_inverse, in_coupling, in_carry, out_inverse, out_coupling):
    shards = lax.axis_size("y")
    split, inv, psi = prepare(gradient, out_inverse, out_coupling, shards)
    grad = exchange(split)
    above = hop_layer(grad, -1)
    coupling = after(in_coupling, grad)[0]
    coupling = [coupling] + [hop_y(coupling, k) for k in range(1, shards)]
    pair = stack([after(in_inverse, split), in_carry])
    near = near_tile(above, psi, shards)
    early, late = after(pair, grad), after(pair, near)
    factors = [pair] + [hop_y(early if k == 2 else late, k) for k in range(1, shards)]
    reduced = reduced_tile(gather_panel(near), coupling, grad, shards)
    pushed, panel = pushed_tile(gather_panel(reduced), factors, inv, psi, shards)
    local_term = local_tile(panel, factors, inv, shards)
    update = update_tile(local_term, hop_layer(pushed, 1))
    return join_columns(exchange(update), shards)


def solution(mesh):
    layers = mesh.shape["layer"]
    fine = Mesh(np.asarray(mesh.devices).reshape(layers, 4, -1), ("layer", "y", "z"))
    rows = P("layer", ("y", "z"), None)
    table = P("layer", None, None, None)
    return jax.shard_map(
        local,
        mesh=fine,
        in_specs=(rows, rows, rows, rows, table, table),
        out_specs=rows,
        check_vma=False,
    )
```

```python
import jax
import jax.numpy as jnp
import numpy as np
from jax import lax
from jax.experimental import pallas as pl
from jax.experimental.pallas import tpu as pltpu
from jax.sharding import Mesh, PartitionSpec as P

BF = jnp.bfloat16
F32 = jnp.float32
HALF = jnp.float16
BLK = 128
CODE = 8
VMEM = pl.BlockSpec(memory_space=pltpu.VMEM)
HBM = pl.BlockSpec(memory_space=pltpu.HBM)


def call(kernel, out, name, operands, scratch=(), mib=16, flops=0, far=()):
    moved = sum(x.size * x.dtype.itemsize for x in operands) + sum(x.size * x.dtype.itemsize for x in jax.tree.leaves(out))
    return pl.pallas_call(
        kernel,
        out_shape=out,
        in_specs=[HBM if i in far else VMEM for i in range(len(operands))],
        out_specs=jax.tree.map(lambda _: VMEM, out),
        scratch_shapes=list(scratch),
        compiler_params=pltpu.CompilerParams(vmem_limit_bytes=mib << 20),
        cost_estimate=pl.CostEstimate(flops=flops, bytes_accessed=moved, transcendentals=0),
        name=name,
    )(*operands)


def like(rows, cols, dtype):
    return jax.ShapeDtypeStruct((rows, cols), dtype)


def hop_layer(x, by):
    size = lax.axis_size("layer")
    return lax.ppermute(x, "layer", [(i, i + by) for i in range(size) if 0 <= i + by < size])


def chunks_of(width):
    return [(at, min(256, width - at)) for at in range(0, width, 256)]


def store_scaled(out_ref, parts, owners, at):
    rows, width = parts[0].shape
    cols = pl.ds(at, width)
    line = lax.broadcasted_iota(jnp.int32, (CODE, width), 0)
    codes = jnp.full((CODE, width), 1.0, F32)
    for part, owner in zip(parts, owners, strict=True):
        top = jnp.max(jnp.abs(part), axis=0, keepdims=True)
        scale = jnp.ones_like(top)
        code = jnp.full_like(top, 128.0)
        for bits in (64, 32, 16, 8):
            small = top < 2.0 ** (15 - bits)
            grow = jnp.where(small, 2.0**bits, 1.0)
            top = top * grow
            scale = scale * grow
            code = code * jnp.where(small, 2.0 ** (-(bits // 8)), 1.0)
        out_ref[rows_of(owner, rows), cols] = (part * scale).astype(BF)
        codes = jnp.where(line == owner, code, codes)
    out_ref[pl.ds(len(parts) * rows, CODE), cols] = codes.astype(BF)


def rows_of(owner, rows):
    return pl.ds(owner * rows if isinstance(owner, int) else pl.multiple_of(owner * rows, 16), rows)


def blocks_of(values, count):
    rows = values.shape[0] // count
    return [values[k * rows : (k + 1) * rows] for k in range(count)]


def owners_of(shards):
    y = lax.axis_index("y")
    return [lax.rem(y + (shards - k), shards) for k in range(shards)]


def joined(pieces, rows, first=0):
    return jnp.concatenate([piece[pl.ds(first, rows), :] for piece in pieces], axis=0)


def load_scaled(in_ref, panel_ref, at, width, shards, rows):
    cols = pl.ds(at, width)
    count = in_ref.shape[0]
    for j in range(count):
        codes = in_ref[j, pl.ds(shards * rows, CODE), cols].astype(F32) * (1.0 / 128.0)
        codes = codes * codes
        codes = codes * codes
        codes = codes * codes
        for k in range(shards):
            part = in_ref[j, pl.ds(k * rows, rows), cols].astype(F32) * codes[k : k + 1]
            panel_ref[pl.ds((k * count + j) * rows, rows), cols] = part.astype(BF)


def near_tile(above, table, shards):
    tile, width = above.shape
    blocks = width // BLK

    def kernel(above_ref, table_ref, out_ref):
        for b in range(blocks):
            block = table_ref[b]
            near = lax.dot_general(
                above_ref[:, pl.ds(b * BLK, BLK)], block, (((1,), (1,)), ((), ())), preferred_element_type=F32
            )
            store_scaled(out_ref, blocks_of(near.astype(BF).astype(F32), shards), list(range(shards)), b * BLK)

    return call(kernel, like(tile + CODE, width, BF), "near", [above, table], flops=2 * tile * width * BLK)


def reduced_tile(panel, factor, grad, shards):
    tile, width = grad.shape
    depth, rows = factor[0].shape[1], tile // shards

    def kernel(panel_in, grad_ref, *refs):
        pieces, (out_ref, panel_ref) = refs[:shards], refs[shards:]
        owners = owners_of(shards)
        for at, w in chunks_of(width):
            cols = pl.ds(at, w)
            load_scaled(panel_in, panel_ref, at, w, shards, rows)
            coupled = jnp.dot(joined(pieces, rows), panel_ref[:, cols], preferred_element_type=F32)
            parts = [
                (grad_ref[rows_of(owner, rows), cols].astype(F32) - part).astype(BF).astype(F32)
                for owner, part in zip(owners, blocks_of(coupled, shards), strict=True)
            ]
            store_scaled(out_ref, parts, owners, at)

    return call(
        kernel,
        like(tile + CODE, width, BF),
        "reduced",
        [panel, grad, *factor],
        [pltpu.VMEM((depth, width), BF)],
        flops=2 * tile * depth * width,
    )


def pushed_tile(panel, factor, inverse, coupling, shards):
    rows, depth = factor[0].shape[0] // 2, factor[0].shape[1]
    tile, width = shards * rows, panel.shape[2]

    def kernel(panel_in, inverse_ref, coupling_ref, *refs):
        pieces, (pushed_ref, panel_ref) = refs[:shards], refs[shards:]
        owners = owners_of(shards)
        carried = []
        for at, w in chunks_of(width):
            load_scaled(panel_in, panel_ref, at, w, shards, rows)
            both = jnp.dot(joined(pieces, rows, rows), panel_ref[:, pl.ds(at, w)], preferred_element_type=F32)
            carried += [both[:, i : i + BLK].astype(BF) for i in range(0, w, BLK)]
        middle = [
            jnp.dot(x, inverse_ref[b], preferred_element_type=F32).astype(BF) for b, x in enumerate(carried)
        ]
        for b, x in enumerate(middle):
            pushed = jnp.dot(x, coupling_ref[b], preferred_element_type=F32).astype(BF)
            for owner, part in zip(owners, blocks_of(pushed, shards), strict=True):
                pushed_ref[rows_of(owner, rows), pl.ds(b * BLK, BLK)] = part

    return call(
        kernel,
        (like(tile, width, BF), like(depth, width, BF)),
        "pushed",
        [panel, inverse, coupling, *factor],
        flops=2 * tile * depth * width,
    )


def local_tile(panel, factor, inverse, shards):
    rows, depth = factor[0].shape[0] // 2, factor[0].shape[1]
    tile, width = shards * rows, panel.shape[1]

    def kernel(panel_ref, inverse_ref, *refs):
        pieces, (local_ref,) = refs[:shards], refs[shards:]
        owners = owners_of(shards)
        whitened = []
        for at, w in chunks_of(width):
            both = jnp.dot(joined(pieces, rows), panel_ref[:, pl.ds(at, w)], preferred_element_type=F32)
            whitened += [both[:, i : i + BLK].astype(BF) for i in range(0, w, BLK)]
        for b, x in enumerate(whitened):
            product = jnp.dot(x, inverse_ref[b], preferred_element_type=F32)
            for owner, part in zip(owners, blocks_of(product, shards), strict=True):
                local_ref[rows_of(owner, rows), pl.ds(b * BLK, BLK)] = part

    return call(
        kernel,
        like(tile, width, F32),
        "local",
        [panel, inverse, *factor],
        flops=2 * tile * depth * width,
    )


def update_pieces(local_term, pushed, shards):
    rows, width = pushed.shape[0] // shards, pushed.shape[1]

    def kernel(local_ref, pushed_ref, *out_refs):
        y = lax.axis_index("y")
        for k in range(shards):
            here = rows_of(lax.rem(y + k, shards), rows)
            out_refs[k][...] = (local_ref[here, :] - pushed_ref[here, :].astype(F32)).astype(BF)

    return call(kernel, tuple(like(rows, width, BF) for _ in range(shards)), "update", [local_term, pushed])


def copies(kernel, out, name, operands, count):
    def body(*refs):
        sems = refs[-1]
        started = []
        for i, (source, target) in enumerate(kernel(*refs[:-1])):
            copy = pltpu.make_async_copy(source, target, sems.at[i])
            copy.start()
            started.append(copy)
        for copy in started:
            copy.wait()

    moved = 2 * sum(x.size * x.dtype.itemsize for x in jax.tree.leaves(out))
    return pl.pallas_call(
        body,
        out_shape=out,
        in_specs=[HBM] * len(operands),
        out_specs=jax.tree.map(lambda _: VMEM, out),
        scratch_shapes=[pltpu.SemaphoreType.DMA((count,))],
        compiler_params=pltpu.CompilerParams(vmem_limit_bytes=16 << 20),
        cost_estimate=pl.CostEstimate(flops=0, bytes_accessed=moved, transcendentals=0),
        name=name,
    )(*[pltpu.with_memory_space_constraint(x, pltpu.HBM) for x in operands])


def prepare(gradient, out_inverse, out_coupling, shards):
    _, rows, width = gradient.shape
    width //= shards
    blocks = out_inverse.shape[1] // shards
    table = jax.ShapeDtypeStruct((blocks, BLK, BLK), BF)

    def kernel(grad_ref, inverse_ref, coupling_ref, *out_refs):
        y = lax.axis_index("y")
        mine = pl.ds(y * blocks, blocks)
        for k in range(shards):
            at = pl.multiple_of(lax.rem(y + k, shards) * width, BLK)
            yield grad_ref.at[0, :, pl.ds(at, width)], out_refs[k]
        yield inverse_ref.at[0, mine], out_refs[shards]
        yield coupling_ref.at[0, mine], out_refs[shards + 1]

    out = (*[like(rows, width, BF)] * shards, table, table)
    out = copies(kernel, out, "prepare", [gradient, out_inverse, out_coupling], shards + 2)
    return out[:shards], *out[shards:]


def assemble(pieces):
    rows, width = pieces[0].shape
    shards = len(pieces)

    def kernel(*refs):
        for k, owner in enumerate(owners_of(shards)):
            refs[shards][rows_of(owner, rows), :] = refs[k][...]

    return call(kernel, like(shards * rows, width, BF), "assemble", pieces)


def stack(parts):
    rows, width = parts[0].shape[1:]
    count = len(parts)

    def kernel(*refs):
        for i in range(count):
            yield refs[i].at[0], refs[count].at[pl.ds(i * rows, rows), :]

    return copies(kernel, like(count * rows, width, BF), "stack", parts, count)


def hop_y(x, by):
    size = lax.axis_size("y")
    return lax.ppermute(x, "y", [(i, (i + by) % size) for i in range(size)])


def exchange(pieces):
    return [pieces[0]] + [hop_y(pieces[k], k) for k in range(1, len(pieces))]


def after(x, *others):
    return lax.optimization_barrier((x, *others))[0]


def join_columns(pieces):
    rows, width = pieces[0].shape
    shards = len(pieces)

    def kernel(*refs):
        for k, owner in enumerate(owners_of(shards)):
            refs[shards][0, :, pl.ds(pl.multiple_of(owner * width, BLK), width)] = refs[k][...]

    return call(kernel, jax.ShapeDtypeStruct((1, rows, shards * width), BF), "join", pieces)


def gather_panel(tile):
    return lax.all_gather(tile.astype(HALF), "z", axis=0).astype(BF)


def local(gradient, in_inverse, in_coupling, in_carry, out_inverse, out_coupling):
    shards = lax.axis_size("y")
    slices, inv, psi = prepare(gradient, out_inverse, out_coupling, shards)
    pieces = exchange(slices)
    pair = stack([after(in_inverse, slices[0]), in_carry])
    grad = assemble(lax.optimization_barrier((*pieces, pair))[:shards])
    above = hop_layer(grad, -1)
    coupling = after(in_coupling, slices[0])[0]
    later = after(coupling, grad)
    coupling = [coupling] + [hop_y(coupling if k < 3 else later, k) for k in range(1, shards)]
    near = near_tile(above, psi, shards)
    early, late = after(pair, grad), after(pair, near)
    factors = [pair] + [hop_y(early if k == 2 else late, k) for k in range(1, shards)]
    reduced = reduced_tile(gather_panel(near), coupling, grad, shards)
    pushed, panel = pushed_tile(gather_panel(reduced), factors, inv, psi, shards)
    local_term = local_tile(panel, factors, inv, shards)
    return join_columns(exchange(update_pieces(local_term, hop_layer(pushed, 1), shards)))


def solution(mesh):
    layers = mesh.shape["layer"]
    fine = Mesh(np.asarray(mesh.devices).reshape(layers, 4, -1), ("layer", "y", "z"))
    rows = P("layer", ("y", "z"), None)
    table = P("layer", None, None, None)
    return jax.shard_map(
        local,
        mesh=fine,
        in_specs=(rows, rows, rows, rows, table, table),
        out_specs=rows,
        check_vma=False,
    )
```

```python
import jax
import jax.numpy as jnp
import numpy as np
from jax import lax
from jax.experimental import pallas as pl
from jax.experimental.pallas import tpu as pltpu
from jax.sharding import Mesh, PartitionSpec as P

BF = jnp.bfloat16
F32 = jnp.float32
HALF = jnp.float16
BLK = 128
CODE = 8
VMEM = pl.BlockSpec(memory_space=pltpu.VMEM)
HBM = pl.BlockSpec(memory_space=pltpu.HBM)


def call(kernel, out, name, operands, scratch=(), mib=16, flops=0, far=()):
    moved = sum(x.size * x.dtype.itemsize for x in operands) + sum(x.size * x.dtype.itemsize for x in jax.tree.leaves(out))
    return pl.pallas_call(
        kernel,
        out_shape=out,
        in_specs=[HBM if i in far else VMEM for i in range(len(operands))],
        out_specs=jax.tree.map(lambda _: VMEM, out),
        scratch_shapes=list(scratch),
        compiler_params=pltpu.CompilerParams(vmem_limit_bytes=mib << 20),
        cost_estimate=pl.CostEstimate(flops=flops, bytes_accessed=moved, transcendentals=0),
        name=name,
    )(*operands)


def like(rows, cols, dtype):
    return jax.ShapeDtypeStruct((rows, cols), dtype)


def hop_layer(x, by):
    size = lax.axis_size("layer")
    return lax.ppermute(x, "layer", [(i, i + by) for i in range(size) if 0 <= i + by < size])


def chunks_of(width):
    return [(at, min(256, width - at)) for at in range(0, width, 256)]


def store_scaled(out_ref, parts, owners, at):
    rows, width = parts[0].shape
    cols = pl.ds(at, width)
    line = lax.broadcasted_iota(jnp.int32, (CODE, width), 0)
    codes = jnp.full((CODE, width), 1.0, F32)
    for part, owner in zip(parts, owners, strict=True):
        top = jnp.max(jnp.abs(part), axis=0, keepdims=True)
        scale = jnp.ones_like(top)
        code = jnp.full_like(top, 128.0)
        for bits in (64, 32, 16, 8):
            small = top < 2.0 ** (15 - bits)
            grow = jnp.where(small, 2.0**bits, 1.0)
            top = top * grow
            scale = scale * grow
            code = code * jnp.where(small, 2.0 ** (-(bits // 8)), 1.0)
        out_ref[rows_of(owner, rows), cols] = (part * scale).astype(BF)
        codes = jnp.where(line == owner, code, codes)
    out_ref[pl.ds(len(parts) * rows, CODE), cols] = codes.astype(BF)


def rows_of(owner, rows):
    return pl.ds(owner * rows if isinstance(owner, int) else pl.multiple_of(owner * rows, 16), rows)


def blocks_of(values, count):
    rows = values.shape[0] // count
    return [values[k * rows : (k + 1) * rows] for k in range(count)]


def owners_of(shards):
    y = lax.axis_index("y")
    return [lax.rem(y + (shards - k), shards) for k in range(shards)]


def joined(pieces, rows, first=0):
    return jnp.concatenate([piece[pl.ds(first, rows), :] for piece in pieces], axis=0)


def load_scaled(in_ref, panel_ref, at, width, shards, rows):
    cols = pl.ds(at, width)
    count = in_ref.shape[0]
    for j in range(count):
        codes = in_ref[j, pl.ds(shards * rows, CODE), cols].astype(F32) * (1.0 / 128.0)
        codes = codes * codes
        codes = codes * codes
        codes = codes * codes
        for k in range(shards):
            part = in_ref[j, pl.ds(k * rows, rows), cols].astype(F32) * codes[k : k + 1]
            panel_ref[pl.ds((k * count + j) * rows, rows), cols] = part.astype(BF)


def hop_z(x, by):
    size = lax.axis_size("z")
    return lax.ppermute(x, "z", [(i, (i + by) % size) for i in range(size)])


def ring_step(pair):
    up, down = pair
    return lax.optimization_barrier((hop_z(up, 1), hop_z(down, -1)))


def ring_steps(tile):
    steps = [(tile, tile)]
    for _ in range(lax.axis_size("z") // 2 - 1):
        steps.append(ring_step(steps[-1]))
    return steps


def panel_pieces(steps):
    tile = steps[0][0]
    half, far = tile.shape[0] // 2, len(steps)
    pieces = [(tile, 0, 0)]
    for step in range(1, far):
        up, down = steps[step]
        pieces += [(up, 0, -step), (down, 0, step)]
    up, down = steps[-1]
    up, down = ring_step((up[:half], down[half:]))
    return pieces + [(up, 0, -far), (down, half, far)]


def spread(refs, places, panel_ref, rows):
    z, zs = lax.axis_index("z"), lax.axis_size("z")
    for ref, (first, distance) in zip(refs, places, strict=True):
        source = lax.rem(z + (distance + zs), zs)
        for k in range(ref.shape[0] // rows):
            at = pl.multiple_of(((first // rows + k) * zs + source) * rows, 16)
            panel_ref[pl.ds(at, rows), :] = ref[pl.ds(k * rows, rows), :]


def near_tile(above, table, shards):
    tile, width = above.shape
    blocks = width // BLK

    def kernel(above_ref, table_ref, out_ref):
        for b in range(blocks):
            block = table_ref[b]
            near = lax.dot_general(
                above_ref[:, pl.ds(b * BLK, BLK)], block, (((1,), (1,)), ((), ())), preferred_element_type=F32
            )
            store_scaled(out_ref, blocks_of(near.astype(BF).astype(F32), shards), list(range(shards)), b * BLK)

    return call(kernel, like(tile + CODE, width, BF), "near", [above, table], flops=2 * tile * width * BLK)


def reduced_tile(panel, factor, grad, shards):
    tile, width = grad.shape
    depth, rows = factor[0].shape[1], tile // shards

    def kernel(panel_in, grad_ref, *refs):
        pieces, (out_ref, panel_ref) = refs[:shards], refs[shards:]
        owners = owners_of(shards)
        for at, w in chunks_of(width):
            cols = pl.ds(at, w)
            load_scaled(panel_in, panel_ref, at, w, shards, rows)
            coupled = jnp.dot(joined(pieces, rows), panel_ref[:, cols], preferred_element_type=F32)
            for owner, part in zip(owners, blocks_of(coupled, shards), strict=True):
                here = rows_of(owner, rows)
                out_ref[here, cols] = (grad_ref[here, cols].astype(F32) - part).astype(BF)

    return call(
        kernel,
        like(tile, width, BF),
        "reduced",
        [panel, grad, *factor],
        [pltpu.VMEM((depth, width), BF)],
        flops=2 * tile * depth * width,
    )


def pushed_tile(line, factor, inverse, coupling, shards):
    rows, depth = factor[0].shape[0] // 2, factor[0].shape[1]
    tiles, places = [p[0] for p in line], [p[1:] for p in line]
    tile, width = tiles[0].shape
    count = len(tiles)

    def kernel(*refs):
        pieces, (inverse_ref, coupling_ref, pushed_ref, panel_ref) = refs[count : count + shards], refs[count + shards :]
        owners = owners_of(shards)
        spread(refs[:count], places, panel_ref, rows)
        carried = []
        for at, w in chunks_of(width):
            both = jnp.dot(joined(pieces, rows, rows), panel_ref[:, pl.ds(at, w)], preferred_element_type=F32)
            carried += [both[:, i : i + BLK].astype(BF) for i in range(0, w, BLK)]
        middle = [
            jnp.dot(x, inverse_ref[b], preferred_element_type=F32).astype(BF) for b, x in enumerate(carried)
        ]
        for b, x in enumerate(middle):
            pushed = jnp.dot(x, coupling_ref[b], preferred_element_type=F32).astype(BF)
            for owner, part in zip(owners, blocks_of(pushed, shards), strict=True):
                pushed_ref[rows_of(owner, rows), pl.ds(b * BLK, BLK)] = part

    return call(
        kernel,
        (like(tile, width, BF), like(depth, width, BF)),
        "pushed",
        [*tiles, *factor, inverse, coupling],
        flops=2 * tile * depth * width,
    )


def local_tile(panel, factor, inverse, shards):
    rows, depth = factor[0].shape[0] // 2, factor[0].shape[1]
    tile, width = shards * rows, panel.shape[1]

    def kernel(panel_ref, inverse_ref, *refs):
        pieces, (local_ref,) = refs[:shards], refs[shards:]
        owners = owners_of(shards)
        whitened = []
        for at, w in chunks_of(width):
            both = jnp.dot(joined(pieces, rows), panel_ref[:, pl.ds(at, w)], preferred_element_type=F32)
            whitened += [both[:, i : i + BLK].astype(BF) for i in range(0, w, BLK)]
        for b, x in enumerate(whitened):
            product = jnp.dot(x, inverse_ref[b], preferred_element_type=F32)
            for owner, part in zip(owners, blocks_of(product, shards), strict=True):
                local_ref[rows_of(owner, rows), pl.ds(b * BLK, BLK)] = part

    return call(
        kernel,
        like(tile, width, F32),
        "local",
        [panel, inverse, *factor],
        flops=2 * tile * depth * width,
    )


def update_pieces(local_term, pushed, shards):
    rows, width = pushed.shape[0] // shards, pushed.shape[1]

    def kernel(local_ref, pushed_ref, *out_refs):
        y = lax.axis_index("y")
        for k in range(shards):
            here = rows_of(lax.rem(y + k, shards), rows)
            out_refs[k][...] = (local_ref[here, :] - pushed_ref[here, :].astype(F32)).astype(BF)

    return call(kernel, tuple(like(rows, width, BF) for _ in range(shards)), "update", [local_term, pushed])


def copies(kernel, out, name, operands, count):
    def body(*refs):
        sems = refs[-1]
        started = []
        for i, (source, target) in enumerate(kernel(*refs[:-1])):
            copy = pltpu.make_async_copy(source, target, sems.at[i])
            copy.start()
            started.append(copy)
        for copy in started:
            copy.wait()

    moved = 2 * sum(x.size * x.dtype.itemsize for x in jax.tree.leaves(out))
    return pl.pallas_call(
        body,
        out_shape=out,
        in_specs=[HBM] * len(operands),
        out_specs=jax.tree.map(lambda _: VMEM, out),
        scratch_shapes=[pltpu.SemaphoreType.DMA((count,))],
        compiler_params=pltpu.CompilerParams(vmem_limit_bytes=16 << 20),
        cost_estimate=pl.CostEstimate(flops=0, bytes_accessed=moved, transcendentals=0),
        name=name,
    )(*[pltpu.with_memory_space_constraint(x, pltpu.HBM) for x in operands])


def prepare(gradient, out_inverse, out_coupling, shards):
    _, rows, width = gradient.shape
    width //= shards
    blocks = out_inverse.shape[1] // shards
    table = jax.ShapeDtypeStruct((blocks, BLK, BLK), BF)

    def kernel(grad_ref, inverse_ref, coupling_ref, *out_refs):
        y = lax.axis_index("y")
        mine = pl.ds(y * blocks, blocks)
        for k in range(shards):
            at = pl.multiple_of(lax.rem(y + k, shards) * width, BLK)
            yield grad_ref.at[0, :, pl.ds(at, width)], out_refs[k]
        yield inverse_ref.at[0, mine], out_refs[shards]
        yield coupling_ref.at[0, mine], out_refs[shards + 1]

    out = (*[like(rows, width, BF)] * shards, table, table)
    out = copies(kernel, out, "prepare", [gradient, out_inverse, out_coupling], shards + 2)
    return out[:shards], *out[shards:]


def assemble(pieces):
    rows, width = pieces[0].shape
    shards = len(pieces)

    def kernel(*refs):
        for k, owner in enumerate(owners_of(shards)):
            refs[shards][rows_of(owner, rows), :] = refs[k][...]

    return call(kernel, like(shards * rows, width, BF), "assemble", pieces)


def stack(parts):
    rows, width = parts[0].shape[1:]
    count = len(parts)

    def kernel(*refs):
        for i in range(count):
            yield refs[i].at[0], refs[count].at[pl.ds(i * rows, rows), :]

    return copies(kernel, like(count * rows, width, BF), "stack", parts, count)


def hop_y(x, by):
    size = lax.axis_size("y")
    return lax.ppermute(x, "y", [(i, (i + by) % size) for i in range(size)])


def exchange(pieces):
    return [pieces[0]] + [hop_y(pieces[k], k) for k in range(1, len(pieces))]


def after(x, *others):
    return lax.optimization_barrier((x, *others))[0]


def join_columns(pieces):
    rows, width = pieces[0].shape
    shards = len(pieces)

    def kernel(*refs):
        for k, owner in enumerate(owners_of(shards)):
            refs[shards][0, :, pl.ds(pl.multiple_of(owner * width, BLK), width)] = refs[k][...]

    return call(kernel, jax.ShapeDtypeStruct((1, rows, shards * width), BF), "join", pieces)


def gather_panel(tile):
    return lax.all_gather(tile.astype(HALF), "z", axis=0).astype(BF)


def local(gradient, in_inverse, in_coupling, in_carry, out_inverse, out_coupling):
    shards = lax.axis_size("y")
    slices, inv, psi = prepare(gradient, out_inverse, out_coupling, shards)
    pieces = exchange(slices)
    pair = stack([after(in_inverse, slices[0]), in_carry])
    grad = assemble(lax.optimization_barrier((*pieces, pair))[:shards])
    above = hop_layer(grad, -1)
    coupling = after(in_coupling, slices[0])[0]
    later = after(coupling, grad)
    coupling = [coupling] + [hop_y(coupling if k < 3 else later, k) for k in range(1, shards)]
    near = near_tile(above, psi, shards)
    pair = after(pair, grad)
    ahead, behind = hop_y(pair, 1), hop_y(pair, -1)
    panel = gather_panel(near)
    panel, ahead, behind = lax.optimization_barrier((panel, ahead, behind))
    reduced = reduced_tile(panel, coupling, grad, shards)
    factors = [pair, ahead, hop_y(behind, -1), behind]
    pushed, panel = pushed_tile(panel_pieces(ring_steps(reduced)), factors, inv, psi, shards)
    local_term = local_tile(panel, factors, inv, shards)
    return join_columns(exchange(update_pieces(local_term, hop_layer(pushed, 1), shards)))


def solution(mesh):
    layers = mesh.shape["layer"]
    fine = Mesh(np.asarray(mesh.devices).reshape(layers, 4, -1), ("layer", "y", "z"))
    rows = P("layer", ("y", "z"), None)
    table = P("layer", None, None, None)
    return jax.shard_map(
        local,
        mesh=fine,
        in_specs=(rows, rows, rows, rows, table, table),
        out_specs=rows,
        check_vma=False,
    )
```

```python
import jax
import jax.numpy as jnp
import numpy as np
from jax import lax
from jax.experimental import pallas as pl
from jax.experimental.pallas import tpu as pltpu
from jax.sharding import Mesh, PartitionSpec as P

BF = jnp.bfloat16
F32 = jnp.float32
HALF = jnp.float16
BLK = 128
CODE = 8
VMEM = pl.BlockSpec(memory_space=pltpu.VMEM)
HBM = pl.BlockSpec(memory_space=pltpu.HBM)


def call(kernel, out, name, operands, scratch=(), mib=16, flops=0, far=()):
    moved = sum(x.size * x.dtype.itemsize for x in operands) + sum(x.size * x.dtype.itemsize for x in jax.tree.leaves(out))
    return pl.pallas_call(
        kernel,
        out_shape=out,
        in_specs=[HBM if i in far else VMEM for i in range(len(operands))],
        out_specs=jax.tree.map(lambda _: VMEM, out),
        scratch_shapes=list(scratch),
        compiler_params=pltpu.CompilerParams(vmem_limit_bytes=mib << 20),
        cost_estimate=pl.CostEstimate(flops=flops, bytes_accessed=moved, transcendentals=0),
        name=name,
    )(*operands)


def like(rows, cols, dtype):
    return jax.ShapeDtypeStruct((rows, cols), dtype)


def hop_layer(x, by):
    size = lax.axis_size("layer")
    return lax.ppermute(x, "layer", [(i, i + by) for i in range(size) if 0 <= i + by < size])


def chunks_of(width):
    return [(at, min(256, width - at)) for at in range(0, width, 256)]


def store_scaled(out_ref, parts, owners, at):
    rows, width = parts[0].shape
    cols = pl.ds(at, width)
    line = lax.broadcasted_iota(jnp.int32, (CODE, width), 0)
    codes = jnp.full((CODE, width), 1.0, F32)
    for part, owner in zip(parts, owners, strict=True):
        top = jnp.max(jnp.abs(part), axis=0, keepdims=True)
        scale = jnp.ones_like(top)
        code = jnp.full_like(top, 128.0)
        for bits in (64, 32, 16, 8):
            small = top < 2.0 ** (15 - bits)
            grow = jnp.where(small, 2.0**bits, 1.0)
            top = top * grow
            scale = scale * grow
            code = code * jnp.where(small, 2.0 ** (-(bits // 8)), 1.0)
        out_ref[rows_of(owner, rows), cols] = (part * scale).astype(BF)
        codes = jnp.where(line == owner, code, codes)
    out_ref[pl.ds(len(parts) * rows, CODE), cols] = codes.astype(BF)


def rows_of(owner, rows):
    return pl.ds(owner * rows if isinstance(owner, int) else pl.multiple_of(owner * rows, 16), rows)


def blocks_of(values, count):
    rows = values.shape[0] // count
    return [values[k * rows : (k + 1) * rows] for k in range(count)]


def owners_of(shards):
    y = lax.axis_index("y")
    return [lax.rem(y + (shards - k), shards) for k in range(shards)]


def joined(pieces, rows, first=0):
    return jnp.concatenate([piece[pl.ds(first, rows), :] for piece in pieces], axis=0)


def load_scaled(in_ref, panel_ref, at, width, shards, rows):
    cols = pl.ds(at, width)
    count = in_ref.shape[0]
    for j in range(count):
        codes = in_ref[j, pl.ds(shards * rows, CODE), cols].astype(F32) * (1.0 / 128.0)
        codes = codes * codes
        codes = codes * codes
        codes = codes * codes
        for k in range(shards):
            part = in_ref[j, pl.ds(k * rows, rows), cols].astype(F32) * codes[k : k + 1]
            panel_ref[pl.ds((k * count + j) * rows, rows), cols] = part.astype(BF)


def near_tile(above, table, shards):
    tile, width = above.shape
    blocks = width // BLK

    def kernel(above_ref, table_ref, out_ref):
        for b in range(blocks):
            block = table_ref[b]
            near = lax.dot_general(
                above_ref[:, pl.ds(b * BLK, BLK)], block, (((1,), (1,)), ((), ())), preferred_element_type=F32
            )
            store_scaled(out_ref, blocks_of(near.astype(BF).astype(F32), shards), list(range(shards)), b * BLK)

    return call(kernel, like(tile + CODE, width, BF), "near", [above, table], flops=2 * tile * width * BLK)


def reduced_tile(panel, factor, grad, shards):
    tile, width = grad.shape
    depth, rows = factor[0].shape[1], tile // shards

    def kernel(panel_in, grad_ref, *refs):
        pieces, (out_ref, panel_ref) = refs[:shards], refs[shards:]
        owners = owners_of(shards)
        for at, w in chunks_of(width):
            cols = pl.ds(at, w)
            load_scaled(panel_in, panel_ref, at, w, shards, rows)
            coupled = jnp.dot(joined(pieces, rows), panel_ref[:, cols], preferred_element_type=F32)
            parts = [
                (grad_ref[rows_of(owner, rows), cols].astype(F32) - part).astype(BF).astype(F32)
                for owner, part in zip(owners, blocks_of(coupled, shards), strict=True)
            ]
            store_scaled(out_ref, parts, owners, at)

    return call(
        kernel,
        like(tile + CODE, width, BF),
        "reduced",
        [panel, grad, *factor],
        [pltpu.VMEM((depth, width), BF)],
        flops=2 * tile * depth * width,
    )


def pushed_tile(panel, factor, inverse, coupling, shards):
    rows, depth = factor[0].shape[0] // 2, factor[0].shape[1]
    tile, width = shards * rows, panel.shape[2]

    def kernel(panel_in, inverse_ref, coupling_ref, *refs):
        pieces, (pushed_ref, panel_ref) = refs[:shards], refs[shards:]
        owners = owners_of(shards)
        carried = []
        for at, w in chunks_of(width):
            load_scaled(panel_in, panel_ref, at, w, shards, rows)
            both = jnp.dot(joined(pieces, rows, rows), panel_ref[:, pl.ds(at, w)], preferred_element_type=F32)
            carried += [both[:, i : i + BLK].astype(BF) for i in range(0, w, BLK)]
        middle = [
            jnp.dot(x, inverse_ref[b], preferred_element_type=F32).astype(BF) for b, x in enumerate(carried)
        ]
        for b, x in enumerate(middle):
            pushed = jnp.dot(x, coupling_ref[b], preferred_element_type=F32).astype(BF)
            for owner, part in zip(owners, blocks_of(pushed, shards), strict=True):
                pushed_ref[rows_of(owner, rows), pl.ds(b * BLK, BLK)] = part

    return call(
        kernel,
        (like(tile, width, BF), like(depth, width, BF)),
        "pushed",
        [panel, inverse, coupling, *factor],
        flops=2 * tile * depth * width,
    )


def local_tile(panel, factor, inverse, shards):
    rows, depth = factor[0].shape[0] // 2, factor[0].shape[1]
    tile, width = shards * rows, panel.shape[1]

    def kernel(panel_ref, inverse_ref, *refs):
        pieces, (local_ref,) = refs[:shards], refs[shards:]
        owners = owners_of(shards)
        whitened = []
        for at, w in chunks_of(width):
            both = jnp.dot(joined(pieces, rows), panel_ref[:, pl.ds(at, w)], preferred_element_type=F32)
            whitened += [both[:, i : i + BLK].astype(BF) for i in range(0, w, BLK)]
        for b, x in enumerate(whitened):
            product = jnp.dot(x, inverse_ref[b], preferred_element_type=F32)
            for owner, part in zip(owners, blocks_of(product, shards), strict=True):
                local_ref[rows_of(owner, rows), pl.ds(b * BLK, BLK)] = part

    return call(
        kernel,
        like(tile, width, F32),
        "local",
        [panel, inverse, *factor],
        flops=2 * tile * depth * width,
    )


def update_pieces(local_term, pushed, shards):
    rows, width = pushed.shape[0] // shards, pushed.shape[1]

    def kernel(local_ref, pushed_ref, *out_refs):
        y = lax.axis_index("y")
        for k in range(shards):
            here = rows_of(lax.rem(y + k, shards), rows)
            out_refs[k][...] = (local_ref[here, :] - pushed_ref[here, :].astype(F32)).astype(BF)

    return call(kernel, tuple(like(rows, width, BF) for _ in range(shards)), "update", [local_term, pushed])


def copies(kernel, out, name, operands, count, near=HBM, far=VMEM):
    def body(*refs):
        sems = refs[-1]
        started = []
        for i, (source, target) in enumerate(kernel(*refs[:-1])):
            copy = pltpu.make_async_copy(source, target, sems.at[i])
            copy.start()
            started.append(copy)
        for copy in started:
            copy.wait()

    moved = 2 * sum(x.size * x.dtype.itemsize for x in jax.tree.leaves(out))
    return pl.pallas_call(
        body,
        out_shape=out,
        in_specs=[near] * len(operands),
        out_specs=jax.tree.map(lambda _: far, out),
        scratch_shapes=[pltpu.SemaphoreType.DMA((count,))],
        compiler_params=pltpu.CompilerParams(vmem_limit_bytes=16 << 20),
        cost_estimate=pl.CostEstimate(flops=0, bytes_accessed=moved, transcendentals=0),
        name=name,
    )(*[pltpu.with_memory_space_constraint(x, pltpu.HBM) if near is HBM else x for x in operands])


def prepare(gradient, out_inverse, out_coupling, shards):
    _, rows, width = gradient.shape
    width //= shards
    blocks = out_inverse.shape[1] // shards
    table = jax.ShapeDtypeStruct((blocks, BLK, BLK), BF)

    def kernel(grad_ref, inverse_ref, coupling_ref, *out_refs):
        y = lax.axis_index("y")
        mine = pl.ds(y * blocks, blocks)
        for k in range(shards):
            at = pl.multiple_of(lax.rem(y + k, shards) * width, BLK)
            yield grad_ref.at[0, :, pl.ds(at, width)], out_refs[k]
        yield inverse_ref.at[0, mine], out_refs[shards]
        yield coupling_ref.at[0, mine], out_refs[shards + 1]

    out = (*[like(rows, width, BF)] * shards, table, table)
    out = copies(kernel, out, "prepare", [gradient, out_inverse, out_coupling], shards + 2)
    return out[:shards], *out[shards:]


def assemble(pieces):
    rows, width = pieces[0].shape
    shards = len(pieces)

    def kernel(*refs):
        for k, owner in enumerate(owners_of(shards)):
            refs[shards][rows_of(owner, rows), :] = refs[k][...]

    return call(kernel, like(shards * rows, width, BF), "assemble", pieces)


def stack(parts):
    rows, width = parts[0].shape[1:]
    count = len(parts)

    def kernel(*refs):
        for i in range(count):
            yield refs[i].at[0], refs[count].at[pl.ds(i * rows, rows), :]

    return copies(kernel, like(count * rows, width, BF), "stack", parts, count)


def hop_y(x, by):
    size = lax.axis_size("y")
    return lax.ppermute(x, "y", [(i, (i + by) % size) for i in range(size)])


def exchange(pieces):
    return [pieces[0]] + [hop_y(pieces[k], k) for k in range(1, len(pieces))]


def after(x, *others):
    return lax.optimization_barrier((x, *others))[0]


def join_columns(pieces):
    rows, width = pieces[0].shape
    shards = len(pieces)

    def kernel(*refs):
        for k, owner in enumerate(owners_of(shards)):
            yield refs[k], refs[shards].at[0, :, pl.ds(pl.multiple_of(owner * width, BLK), width)]

    out = jax.ShapeDtypeStruct((1, rows, shards * width), BF)
    return copies(kernel, out, "join", pieces, shards, near=VMEM, far=HBM)


def gather_panel(tile):
    return lax.all_gather(tile.astype(HALF), "z", axis=0).astype(BF)


def local(gradient, in_inverse, in_coupling, in_carry, out_inverse, out_coupling):
    shards = lax.axis_size("y")
    slices, inv, psi = prepare(gradient, out_inverse, out_coupling, shards)
    pieces = exchange(slices)
    pair = stack([after(in_inverse, slices[0]), in_carry])
    grad = assemble(lax.optimization_barrier((*pieces, pair))[:shards])
    above = hop_layer(grad, -1)
    coupling = after(in_coupling, slices[0])[0]
    later = after(coupling, grad)
    coupling = [coupling] + [hop_y(coupling if k < 3 else later, k) for k in range(1, shards)]
    near = near_tile(above, psi, shards)
    pair = after(pair, grad)
    ahead, behind = hop_y(pair, 1), hop_y(pair, -1)
    panel = gather_panel(near)
    reduced = reduced_tile(panel, coupling, grad, shards)
    factors = [pair, ahead, hop_y(behind, -1), behind]
    pushed, panel = pushed_tile(gather_panel(reduced), factors, inv, psi, shards)
    local_term = local_tile(panel, factors, inv, shards)
    return join_columns(exchange(update_pieces(local_term, hop_layer(pushed, 1), shards)))


def solution(mesh):
    layers = mesh.shape["layer"]
    fine = Mesh(np.asarray(mesh.devices).reshape(layers, 4, -1), ("layer", "y", "z"))
    rows = P("layer", ("y", "z"), None)
    table = P("layer", None, None, None)
    return jax.shard_map(
        local,
        mesh=fine,
        in_specs=(rows, rows, rows, rows, table, table),
        out_specs=rows,
        check_vma=False,
    )
```

```python
import jax
import jax.numpy as jnp
import numpy as np
from jax import lax
from jax.experimental import pallas as pl
from jax.experimental.pallas import tpu as pltpu
from jax.sharding import Mesh, PartitionSpec as P

BF = jnp.bfloat16
F32 = jnp.float32
HALF = jnp.float16
BLK = 128
CODE = 8
VMEM = pl.BlockSpec(memory_space=pltpu.VMEM)
HBM = pl.BlockSpec(memory_space=pltpu.HBM)


def call(kernel, out, name, operands, scratch=(), mib=16, flops=0, far=()):
    moved = sum(x.size * x.dtype.itemsize for x in operands) + sum(x.size * x.dtype.itemsize for x in jax.tree.leaves(out))
    return pl.pallas_call(
        kernel,
        out_shape=out,
        in_specs=[HBM if i in far else VMEM for i in range(len(operands))],
        out_specs=jax.tree.map(lambda _: VMEM, out),
        scratch_shapes=list(scratch),
        compiler_params=pltpu.CompilerParams(vmem_limit_bytes=mib << 20),
        cost_estimate=pl.CostEstimate(flops=flops, bytes_accessed=moved, transcendentals=0),
        name=name,
    )(*operands)


def like(rows, cols, dtype):
    return jax.ShapeDtypeStruct((rows, cols), dtype)


def hop_layer(x, by):
    size = lax.axis_size("layer")
    return lax.ppermute(x, "layer", [(i, i + by) for i in range(size) if 0 <= i + by < size])


def chunks_of(width):
    return [(at, min(256, width - at)) for at in range(0, width, 256)]


def store_scaled(out_ref, parts, owners, at):
    rows, width = parts[0].shape
    cols = pl.ds(at, width)
    line = lax.broadcasted_iota(jnp.int32, (CODE, width), 0)
    codes = jnp.full((CODE, width), 1.0, F32)
    for part, owner in zip(parts, owners, strict=True):
        top = jnp.max(jnp.abs(part), axis=0, keepdims=True)
        scale = jnp.ones_like(top)
        code = jnp.full_like(top, 128.0)
        for bits in (64, 32, 16, 8):
            small = top < 2.0 ** (15 - bits)
            grow = jnp.where(small, 2.0**bits, 1.0)
            top = top * grow
            scale = scale * grow
            code = code * jnp.where(small, 2.0 ** (-(bits // 8)), 1.0)
        out_ref[rows_of(owner, rows), cols] = (part * scale).astype(BF)
        codes = jnp.where(line == owner, code, codes)
    out_ref[pl.ds(len(parts) * rows, CODE), cols] = codes.astype(BF)


def rows_of(owner, rows):
    return pl.ds(owner * rows if isinstance(owner, int) else pl.multiple_of(owner * rows, 16), rows)


def blocks_of(values, count):
    rows = values.shape[0] // count
    return [values[k * rows : (k + 1) * rows] for k in range(count)]


def owners_of(shards):
    y = lax.axis_index("y")
    return [lax.rem(y + (shards - k), shards) for k in distances(shards)]


def joined(pieces, rows, first=0):
    return jnp.concatenate([piece[pl.ds(first, rows), :] for piece in pieces], axis=0)


def load_scaled(in_ref, panel_ref, at, width, shards, rows):
    cols = pl.ds(at, width)
    count = in_ref.shape[0]
    for j in range(count):
        codes = in_ref[j, pl.ds(shards * rows, CODE), cols].astype(F32) * (1.0 / 128.0)
        codes = codes * codes
        codes = codes * codes
        codes = codes * codes
        for k in range(shards):
            part = in_ref[j, pl.ds(k * rows, rows), cols].astype(F32) * codes[k : k + 1]
            panel_ref[pl.ds((k * count + j) * rows, rows), cols] = part.astype(BF)


def near_tile(above, table, shards):
    tile, width = above.shape
    blocks = width // BLK

    def kernel(above_ref, table_ref, out_ref):
        for b in range(blocks):
            block = table_ref[b]
            near = lax.dot_general(
                above_ref[:, pl.ds(b * BLK, BLK)], block, (((1,), (1,)), ((), ())), preferred_element_type=F32
            )
            store_scaled(out_ref, blocks_of(near.astype(BF).astype(F32), shards), list(range(shards)), b * BLK)

    return call(kernel, like(tile + CODE, width, BF), "near", [above, table], flops=2 * tile * width * BLK)


def reduced_tile(panel, factor, grad, shards):
    tile, width = grad.shape
    depth, rows = factor[0].shape[1], tile // shards

    def kernel(panel_in, grad_ref, *refs):
        pieces, (out_ref, panel_ref) = refs[:shards], refs[shards:]
        owners = owners_of(shards)
        for at, w in chunks_of(width):
            cols = pl.ds(at, w)
            load_scaled(panel_in, panel_ref, at, w, shards, rows)
            coupled = jnp.dot(joined(pieces, rows), panel_ref[:, cols], preferred_element_type=F32)
            parts = [
                (grad_ref[rows_of(owner, rows), cols].astype(F32) - part).astype(BF).astype(F32)
                for owner, part in zip(owners, blocks_of(coupled, shards), strict=True)
            ]
            store_scaled(out_ref, parts, owners, at)

    return call(
        kernel,
        like(tile + CODE, width, BF),
        "reduced",
        [panel, grad, *factor],
        [pltpu.VMEM((depth, width), BF)],
        flops=2 * tile * depth * width,
    )


def pushed_tile(panel, factor, inverse, coupling, shards):
    rows, depth = factor[0].shape[0] // 2, factor[0].shape[1]
    tile, width = shards * rows, panel.shape[2]

    def kernel(panel_in, inverse_ref, coupling_ref, *refs):
        pieces, (pushed_ref, panel_ref) = refs[:shards], refs[shards:]
        owners = owners_of(shards)
        carried = []
        for at, w in chunks_of(width):
            load_scaled(panel_in, panel_ref, at, w, shards, rows)
            both = jnp.dot(joined(pieces, rows, rows), panel_ref[:, pl.ds(at, w)], preferred_element_type=F32)
            carried += [both[:, i : i + BLK].astype(BF) for i in range(0, w, BLK)]
        middle = [
            jnp.dot(x, inverse_ref[b], preferred_element_type=F32).astype(BF) for b, x in enumerate(carried)
        ]
        for b, x in enumerate(middle):
            pushed = jnp.dot(x, coupling_ref[b], preferred_element_type=F32).astype(BF)
            for owner, part in zip(owners, blocks_of(pushed, shards), strict=True):
                pushed_ref[rows_of(owner, rows), pl.ds(b * BLK, BLK)] = part

    return call(
        kernel,
        (like(tile, width, BF), like(depth, width, BF)),
        "pushed",
        [panel, inverse, coupling, *factor],
        flops=2 * tile * depth * width,
    )


def local_tile(panel, factor, inverse, shards):
    rows, depth = factor[0].shape[0] // 2, factor[0].shape[1]
    tile, width = shards * rows, panel.shape[1]

    def kernel(panel_ref, inverse_ref, *refs):
        pieces, (local_ref,) = refs[:shards], refs[shards:]
        owners = owners_of(shards)
        whitened = []
        for at, w in chunks_of(width):
            both = jnp.dot(joined(pieces, rows), panel_ref[:, pl.ds(at, w)], preferred_element_type=F32)
            whitened += [both[:, i : i + BLK].astype(BF) for i in range(0, w, BLK)]
        for b, x in enumerate(whitened):
            product = jnp.dot(x, inverse_ref[b], preferred_element_type=F32)
            for owner, part in zip(owners, blocks_of(product, shards), strict=True):
                local_ref[rows_of(owner, rows), pl.ds(b * BLK, BLK)] = part

    return call(
        kernel,
        like(tile, width, F32),
        "local",
        [panel, inverse, *factor],
        flops=2 * tile * depth * width,
    )


def update_pieces(local_term, pushed, shards):
    rows, width = pushed.shape[0] // shards, pushed.shape[1]

    def kernel(local_ref, pushed_ref, *out_refs):
        y = lax.axis_index("y")
        for k, out_ref in zip(distances(shards), out_refs, strict=True):
            here = rows_of(lax.rem(y + k, shards), rows)
            out_ref[...] = (local_ref[here, :] - pushed_ref[here, :].astype(F32)).astype(BF)

    return call(kernel, tuple(like(rows, width, BF) for _ in range(shards)), "update", [local_term, pushed])


def copies(kernel, out, name, operands, count, near=HBM, far=VMEM):
    def body(*refs):
        sems = refs[-1]
        started = []
        for i, (source, target) in enumerate(kernel(*refs[:-1])):
            copy = pltpu.make_async_copy(source, target, sems.at[i])
            copy.start()
            started.append(copy)
        for copy in started:
            copy.wait()

    moved = 2 * sum(x.size * x.dtype.itemsize for x in jax.tree.leaves(out))
    return pl.pallas_call(
        body,
        out_shape=out,
        in_specs=[near] * len(operands),
        out_specs=jax.tree.map(lambda _: far, out),
        scratch_shapes=[pltpu.SemaphoreType.DMA((count,))],
        compiler_params=pltpu.CompilerParams(vmem_limit_bytes=16 << 20),
        cost_estimate=pl.CostEstimate(flops=0, bytes_accessed=moved, transcendentals=0),
        name=name,
    )(*[pltpu.with_memory_space_constraint(x, pltpu.HBM) if near is HBM else x for x in operands])


def column_blocks(gradient, shards):
    _, rows, width = gradient.shape
    width //= shards

    def kernel(grad_ref, *out_refs):
        y = lax.axis_index("y")
        for k, out_ref in zip(distances(shards), out_refs, strict=True):
            at = pl.multiple_of(lax.rem(y + k, shards) * width, BLK)
            yield grad_ref.at[0, :, pl.ds(at, width)], out_ref

    return copies(kernel, (like(rows, width, BF),) * shards, "blocks", [gradient], shards)


def operands(in_inverse, in_carry, out_inverse, out_coupling, shards):
    _, rows, width = in_inverse.shape
    blocks = out_inverse.shape[1] // shards
    table = jax.ShapeDtypeStruct((blocks, BLK, BLK), BF)

    def kernel(first_ref, second_ref, inverse_ref, coupling_ref, pair_ref, inv_ref, psi_ref):
        mine = pl.ds(lax.axis_index("y") * blocks, blocks)
        yield first_ref.at[0], pair_ref.at[pl.ds(0, rows), :]
        yield second_ref.at[0], pair_ref.at[pl.ds(rows, rows), :]
        yield coupling_ref.at[0, mine], psi_ref
        yield inverse_ref.at[0, mine], inv_ref

    out = (like(2 * rows, width, BF), table, table)
    return copies(kernel, out, "operands", [in_inverse, in_carry, out_inverse, out_coupling], 4)


def assemble(pieces):
    rows, width = pieces[0].shape
    shards = len(pieces)

    def kernel(*refs):
        for k, owner in enumerate(owners_of(shards)):
            refs[shards][rows_of(owner, rows), :] = refs[k][...]

    return call(kernel, like(shards * rows, width, BF), "assemble", pieces)


def hop_y(x, by):
    size = lax.axis_size("y")
    return lax.ppermute(x, "y", [(i, (i + by) % size) for i in range(size)])


def distances(shards):
    return [0] + sorted(range(1, shards), key=lambda k: -min(k, shards - k))


def exchange(pieces):
    return [hop_y(piece, k) if k else piece for piece, k in zip(pieces, distances(len(pieces)), strict=True)]


def after(x, *others):
    return lax.optimization_barrier((x, *others))[0]


def join_columns(pieces):
    rows, width = pieces[0].shape
    shards = len(pieces)

    def kernel(*refs):
        for k, owner in enumerate(owners_of(shards)):
            yield refs[k], refs[shards].at[0, :, pl.ds(pl.multiple_of(owner * width, BLK), width)]

    out = jax.ShapeDtypeStruct((1, rows, shards * width), BF)
    return copies(kernel, out, "join", pieces, shards, near=VMEM, far=HBM)


def gather_panel(tile):
    return lax.all_gather(tile.astype(HALF), "z", axis=0).astype(BF)


def local(gradient, in_inverse, in_coupling, in_carry, out_inverse, out_coupling):
    shards = lax.axis_size("y")
    slices = column_blocks(gradient, shards)
    pieces = exchange(slices)
    pair, inv, psi = operands(after(in_inverse, slices[0]), in_carry, out_inverse, out_coupling, shards)
    grad = assemble(lax.optimization_barrier((*pieces, pair))[:shards])
    above = hop_layer(grad, -1)
    coupling = after(in_coupling, grad)[0]
    coupling = exchange([coupling] * shards)
    near = near_tile(above, psi, shards)
    pair = after(pair, grad)
    ahead, behind = hop_y(pair, 1), hop_y(pair, -1)
    reduced = reduced_tile(gather_panel(near), coupling, grad, shards)
    factors = [pair, hop_y(behind, -1), ahead, behind]
    pushed, panel = pushed_tile(gather_panel(reduced), factors, inv, psi, shards)
    local_term = local_tile(panel, factors, inv, shards)
    return join_columns(exchange(update_pieces(local_term, hop_layer(pushed, 1), shards)))


def solution(mesh):
    layers = mesh.shape["layer"]
    fine = Mesh(np.asarray(mesh.devices).reshape(layers, 4, -1), ("layer", "y", "z"))
    rows = P("layer", ("y", "z"), None)
    table = P("layer", None, None, None)
    return jax.shard_map(
        local,
        mesh=fine,
        in_specs=(rows, rows, rows, rows, table, table),
        out_specs=rows,
        check_vma=False,
    )
```

```python
import jax
import jax.numpy as jnp
import numpy as np
from jax import lax
from jax.experimental import pallas as pl
from jax.experimental.pallas import tpu as pltpu
from jax.sharding import Mesh, PartitionSpec as P

BF = jnp.bfloat16
F32 = jnp.float32
HALF = jnp.float16
BLK = 128
CODE = 8
VMEM = pl.BlockSpec(memory_space=pltpu.VMEM)
HBM = pl.BlockSpec(memory_space=pltpu.HBM)


def call(kernel, out, name, operands, scratch=(), mib=16, flops=0, far=()):
    moved = sum(x.size * x.dtype.itemsize for x in operands) + sum(x.size * x.dtype.itemsize for x in jax.tree.leaves(out))
    return pl.pallas_call(
        kernel,
        out_shape=out,
        in_specs=[HBM if i in far else VMEM for i in range(len(operands))],
        out_specs=jax.tree.map(lambda _: VMEM, out),
        scratch_shapes=list(scratch),
        compiler_params=pltpu.CompilerParams(vmem_limit_bytes=mib << 20),
        cost_estimate=pl.CostEstimate(flops=flops, bytes_accessed=moved, transcendentals=0),
        name=name,
    )(*operands)


def like(rows, cols, dtype):
    return jax.ShapeDtypeStruct((rows, cols), dtype)


def hop_layer(x, by):
    size = lax.axis_size("layer")
    return lax.ppermute(x, "layer", [(i, i + by) for i in range(size) if 0 <= i + by < size])


def chunks_of(width):
    return [(at, min(256, width - at)) for at in range(0, width, 256)]


def store_scaled(out_ref, parts, owners, at):
    rows, width = parts[0].shape
    cols = pl.ds(at, width)
    line = lax.broadcasted_iota(jnp.int32, (CODE, width), 0)
    codes = jnp.full((CODE, width), 1.0, F32)
    for part, owner in zip(parts, owners, strict=True):
        top = jnp.max(jnp.abs(part), axis=0, keepdims=True)
        scale = jnp.ones_like(top)
        code = jnp.full_like(top, 128.0)
        for bits in (64, 32, 16, 8):
            small = top < 2.0 ** (15 - bits)
            grow = jnp.where(small, 2.0**bits, 1.0)
            top = top * grow
            scale = scale * grow
            code = code * jnp.where(small, 2.0 ** (-(bits // 8)), 1.0)
        out_ref[rows_of(owner, rows), cols] = (part * scale).astype(BF)
        codes = jnp.where(line == owner, code, codes)
    out_ref[pl.ds(len(parts) * rows, CODE), cols] = codes.astype(BF)


def rows_of(owner, rows):
    return pl.ds(owner * rows if isinstance(owner, int) else pl.multiple_of(owner * rows, 16), rows)


def blocks_of(values, count):
    rows = values.shape[0] // count
    return [values[k * rows : (k + 1) * rows] for k in range(count)]


def owners_of(shards):
    y = lax.axis_index("y")
    return [lax.rem(y + (shards - k), shards) for k in distances(shards)]


def joined(pieces, rows, last=None):
    firsts = [piece.shape[0] - last if last else 0 for piece in pieces]
    return jnp.concatenate([piece[pl.ds(first, rows), :] for first, piece in zip(firsts, pieces, strict=True)], axis=0)


def load_scaled(in_ref, panel_ref, at, width, shards, rows):
    cols = pl.ds(at, width)
    count = in_ref.shape[0]
    for j in range(count):
        codes = in_ref[j, pl.ds(shards * rows, CODE), cols].astype(F32) * (1.0 / 128.0)
        codes = codes * codes
        codes = codes * codes
        codes = codes * codes
        for k in range(shards):
            undo = jnp.broadcast_to(codes[k : k + 1], (rows, width)).astype(BF)
            panel_ref[pl.ds((k * count + j) * rows, rows), cols] = in_ref[j, pl.ds(k * rows, rows), cols] * undo


def near_tile(above, table, shards):
    tile, width = above.shape
    blocks = width // BLK

    def kernel(above_ref, table_ref, out_ref):
        for b in range(blocks):
            block = table_ref[b]
            near = lax.dot_general(
                above_ref[:, pl.ds(b * BLK, BLK)], block, (((1,), (1,)), ((), ())), preferred_element_type=F32
            )
            store_scaled(out_ref, blocks_of(near.astype(BF).astype(F32), shards), list(range(shards)), b * BLK)

    return call(kernel, like(tile + CODE, width, BF), "near", [above, table], flops=2 * tile * width * BLK)


def reduced_tile(panel, factor, grad, shards):
    tile, width = grad.shape
    depth, rows = factor[0].shape[1], tile // shards

    def kernel(panel_in, grad_ref, *refs):
        pieces, (out_ref, panel_ref) = refs[:shards], refs[shards:]
        owners = owners_of(shards)
        for at, w in chunks_of(width):
            cols = pl.ds(at, w)
            load_scaled(panel_in, panel_ref, at, w, shards, rows)
            coupled = jnp.dot(joined(pieces, rows), panel_ref[:, cols], preferred_element_type=F32)
            parts = [
                (grad_ref[rows_of(owner, rows), cols].astype(F32) - part).astype(BF).astype(F32)
                for owner, part in zip(owners, blocks_of(coupled, shards), strict=True)
            ]
            store_scaled(out_ref, parts, owners, at)

    return call(
        kernel,
        like(tile + CODE, width, BF),
        "reduced",
        [panel, grad, *factor],
        [pltpu.VMEM((depth, width), BF)],
        flops=2 * tile * depth * width,
    )


def pushed_tile(panel, factor, inverse, coupling, shards):
    rows, depth = factor[0].shape[0] // 2, factor[0].shape[1]
    tile, width = shards * rows, panel.shape[2]

    def kernel(panel_in, inverse_ref, coupling_ref, *refs):
        pieces, (pushed_ref, panel_ref) = refs[:shards], refs[shards:]
        owners = owners_of(shards)
        carried = []
        for at, w in chunks_of(width):
            load_scaled(panel_in, panel_ref, at, w, shards, rows)
            both = jnp.dot(joined(pieces, rows, rows), panel_ref[:, pl.ds(at, w)], preferred_element_type=F32)
            carried += [both[:, i : i + BLK].astype(BF) for i in range(0, w, BLK)]
        middle = [
            jnp.dot(x, inverse_ref[b], preferred_element_type=F32).astype(BF) for b, x in enumerate(carried)
        ]
        for b, x in enumerate(middle):
            pushed = jnp.dot(x, coupling_ref[b], preferred_element_type=F32).astype(BF)
            for owner, part in zip(owners, blocks_of(pushed, shards), strict=True):
                pushed_ref[rows_of(owner, rows), pl.ds(b * BLK, BLK)] = part

    return call(
        kernel,
        (like(tile, width, BF), like(depth, width, BF)),
        "pushed",
        [panel, inverse, coupling, *factor],
        flops=2 * tile * depth * width,
    )


def local_tile(panel, factor, inverse, shards):
    rows, depth = factor[0].shape[0] // 2, factor[0].shape[1]
    tile, width = shards * rows, panel.shape[1]

    def kernel(panel_ref, inverse_ref, *refs):
        pieces, (local_ref,) = refs[:shards], refs[shards:]
        owners = owners_of(shards)
        whitened = []
        for at, w in chunks_of(width):
            both = jnp.dot(joined(pieces, rows, 2 * rows), panel_ref[:, pl.ds(at, w)], preferred_element_type=F32)
            whitened += [both[:, i : i + BLK].astype(BF) for i in range(0, w, BLK)]
        for b, x in enumerate(whitened):
            product = jnp.dot(x, inverse_ref[b], preferred_element_type=F32)
            for owner, part in zip(owners, blocks_of(product, shards), strict=True):
                local_ref[rows_of(owner, rows), pl.ds(b * BLK, BLK)] = part

    return call(
        kernel,
        like(tile, width, F32),
        "local",
        [panel, inverse, *factor],
        flops=2 * tile * depth * width,
    )


def update_pieces(local_term, pushed, shards):
    rows, width = pushed.shape[0] // shards, pushed.shape[1]

    def kernel(local_ref, pushed_ref, *out_refs):
        y = lax.axis_index("y")
        for k, out_ref in zip(distances(shards), out_refs, strict=True):
            here = rows_of(lax.rem(y + k, shards), rows)
            out_ref[...] = (local_ref[here, :] - pushed_ref[here, :].astype(F32)).astype(BF)

    return call(kernel, tuple(like(rows, width, BF) for _ in range(shards)), "update", [local_term, pushed])


def copies(kernel, out, name, operands, count, near=HBM, far=VMEM):
    def body(*refs):
        sems = refs[-1]
        started = []
        for i, (source, target) in enumerate(kernel(*refs[:-1])):
            copy = pltpu.make_async_copy(source, target, sems.at[i])
            copy.start()
            started.append(copy)
        for copy in started:
            copy.wait()

    moved = 2 * sum(x.size * x.dtype.itemsize for x in jax.tree.leaves(out))
    return pl.pallas_call(
        body,
        out_shape=out,
        in_specs=[near] * len(operands),
        out_specs=jax.tree.map(lambda _: far, out),
        scratch_shapes=[pltpu.SemaphoreType.DMA((count,))],
        compiler_params=pltpu.CompilerParams(vmem_limit_bytes=16 << 20),
        cost_estimate=pl.CostEstimate(flops=0, bytes_accessed=moved, transcendentals=0),
        name=name,
    )(*[pltpu.with_memory_space_constraint(x, pltpu.HBM) if near is HBM else x for x in operands])


def column_blocks(gradient, shards):
    _, rows, width = gradient.shape
    width //= shards

    def kernel(grad_ref, *out_refs):
        y = lax.axis_index("y")
        for k, out_ref in zip(distances(shards), out_refs, strict=True):
            at = pl.multiple_of(lax.rem(y + k, shards) * width, BLK)
            yield grad_ref.at[0, :, pl.ds(at, width)], out_ref

    return copies(kernel, (like(rows, width, BF),) * shards, "blocks", [gradient], shards)


def operands(in_coupling, in_inverse, in_carry, out_inverse, out_coupling, shards):
    _, rows, width = in_inverse.shape
    blocks = out_inverse.shape[1] // shards
    table = jax.ShapeDtypeStruct((blocks, BLK, BLK), BF)

    def kernel(rows_ref, first_ref, second_ref, inverse_ref, coupling_ref, pair_ref, trio_ref, inv_ref, psi_ref):
        mine = pl.ds(lax.axis_index("y") * blocks, blocks)
        for i, ref in enumerate((rows_ref, first_ref, second_ref)):
            yield ref.at[0], trio_ref.at[pl.ds(i * rows, rows), :]
            if i:
                yield ref.at[0], pair_ref.at[pl.ds((i - 1) * rows, rows), :]
        yield coupling_ref.at[0, mine], psi_ref
        yield inverse_ref.at[0, mine], inv_ref

    out = (like(2 * rows, width, BF), like(3 * rows, width, BF), table, table)
    return copies(kernel, out, "operands", [in_coupling, in_inverse, in_carry, out_inverse, out_coupling], 7)


def assemble(pieces):
    rows, width = pieces[0].shape
    shards = len(pieces)

    def kernel(*refs):
        for k, owner in enumerate(owners_of(shards)):
            refs[shards][rows_of(owner, rows), :] = refs[k][...]

    return call(kernel, like(shards * rows, width, BF), "assemble", pieces)


def hop_y(x, by):
    size = lax.axis_size("y")
    return lax.ppermute(x, "y", [(i, (i + by) % size) for i in range(size)])


def distances(shards):
    return [0] + sorted(range(1, shards), key=lambda k: -min(k, shards - k))


def exchange(pieces):
    return [hop_y(piece, k) if k else piece for piece, k in zip(pieces, distances(len(pieces)), strict=True)]


def after(x, *others):
    return lax.optimization_barrier((x, *others))[0]


def join_columns(pieces):
    rows, width = pieces[0].shape
    shards = len(pieces)

    def kernel(*refs):
        for k, owner in enumerate(owners_of(shards)):
            yield refs[k], refs[shards].at[0, :, pl.ds(pl.multiple_of(owner * width, BLK), width)]

    out = jax.ShapeDtypeStruct((1, rows, shards * width), BF)
    return copies(kernel, out, "join", pieces, shards, near=VMEM, far=HBM)


def gather_panel(tile):
    return lax.all_gather(tile.astype(HALF), "z", axis=0).astype(BF)


def local(gradient, in_inverse, in_coupling, in_carry, out_inverse, out_coupling):
    shards = lax.axis_size("y")
    slices = column_blocks(gradient, shards)
    pieces = exchange(slices)
    first = after(in_coupling, slices[0])
    pair, trio, inv, psi = operands(first, in_inverse, in_carry, out_inverse, out_coupling, shards)
    grad = assemble(lax.optimization_barrier((*pieces, pair))[:shards])
    above = hop_layer(grad, -1)
    pair, trio, own = lax.optimization_barrier((pair, trio, in_coupling[0], grad))[:3]
    ahead, behind = hop_y(pair, 1), hop_y(trio, -1)
    coupling = [own, hop_y(own, 2), hop_y(own, 1), behind]
    near = near_tile(above, psi, shards)
    reduced = reduced_tile(gather_panel(near), coupling, grad, shards)
    factors = [pair, hop_y(behind, -1), ahead, behind]
    pushed, panel = pushed_tile(gather_panel(reduced), factors, inv, psi, shards)
    local_term = local_tile(panel, factors, inv, shards)
    return join_columns(exchange(update_pieces(local_term, hop_layer(pushed, 1), shards)))


def solution(mesh):
    layers = mesh.shape["layer"]
    fine = Mesh(np.asarray(mesh.devices).reshape(layers, 4, -1), ("layer", "y", "z"))
    rows = P("layer", ("y", "z"), None)
    table = P("layer", None, None, None)
    return jax.shard_map(
        local,
        mesh=fine,
        in_specs=(rows, rows, rows, rows, table, table),
        out_specs=rows,
        check_vma=False,
    )
```

```python
import jax
import jax.numpy as jnp
import numpy as np
from jax import lax
from jax.experimental import pallas as pl
from jax.experimental.pallas import tpu as pltpu
from jax.sharding import Mesh, PartitionSpec as P

BF = jnp.bfloat16
F32 = jnp.float32
HALF = jnp.float16
BLK = 128
CODE = 8
VMEM = pl.BlockSpec(memory_space=pltpu.VMEM)
HBM = pl.BlockSpec(memory_space=pltpu.HBM)


def call(kernel, out, name, operands, scratch=(), mib=16, flops=0, far=()):
    moved = sum(x.size * x.dtype.itemsize for x in operands) + sum(x.size * x.dtype.itemsize for x in jax.tree.leaves(out))
    return pl.pallas_call(
        kernel,
        out_shape=out,
        in_specs=[HBM if i in far else VMEM for i in range(len(operands))],
        out_specs=jax.tree.map(lambda _: VMEM, out),
        scratch_shapes=list(scratch),
        compiler_params=pltpu.CompilerParams(vmem_limit_bytes=mib << 20),
        cost_estimate=pl.CostEstimate(flops=flops, bytes_accessed=moved, transcendentals=0),
        name=name,
    )(*operands)


def like(rows, cols, dtype):
    return jax.ShapeDtypeStruct((rows, cols), dtype)


def hop_layer(x, by):
    size = lax.axis_size("layer")
    return lax.ppermute(x, "layer", [(i, i + by) for i in range(size) if 0 <= i + by < size])


def chunks_of(width):
    return [(at, min(256, width - at)) for at in range(0, width, 256)]


def store_scaled(out_ref, parts, owners, at):
    rows, width = parts[0].shape
    cols = pl.ds(at, width)
    line = lax.broadcasted_iota(jnp.int32, (CODE, width), 0)
    codes = jnp.full((CODE, width), 1.0, F32)
    for part, owner in zip(parts, owners, strict=True):
        top = jnp.max(jnp.abs(part), axis=0, keepdims=True)
        scale = jnp.ones_like(top)
        code = jnp.full_like(top, 128.0)
        for bits in (64, 32, 16, 8):
            small = top < 2.0 ** (15 - bits)
            grow = jnp.where(small, 2.0**bits, 1.0)
            top = top * grow
            scale = scale * grow
            code = code * jnp.where(small, 2.0 ** (-(bits // 8)), 1.0)
        out_ref[rows_of(owner, rows), cols] = (part * scale).astype(BF)
        codes = jnp.where(line == owner, code, codes)
    out_ref[pl.ds(len(parts) * rows, CODE), cols] = codes.astype(BF)


def rows_of(owner, rows):
    return pl.ds(owner * rows if isinstance(owner, int) else pl.multiple_of(owner * rows, 16), rows)


def blocks_of(values, count):
    rows = values.shape[0] // count
    return [values[k * rows : (k + 1) * rows] for k in range(count)]


def owners_of(shards):
    y = lax.axis_index("y")
    return [lax.rem(y + (shards - k), shards) for k in distances(shards)]


def joined(pieces, rows, last=None):
    firsts = [piece.shape[0] - last if last else 0 for piece in pieces]
    return jnp.concatenate([piece[pl.ds(first, rows), :] for first, piece in zip(firsts, pieces, strict=True)], axis=0)


def load_scaled(in_ref, panel_ref, at, width, shards, rows):
    cols = pl.ds(at, width)
    count = in_ref.shape[0]
    for j in range(count):
        codes = in_ref[j, pl.ds(shards * rows, CODE), cols].astype(F32) * (1.0 / 128.0)
        codes = codes * codes
        codes = codes * codes
        codes = codes * codes
        for k in range(shards):
            undo = jnp.broadcast_to(codes[k : k + 1], (rows, width)).astype(BF)
            panel_ref[pl.ds((k * count + j) * rows, rows), cols] = in_ref[j, pl.ds(k * rows, rows), cols] * undo


def near_tile(halves, table, shards):
    part, width = halves[0].shape
    tile = part * len(halves)
    rows = tile // shards

    def kernel(*refs):
        above_refs, (table_ref, out_ref) = refs[: len(halves)], refs[len(halves) :]
        owners = owners_of(shards)
        for b in range(width // BLK):
            parts = []
            for ref in above_refs:
                near = lax.dot_general(
                    ref[:, pl.ds(b * BLK, BLK)], table_ref[b], (((1,), (1,)), ((), ())), preferred_element_type=F32
                )
                parts += blocks_of(near.astype(BF).astype(F32), part // rows)
            store_scaled(out_ref, parts, owners, b * BLK)

    return call(kernel, like(tile + CODE, width, BF), "near", [*halves, table], flops=2 * tile * width * BLK)


def reduced_tile(panel, factor, halves, shards):
    part, width = halves[0].shape
    tile = part * len(halves)
    depth, rows = factor[0].shape[1], tile // shards

    def kernel(panel_in, *refs):
        pieces, grad_refs, (out_ref, panel_ref) = refs[:shards], refs[shards:-2], refs[-2:]
        owners = owners_of(shards)
        for at, w in chunks_of(width):
            cols = pl.ds(at, w)
            load_scaled(panel_in, panel_ref, at, w, shards, rows)
            coupled = jnp.dot(joined(pieces, rows), panel_ref[:, cols], preferred_element_type=F32)
            grads = [ref[pl.ds(at_row, rows), cols] for ref in grad_refs for at_row in range(0, part, rows)]
            parts = [
                (grad.astype(F32) - block).astype(BF).astype(F32)
                for grad, block in zip(grads, blocks_of(coupled, shards), strict=True)
            ]
            store_scaled(out_ref, parts, owners, at)

    return call(
        kernel,
        like(tile + CODE, width, BF),
        "reduced",
        [panel, *factor, *halves],
        [pltpu.VMEM((depth, width), BF)],
        flops=2 * tile * depth * width,
    )


def halves_out(shards):
    order = distances(shards)
    order = order[1:] + order[:1]
    return order[: shards // 2], order[shards // 2 :]


def places_out(shards):
    halves = halves_out(shards)
    where = {k: (half, place) for half, ks in enumerate(halves) for place, k in enumerate(ks)}
    return [where[(shards - k) % shards] for k in distances(shards)]


def pushed_tile(panel, factor, inverse, coupling, shards):
    rows, depth = factor[0].shape[0] // 2, factor[0].shape[1]
    tile, width = shards * rows, panel.shape[2]

    def kernel(panel_in, inverse_ref, coupling_ref, *refs):
        pieces, (*pushed_refs, panel_ref) = refs[:shards], refs[shards:]
        carried = []
        for at, w in chunks_of(width):
            load_scaled(panel_in, panel_ref, at, w, shards, rows)
            both = jnp.dot(joined(pieces, rows, rows), panel_ref[:, pl.ds(at, w)], preferred_element_type=F32)
            carried += [both[:, i : i + BLK].astype(BF) for i in range(0, w, BLK)]
        middle = [
            jnp.dot(x, inverse_ref[b], preferred_element_type=F32).astype(BF) for b, x in enumerate(carried)
        ]
        for b, x in enumerate(middle):
            pushed = jnp.dot(x, coupling_ref[b], preferred_element_type=F32).astype(BF)
            for (half, place), part in zip(places_out(shards), blocks_of(pushed, shards), strict=True):
                pushed_refs[half][pl.ds(place * rows, rows), pl.ds(b * BLK, BLK)] = part

    return call(
        kernel,
        (*[like(tile // 2, width, BF)] * 2, like(depth, width, BF)),
        "pushed",
        [panel, inverse, coupling, *factor],
        flops=2 * tile * depth * width,
    )


def local_tile(panel, factor, inverse, shards):
    rows, depth = factor[0].shape[0] // 2, factor[0].shape[1]
    tile, width = shards * rows, panel.shape[1]

    def kernel(panel_ref, inverse_ref, *refs):
        pieces, local_refs = refs[:shards], refs[shards:]
        whitened = []
        for at, w in chunks_of(width):
            both = jnp.dot(joined(pieces, rows, 2 * rows), panel_ref[:, pl.ds(at, w)], preferred_element_type=F32)
            whitened += [both[:, i : i + BLK].astype(BF) for i in range(0, w, BLK)]
        for b, x in enumerate(whitened):
            product = jnp.dot(x, inverse_ref[b], preferred_element_type=F32)
            for (half, place), part in zip(places_out(shards), blocks_of(product, shards), strict=True):
                local_refs[half][pl.ds(place * rows, rows), pl.ds(b * BLK, BLK)] = part

    return call(
        kernel,
        (like(tile // 2, width, F32),) * 2,
        "local",
        [panel, inverse, *factor],
        flops=2 * tile * depth * width,
    )


def update_pieces(local_term, pushed, count, name):
    rows, width = pushed.shape[0] // count, pushed.shape[1]

    def kernel(local_ref, pushed_ref, *out_refs):
        for i, out_ref in enumerate(out_refs):
            here = pl.ds(i * rows, rows)
            out_ref[...] = (local_ref[here, :] - pushed_ref[here, :].astype(F32)).astype(BF)

    return call(kernel, tuple(like(rows, width, BF) for _ in range(count)), name, [local_term, pushed])


def copies(kernel, out, name, operands, count, near=HBM, far=VMEM):
    def body(*refs):
        sems = refs[-1]
        started = []
        for i, (source, target) in enumerate(kernel(*refs[:-1])):
            copy = pltpu.make_async_copy(source, target, sems.at[i])
            copy.start()
            started.append(copy)
        for copy in started:
            copy.wait()

    moved = 2 * sum(x.size * x.dtype.itemsize for x in jax.tree.leaves(out))
    return pl.pallas_call(
        body,
        out_shape=out,
        in_specs=[near] * len(operands),
        out_specs=jax.tree.map(lambda _: far, out),
        scratch_shapes=[pltpu.SemaphoreType.DMA((count,))],
        compiler_params=pltpu.CompilerParams(vmem_limit_bytes=16 << 20),
        cost_estimate=pl.CostEstimate(flops=0, bytes_accessed=moved, transcendentals=0),
        name=name,
    )(*[pltpu.with_memory_space_constraint(x, pltpu.HBM) if near is HBM else x for x in operands])


def column_blocks(gradient, shards):
    _, rows, width = gradient.shape
    width //= shards

    def kernel(grad_ref, *out_refs):
        y = lax.axis_index("y")
        for k, out_ref in zip(distances(shards), out_refs, strict=True):
            at = pl.multiple_of(lax.rem(y + k, shards) * width, BLK)
            yield grad_ref.at[0, :, pl.ds(at, width)], out_ref

    return copies(kernel, (like(rows, width, BF),) * shards, "blocks", [gradient], shards)


def operands(in_coupling, in_inverse, in_carry, out_inverse, out_coupling, shards):
    _, rows, width = in_inverse.shape
    blocks = out_inverse.shape[1] // shards
    table = jax.ShapeDtypeStruct((blocks, BLK, BLK), BF)

    def kernel(rows_ref, first_ref, second_ref, inverse_ref, coupling_ref, pair_ref, trio_ref, inv_ref, psi_ref):
        mine = pl.ds(lax.axis_index("y") * blocks, blocks)
        for i, ref in enumerate((rows_ref, first_ref, second_ref)):
            yield ref.at[0], trio_ref.at[pl.ds(i * rows, rows), :]
            if i:
                yield ref.at[0], pair_ref.at[pl.ds((i - 1) * rows, rows), :]
        yield coupling_ref.at[0, mine], psi_ref
        yield inverse_ref.at[0, mine], inv_ref

    out = (like(2 * rows, width, BF), like(3 * rows, width, BF), table, table)
    return copies(kernel, out, "operands", [in_coupling, in_inverse, in_carry, out_inverse, out_coupling], 7)


def stacked(pieces, name):
    rows, width = pieces[0].shape
    count = len(pieces)

    def kernel(*refs):
        for i in range(count):
            refs[count][pl.ds(i * rows, rows), :] = refs[i][...]

    return call(kernel, like(count * rows, width, BF), name, pieces)


def hop_y(x, by):
    size = lax.axis_size("y")
    return lax.ppermute(x, "y", [(i, (i + by) % size) for i in range(size)])


def distances(shards):
    return [0] + sorted(range(1, shards), key=lambda k: -min(k, shards - k))


def exchange(pieces):
    return [hop_y(piece, k) if k else piece for piece, k in zip(pieces, distances(len(pieces)), strict=True)]


def after(x, *others):
    return lax.optimization_barrier((x, *others))[0]


def join_columns(pieces):
    rows, width = pieces[0].shape
    shards = len(pieces)

    def kernel(*refs):
        for k, owner in enumerate(owners_of(shards)):
            yield refs[k], refs[shards].at[0, :, pl.ds(pl.multiple_of(owner * width, BLK), width)]

    out = jax.ShapeDtypeStruct((1, rows, shards * width), BF)
    return copies(kernel, out, "join", pieces, shards, near=VMEM, far=HBM)


def gather_panel(tile):
    return lax.all_gather(tile.astype(HALF), "z", axis=0).astype(BF)


def local(gradient, in_inverse, in_coupling, in_carry, out_inverse, out_coupling):
    shards = lax.axis_size("y")
    slices = column_blocks(gradient, shards)
    pieces = exchange(slices)
    first = after(in_coupling, slices[0])
    pair, trio, inv, psi = operands(first, in_inverse, in_carry, out_inverse, out_coupling, shards)
    half = shards // 2
    grads = [stacked(lax.optimization_barrier((*pieces[:half], pair))[:half], "early"), stacked(pieces[half:], "late")]
    above = [hop_layer(grad, -1) for grad in grads]
    pair, trio, own = lax.optimization_barrier((pair, trio, in_coupling[0], *grads))[:3]
    ahead, behind = hop_y(pair, 1), hop_y(trio, -1)
    coupling = [own, hop_y(own, 2), hop_y(own, 1), behind]
    near = near_tile(above, psi, shards)
    reduced = reduced_tile(gather_panel(near), coupling, grads, shards)
    factors = [pair, hop_y(behind, -1), ahead, behind]
    *pushed, panel = pushed_tile(gather_panel(reduced), factors, inv, psi, shards)
    pushed = [hop_layer(x, 1) for x in pushed]
    local_terms = local_tile(panel, factors, inv, shards)
    came = {}
    for ks, mine, below, name in zip(halves_out(shards), local_terms, pushed, ("update_a", "update_b"), strict=True):
        for k, piece in zip(ks, update_pieces(mine, below, len(ks), name), strict=True):
            came[k] = hop_y(piece, k) if k else piece
    return join_columns([came[k] for k in distances(shards)])


def solution(mesh):
    layers = mesh.shape["layer"]
    fine = Mesh(np.asarray(mesh.devices).reshape(layers, 4, -1), ("layer", "y", "z"))
    rows = P("layer", ("y", "z"), None)
    table = P("layer", None, None, None)
    return jax.shard_map(
        local,
        mesh=fine,
        in_specs=(rows, rows, rows, rows, table, table),
        out_specs=rows,
        check_vma=False,
    )
```

```python
import jax
import jax.numpy as jnp
import numpy as np
from jax import lax
from jax.experimental import pallas as pl
from jax.experimental.pallas import tpu as pltpu
from jax.sharding import Mesh, PartitionSpec as P

BF = jnp.bfloat16
F32 = jnp.float32
HALF = jnp.float16
BLK = 128
CODE = 8
VMEM = pl.BlockSpec(memory_space=pltpu.VMEM)
HBM = pl.BlockSpec(memory_space=pltpu.HBM)


def call(kernel, out, name, operands, scratch=(), mib=16, flops=0, far=()):
    moved = sum(x.size * x.dtype.itemsize for x in operands) + sum(x.size * x.dtype.itemsize for x in jax.tree.leaves(out))
    return pl.pallas_call(
        kernel,
        out_shape=out,
        in_specs=[HBM if i in far else VMEM for i in range(len(operands))],
        out_specs=jax.tree.map(lambda _: VMEM, out),
        scratch_shapes=list(scratch),
        compiler_params=pltpu.CompilerParams(vmem_limit_bytes=mib << 20),
        cost_estimate=pl.CostEstimate(flops=flops, bytes_accessed=moved, transcendentals=0),
        name=name,
    )(*operands)


def like(rows, cols, dtype):
    return jax.ShapeDtypeStruct((rows, cols), dtype)


def hop_layer(x, by):
    size = lax.axis_size("layer")
    return lax.ppermute(x, "layer", [(i, i + by) for i in range(size) if 0 <= i + by < size])


def chunks_of(width):
    return [(at, min(256, width - at)) for at in range(0, width, 256)]


def store_scaled(out_ref, parts, owners, at):
    rows, width = parts[0].shape
    cols = pl.ds(at, width)
    line = lax.broadcasted_iota(jnp.int32, (CODE, width), 0)
    codes = jnp.full((CODE, width), 1.0, F32)
    for part, owner in zip(parts, owners, strict=True):
        top = jnp.max(jnp.abs(part), axis=0, keepdims=True)
        scale = jnp.ones_like(top)
        code = jnp.full_like(top, 128.0)
        for bits in (64, 32, 16, 8):
            small = top < 2.0 ** (15 - bits)
            grow = jnp.where(small, 2.0**bits, 1.0)
            top = top * grow
            scale = scale * grow
            code = code * jnp.where(small, 2.0 ** (-(bits // 8)), 1.0)
        out_ref[rows_of(owner, rows), cols] = (part * scale).astype(BF)
        codes = jnp.where(line == owner, code, codes)
    out_ref[pl.ds(len(parts) * rows, CODE), cols] = codes.astype(BF)


def rows_of(owner, rows):
    return pl.ds(owner * rows if isinstance(owner, int) else pl.multiple_of(owner * rows, 16), rows)


def blocks_of(values, count):
    rows = values.shape[0] // count
    return [values[k * rows : (k + 1) * rows] for k in range(count)]


def owners_of(shards):
    y = lax.axis_index("y")
    return [lax.rem(y + (shards - k), shards) for k in distances(shards)]


def joined(pieces, rows, last=None):
    firsts = [piece.shape[0] - last if last else 0 for piece in pieces]
    return jnp.concatenate([piece[pl.ds(first, rows), :] for first, piece in zip(firsts, pieces, strict=True)], axis=0)


def load_scaled(in_ref, panel_ref, at, width, shards, rows):
    cols = pl.ds(at, width)
    count = in_ref.shape[0]
    for j in range(count):
        codes = in_ref[j, pl.ds(shards * rows, CODE), cols].astype(F32) * (1.0 / 128.0)
        codes = codes * codes
        codes = codes * codes
        codes = codes * codes
        for k in range(shards):
            undo = jnp.broadcast_to(codes[k : k + 1], (rows, width)).astype(BF)
            panel_ref[pl.ds((k * count + j) * rows, rows), cols] = in_ref[j, pl.ds(k * rows, rows), cols] * undo


def near_tile(halves, table, shards):
    part, width = halves[0].shape
    tile = part * len(halves)
    rows = tile // shards

    def kernel(*refs):
        above_refs, (table_ref, out_ref) = refs[: len(halves)], refs[len(halves) :]
        owners = owners_of(shards)
        for b in range(width // BLK):
            parts = []
            for ref in above_refs:
                near = lax.dot_general(
                    ref[:, pl.ds(b * BLK, BLK)], table_ref[b], (((1,), (1,)), ((), ())), preferred_element_type=F32
                )
                parts += blocks_of(near.astype(BF).astype(F32), part // rows)
            store_scaled(out_ref, parts, owners, b * BLK)

    return call(kernel, like(tile + CODE, width, BF), "near", [*halves, table], flops=2 * tile * width * BLK)


def reduced_tile(panel, factor, halves, shards):
    part, width = halves[0].shape
    tile = part * len(halves)
    depth, rows = factor[0].shape[1], tile // shards

    def kernel(panel_in, *refs):
        pieces, grad_refs, (out_ref, panel_ref) = refs[:shards], refs[shards:-2], refs[-2:]
        owners = owners_of(shards)
        for at, w in chunks_of(width):
            cols = pl.ds(at, w)
            load_scaled(panel_in, panel_ref, at, w, shards, rows)
            coupled = jnp.dot(joined(pieces, rows), panel_ref[:, cols], preferred_element_type=F32)
            grads = [ref[pl.ds(at_row, rows), cols] for ref in grad_refs for at_row in range(0, part, rows)]
            parts = [
                (grad.astype(F32) - block).astype(BF).astype(F32)
                for grad, block in zip(grads, blocks_of(coupled, shards), strict=True)
            ]
            store_scaled(out_ref, parts, owners, at)

    return call(
        kernel,
        like(tile + CODE, width, BF),
        "reduced",
        [panel, *factor, *halves],
        [pltpu.VMEM((depth, width), BF)],
        flops=2 * tile * depth * width,
    )


def halves_out(shards):
    order = distances(shards)
    order = order[1:] + order[:1]
    return order[: shards // 2], order[shards // 2 :]


def places_out(shards):
    halves = halves_out(shards)
    where = {k: (half, place) for half, ks in enumerate(halves) for place, k in enumerate(ks)}
    return [where[(shards - k) % shards] for k in distances(shards)]


def pushed_tile(panel, factor, inverse, coupling, shards):
    rows, depth = factor[0].shape[0] // 2, factor[0].shape[1]
    tile, width = shards * rows, panel.shape[2]

    def kernel(panel_in, inverse_ref, coupling_ref, *refs):
        pieces, (*pushed_refs, panel_ref) = refs[:shards], refs[shards:]
        carried = []
        for at, w in chunks_of(width):
            load_scaled(panel_in, panel_ref, at, w, shards, rows)
            both = jnp.dot(joined(pieces, rows, rows), panel_ref[:, pl.ds(at, w)], preferred_element_type=F32)
            carried += [both[:, i : i + BLK].astype(BF) for i in range(0, w, BLK)]
        middle = [
            jnp.dot(x, inverse_ref[b], preferred_element_type=F32).astype(BF) for b, x in enumerate(carried)
        ]
        for b, x in enumerate(middle):
            pushed = jnp.dot(x, coupling_ref[b], preferred_element_type=F32).astype(BF)
            for (half, place), part in zip(places_out(shards), blocks_of(pushed, shards), strict=True):
                pushed_refs[half][pl.ds(place * rows, rows), pl.ds(b * BLK, BLK)] = part

    return call(
        kernel,
        (*[like(tile // 2, width, BF)] * 2, like(depth, width, BF)),
        "pushed",
        [panel, inverse, coupling, *factor],
        flops=2 * tile * depth * width,
    )


def local_tile(panel, factor, inverse, shards):
    rows, depth = factor[0].shape[0] // 2, factor[0].shape[1]
    tile, width = shards * rows, panel.shape[1]

    def kernel(panel_ref, inverse_ref, *refs):
        pieces, local_refs = refs[:shards], refs[shards:]
        whitened = []
        for at, w in chunks_of(width):
            both = jnp.dot(joined(pieces, rows, 2 * rows), panel_ref[:, pl.ds(at, w)], preferred_element_type=F32)
            whitened += [both[:, i : i + BLK].astype(BF) for i in range(0, w, BLK)]
        for b, x in enumerate(whitened):
            product = jnp.dot(x, inverse_ref[b], preferred_element_type=F32)
            for (half, place), part in zip(places_out(shards), blocks_of(product, shards), strict=True):
                local_refs[half][pl.ds(place * rows, rows), pl.ds(b * BLK, BLK)] = part

    return call(
        kernel,
        (like(tile // 2, width, F32),) * 2,
        "local",
        [panel, inverse, *factor],
        flops=2 * tile * depth * width,
    )


def update_pieces(local_term, pushed, count, name):
    rows, width = pushed.shape[0] // count, pushed.shape[1]

    def kernel(local_ref, pushed_ref, *out_refs):
        for i, out_ref in enumerate(out_refs):
            here = pl.ds(i * rows, rows)
            out_ref[...] = (local_ref[here, :] - pushed_ref[here, :].astype(F32)).astype(BF)

    return call(kernel, tuple(like(rows, width, BF) for _ in range(count)), name, [local_term, pushed])


def copies(kernel, out, name, operands, count, near=HBM, far=VMEM):
    def body(*refs):
        sems = refs[-1]
        started = []
        for i, (source, target) in enumerate(kernel(*refs[:-1])):
            copy = pltpu.make_async_copy(source, target, sems.at[i])
            copy.start()
            started.append(copy)
        for copy in started:
            copy.wait()

    moved = 2 * sum(x.size * x.dtype.itemsize for x in jax.tree.leaves(out))
    return pl.pallas_call(
        body,
        out_shape=out,
        in_specs=[near] * len(operands),
        out_specs=jax.tree.map(lambda _: far, out),
        scratch_shapes=[pltpu.SemaphoreType.DMA((count,))],
        compiler_params=pltpu.CompilerParams(vmem_limit_bytes=16 << 20),
        cost_estimate=pl.CostEstimate(flops=0, bytes_accessed=moved, transcendentals=0),
        name=name,
    )(*[pltpu.with_memory_space_constraint(x, pltpu.HBM) if near is HBM else x for x in operands])


def column_blocks(gradient, shards):
    _, rows, width = gradient.shape
    width //= shards

    def kernel(grad_ref, *out_refs):
        y = lax.axis_index("y")
        for k, out_ref in zip(distances(shards), out_refs, strict=True):
            at = pl.multiple_of(lax.rem(y + k, shards) * width, BLK)
            yield grad_ref.at[0, :, pl.ds(at, width)], out_ref

    return copies(kernel, (like(rows, width, BF),) * shards, "blocks", [gradient], shards)


def operands(in_coupling, in_inverse, in_carry, out_inverse, out_coupling, shards):
    _, rows, width = in_inverse.shape
    blocks = out_inverse.shape[1] // shards
    table = jax.ShapeDtypeStruct((blocks, BLK, BLK), BF)

    def kernel(rows_ref, first_ref, second_ref, inverse_ref, coupling_ref, pair_ref, trio_ref, inv_ref, psi_ref):
        mine = pl.ds(lax.axis_index("y") * blocks, blocks)
        for i, ref in enumerate((rows_ref, first_ref, second_ref)):
            yield ref.at[0], trio_ref.at[pl.ds(i * rows, rows), :]
            if i:
                yield ref.at[0], pair_ref.at[pl.ds((i - 1) * rows, rows), :]
        yield coupling_ref.at[0, mine], psi_ref
        yield inverse_ref.at[0, mine], inv_ref

    out = (like(2 * rows, width, BF), like(3 * rows, width, BF), table, table)
    return copies(kernel, out, "operands", [in_coupling, in_inverse, in_carry, out_inverse, out_coupling], 7)


def stacked(pieces, name):
    rows, width = pieces[0].shape
    count = len(pieces)

    def kernel(*refs):
        for i in range(count):
            refs[count][pl.ds(i * rows, rows), :] = refs[i][...]

    return call(kernel, like(count * rows, width, BF), name, pieces)


def hop_y(x, by):
    size = lax.axis_size("y")
    return lax.ppermute(x, "y", [(i, (i + by) % size) for i in range(size)])


def distances(shards):
    return [0] + sorted(range(1, shards), key=lambda k: -min(k, shards - k))


def exchange(pieces):
    return [hop_y(piece, k) if k else piece for piece, k in zip(pieces, distances(len(pieces)), strict=True)]


def after(x, *others):
    return lax.optimization_barrier((x, *others))[0]


def join_columns(pieces):
    rows, width = pieces[0].shape
    shards = len(pieces)

    def kernel(*refs):
        for k, owner in enumerate(owners_of(shards)):
            yield refs[k], refs[shards].at[0, :, pl.ds(pl.multiple_of(owner * width, BLK), width)]

    out = jax.ShapeDtypeStruct((1, rows, shards * width), BF)
    return copies(kernel, out, "join", pieces, shards, near=VMEM, far=HBM)


def gather_panel(tile):
    return lax.all_gather(tile.astype(HALF), "z", axis=0).astype(BF)


def local(gradient, in_inverse, in_coupling, in_carry, out_inverse, out_coupling):
    shards = lax.axis_size("y")
    slices = column_blocks(gradient, shards)
    pieces = exchange(slices)
    first = after(in_coupling, slices[0])
    pair, trio, inv, psi = operands(first, in_inverse, in_carry, out_inverse, out_coupling, shards)
    grads = [stacked(lax.optimization_barrier((*pieces, pair))[:shards], "stacked")]
    above = [hop_layer(grad, -1) for grad in grads]
    pair, trio, own = lax.optimization_barrier((pair, trio, in_coupling[0], *grads))[:3]
    ahead, behind = hop_y(pair, 1), hop_y(trio, -1)
    coupling = [own, hop_y(own, 2), hop_y(own, 1), behind]
    near = near_tile(above, psi, shards)
    reduced = reduced_tile(gather_panel(near), coupling, grads, shards)
    factors = [pair, hop_y(behind, -1), ahead, behind]
    *pushed, panel = pushed_tile(gather_panel(reduced), factors, inv, psi, shards)
    pushed = [hop_layer(x, 1) for x in pushed]
    local_terms = local_tile(panel, factors, inv, shards)
    came = {}
    for ks, mine, below, name in zip(halves_out(shards), local_terms, pushed, ("update_a", "update_b"), strict=True):
        for k, piece in zip(ks, update_pieces(mine, below, len(ks), name), strict=True):
            came[k] = hop_y(piece, k) if k else piece
    return join_columns([came[k] for k in distances(shards)])


def solution(mesh):
    layers = mesh.shape["layer"]
    fine = Mesh(np.asarray(mesh.devices).reshape(layers, 4, -1), ("layer", "y", "z"))
    rows = P("layer", ("y", "z"), None)
    table = P("layer", None, None, None)
    return jax.shard_map(
        local,
        mesh=fine,
        in_specs=(rows, rows, rows, rows, table, table),
        out_specs=rows,
        check_vma=False,
    )
```

```python
import jax
import jax.numpy as jnp
import numpy as np
from jax import lax
from jax.experimental import pallas as pl
from jax.experimental.pallas import tpu as pltpu
from jax.sharding import Mesh, PartitionSpec as P

BF = jnp.bfloat16
F32 = jnp.float32
HALF = jnp.float16
BLK = 128
CODE = 8
VMEM = pl.BlockSpec(memory_space=pltpu.VMEM)
HBM = pl.BlockSpec(memory_space=pltpu.HBM)


def call(kernel, out, name, operands, scratch=(), mib=16, flops=0, far=()):
    moved = sum(x.size * x.dtype.itemsize for x in operands) + sum(x.size * x.dtype.itemsize for x in jax.tree.leaves(out))
    return pl.pallas_call(
        kernel,
        out_shape=out,
        in_specs=[HBM if i in far else VMEM for i in range(len(operands))],
        out_specs=jax.tree.map(lambda _: VMEM, out),
        scratch_shapes=list(scratch),
        compiler_params=pltpu.CompilerParams(vmem_limit_bytes=mib << 20),
        cost_estimate=pl.CostEstimate(flops=flops, bytes_accessed=moved, transcendentals=0),
        name=name,
    )(*operands)


def like(rows, cols, dtype):
    return jax.ShapeDtypeStruct((rows, cols), dtype)


def hop_layer(x, by):
    size = lax.axis_size("layer")
    return lax.ppermute(x, "layer", [(i, i + by) for i in range(size) if 0 <= i + by < size])


def chunks_of(width):
    return [(at, min(256, width - at)) for at in range(0, width, 256)]


def store_scaled(out_ref, parts, owners, at):
    rows, width = parts[0].shape
    cols = pl.ds(at, width)
    line = lax.broadcasted_iota(jnp.int32, (CODE, width), 0)
    codes = jnp.full((CODE, width), 1.0, F32)
    for part, owner in zip(parts, owners, strict=True):
        top = jnp.max(jnp.abs(part), axis=0, keepdims=True)
        scale = jnp.ones_like(top)
        code = jnp.full_like(top, 128.0)
        for bits in (64, 32, 16, 8):
            small = top < 2.0 ** (15 - bits)
            grow = jnp.where(small, 2.0**bits, 1.0)
            top = top * grow
            scale = scale * grow
            code = code * jnp.where(small, 2.0 ** (-(bits // 8)), 1.0)
        out_ref[rows_of(owner, rows), cols] = (part * scale).astype(BF)
        codes = jnp.where(line == owner, code, codes)
    out_ref[pl.ds(len(parts) * rows, CODE), cols] = codes.astype(BF)


def rows_of(owner, rows):
    return pl.ds(owner * rows if isinstance(owner, int) else pl.multiple_of(owner * rows, 16), rows)


def blocks_of(values, count):
    rows = values.shape[0] // count
    return [values[k * rows : (k + 1) * rows] for k in range(count)]


def owners_of(shards):
    y = lax.axis_index("y")
    return [lax.rem(y + (shards - k), shards) for k in distances(shards)]


def joined(pieces, rows, last=None):
    firsts = [piece.shape[0] - last if last else 0 for piece in pieces]
    return jnp.concatenate([piece[pl.ds(first, rows), :] for first, piece in zip(firsts, pieces, strict=True)], axis=0)


def load_scaled(in_ref, panel_ref, at, width, shards, rows):
    cols = pl.ds(at, width)
    count = in_ref.shape[0]
    for j in range(count):
        codes = in_ref[j, pl.ds(shards * rows, CODE), cols].astype(F32) * (1.0 / 128.0)
        codes = codes * codes
        codes = codes * codes
        codes = codes * codes
        for k in range(shards):
            undo = jnp.broadcast_to(codes[k : k + 1], (rows, width)).astype(BF)
            panel_ref[pl.ds((k * count + j) * rows, rows), cols] = in_ref[j, pl.ds(k * rows, rows), cols] * undo


def near_tile(halves, table, shards):
    part, width = halves[0].shape
    tile = part * len(halves)
    rows = tile // shards

    def kernel(*refs):
        above_refs, (table_ref, out_ref) = refs[: len(halves)], refs[len(halves) :]
        owners = owners_of(shards)
        for b in range(width // BLK):
            parts = []
            for ref in above_refs:
                near = lax.dot_general(
                    ref[:, pl.ds(b * BLK, BLK)], table_ref[b], (((1,), (1,)), ((), ())), preferred_element_type=F32
                )
                parts += blocks_of(near.astype(BF).astype(F32), part // rows)
            store_scaled(out_ref, parts, owners, b * BLK)

    return call(kernel, like(tile + CODE, width, BF), "near", [*halves, table], flops=2 * tile * width * BLK)


def reduced_tile(panel, factor, halves, shards):
    part, width = halves[0].shape
    tile = part * len(halves)
    depth, rows = factor[0].shape[1], tile // shards

    def kernel(panel_in, *refs):
        pieces, grad_refs, (out_ref, panel_ref) = refs[:shards], refs[shards:-2], refs[-2:]
        owners = owners_of(shards)
        for at, w in chunks_of(width):
            cols = pl.ds(at, w)
            load_scaled(panel_in, panel_ref, at, w, shards, rows)
            coupled = jnp.dot(joined(pieces, rows), panel_ref[:, cols], preferred_element_type=F32)
            grads = [ref[pl.ds(at_row, rows), cols] for ref in grad_refs for at_row in range(0, part, rows)]
            parts = [
                (grad.astype(F32) - block).astype(BF).astype(F32)
                for grad, block in zip(grads, blocks_of(coupled, shards), strict=True)
            ]
            store_scaled(out_ref, parts, owners, at)

    return call(
        kernel,
        like(tile + CODE, width, BF),
        "reduced",
        [panel, *factor, *halves],
        [pltpu.VMEM((depth, width), BF)],
        flops=2 * tile * depth * width,
    )


def halves_out(shards):
    order = distances(shards)
    order = order[1:] + order[:1]
    return order[: shards // 2], order[shards // 2 :]


def halves_of(factors):
    shards = len(factors)
    order = distances(shards)
    return [[factors[order.index((shards - k) % shards)] for k in ks] for ks in halves_out(shards)]


def product_rows(panel, pieces, tables, rows, last, kind, name, shards=0, below=None):
    depth, width = pieces[0].shape[1], panel.shape[-1]
    tile, count = len(pieces) * rows, len(pieces)
    operands_in = [panel, *pieces, *tables] + ([] if below is None else [below])

    def kernel(*refs):
        panel_in, piece_refs, table_refs = refs[0], refs[1 : 1 + count], refs[1 + count : 1 + count + len(tables)]
        out_refs = refs[len(operands_in) :]
        panel_ref = out_refs[-1] if shards else panel_in
        values = []
        for at, w in chunks_of(width):
            if shards:
                load_scaled(panel_in, panel_ref, at, w, shards, rows)
            both = jnp.dot(
                joined(piece_refs, rows, last * rows), panel_ref[:, pl.ds(at, w)], preferred_element_type=F32
            )
            values += [both[:, i : i + BLK] for i in range(0, w, BLK)]
        for table_ref in table_refs:
            values = [
                jnp.dot(x.astype(BF), table_ref[b], preferred_element_type=F32) for b, x in enumerate(values)
            ]
        for b, x in enumerate(values):
            cols = pl.ds(b * BLK, BLK)
            if below is None:
                out_refs[0][:, cols] = x.astype(kind)
            else:
                x = (x - refs[len(operands_in) - 1][:, cols].astype(F32)).astype(kind)
                for out_ref, part in zip(out_refs, blocks_of(x, count), strict=True):
                    out_ref[:, cols] = part

    out = like(tile, width, kind)
    if shards:
        out = (out, like(depth, width, BF))
    if below is not None:
        out = (like(rows, width, kind),) * count
    return call(kernel, out, name, operands_in, flops=2 * tile * depth * width)


def update_pieces(local_term, pushed, count, name):
    rows, width = pushed.shape[0] // count, pushed.shape[1]

    def kernel(local_ref, pushed_ref, *out_refs):
        for i, out_ref in enumerate(out_refs):
            here = pl.ds(i * rows, rows)
            out_ref[...] = (local_ref[here, :] - pushed_ref[here, :].astype(F32)).astype(BF)

    return call(kernel, tuple(like(rows, width, BF) for _ in range(count)), name, [local_term, pushed])


def copies(kernel, out, name, operands, count, near=HBM, far=VMEM):
    def body(*refs):
        sems = refs[-1]
        started = []
        for i, (source, target) in enumerate(kernel(*refs[:-1])):
            copy = pltpu.make_async_copy(source, target, sems.at[i])
            copy.start()
            started.append(copy)
        for copy in started:
            copy.wait()

    moved = 2 * sum(x.size * x.dtype.itemsize for x in jax.tree.leaves(out))
    return pl.pallas_call(
        body,
        out_shape=out,
        in_specs=[near] * len(operands),
        out_specs=jax.tree.map(lambda _: far, out),
        scratch_shapes=[pltpu.SemaphoreType.DMA((count,))],
        compiler_params=pltpu.CompilerParams(vmem_limit_bytes=16 << 20),
        cost_estimate=pl.CostEstimate(flops=0, bytes_accessed=moved, transcendentals=0),
        name=name,
    )(*[pltpu.with_memory_space_constraint(x, pltpu.HBM) if near is HBM else x for x in operands])


def column_blocks(gradient, shards):
    _, rows, width = gradient.shape
    width //= shards

    def kernel(grad_ref, *out_refs):
        y = lax.axis_index("y")
        for k, out_ref in zip(distances(shards), out_refs, strict=True):
            at = pl.multiple_of(lax.rem(y + k, shards) * width, BLK)
            yield grad_ref.at[0, :, pl.ds(at, width)], out_ref

    return copies(kernel, (like(rows, width, BF),) * shards, "blocks", [gradient], shards)


def operands(in_coupling, in_inverse, in_carry, out_inverse, out_coupling, shards):
    _, rows, width = in_inverse.shape
    blocks = out_inverse.shape[1] // shards
    table = jax.ShapeDtypeStruct((blocks, BLK, BLK), BF)

    def kernel(rows_ref, first_ref, second_ref, inverse_ref, coupling_ref, pair_ref, trio_ref, inv_ref, psi_ref):
        mine = pl.ds(lax.axis_index("y") * blocks, blocks)
        for i, ref in enumerate((rows_ref, first_ref, second_ref)):
            yield ref.at[0], trio_ref.at[pl.ds(i * rows, rows), :]
            if i:
                yield ref.at[0], pair_ref.at[pl.ds((i - 1) * rows, rows), :]
        yield coupling_ref.at[0, mine], psi_ref
        yield inverse_ref.at[0, mine], inv_ref

    out = (like(2 * rows, width, BF), like(3 * rows, width, BF), table, table)
    return copies(kernel, out, "operands", [in_coupling, in_inverse, in_carry, out_inverse, out_coupling], 7)


def stacked(pieces, name):
    rows, width = pieces[0].shape
    count = len(pieces)

    def kernel(*refs):
        for i in range(count):
            refs[count][pl.ds(i * rows, rows), :] = refs[i][...]

    return call(kernel, like(count * rows, width, BF), name, pieces)


def hop_y(x, by):
    size = lax.axis_size("y")
    return lax.ppermute(x, "y", [(i, (i + by) % size) for i in range(size)])


def distances(shards):
    return [0] + sorted(range(1, shards), key=lambda k: -min(k, shards - k))


def exchange(pieces):
    return [hop_y(piece, k) if k else piece for piece, k in zip(pieces, distances(len(pieces)), strict=True)]


def after(x, *others):
    return lax.optimization_barrier((x, *others))[0]


def join_columns(pieces):
    rows, width = pieces[0].shape
    shards = len(pieces)

    def kernel(*refs):
        for k, owner in enumerate(owners_of(shards)):
            yield refs[k], refs[shards].at[0, :, pl.ds(pl.multiple_of(owner * width, BLK), width)]

    out = jax.ShapeDtypeStruct((1, rows, shards * width), BF)
    return copies(kernel, out, "join", pieces, shards, near=VMEM, far=HBM)


def gather_panel(tile):
    return lax.all_gather(tile.astype(HALF), "z", axis=0).astype(BF)


def local(gradient, in_inverse, in_coupling, in_carry, out_inverse, out_coupling):
    shards = lax.axis_size("y")
    slices = column_blocks(gradient, shards)
    pieces = exchange(slices)
    first = after(in_coupling, slices[0])
    pair, trio, inv, psi = operands(first, in_inverse, in_carry, out_inverse, out_coupling, shards)
    grads = [stacked(lax.optimization_barrier((*pieces, pair))[:shards], "stacked")]
    above = [hop_layer(grad, -1) for grad in grads]
    pair, trio, own = lax.optimization_barrier((pair, trio, in_coupling[0], *grads))[:3]
    ahead, behind = hop_y(pair, 1), hop_y(trio, -1)
    coupling = [own, hop_y(own, 2), hop_y(own, 1), behind]
    near = near_tile(above, psi, shards)
    reduced = reduced_tile(gather_panel(near), coupling, grads, shards)
    factors = [pair, hop_y(behind, -1), ahead, behind]
    early, late = halves_of(factors)
    rows = own.shape[0]
    pushed_a, panel = product_rows(gather_panel(reduced), early, [inv, psi], rows, 1, BF, "pushed_a", shards)
    pushed_b = product_rows(panel, late, [inv, psi], rows, 1, BF, "pushed_b")
    below_a, below_b = hop_layer(pushed_a, 1), hop_layer(pushed_b, 1)
    local_a = product_rows(panel, early, [inv], rows, 2, F32, "local_a")
    pieces_a = update_pieces(local_a, below_a, len(early), "update_a")
    pieces_b = product_rows(panel, late, [inv], rows, 2, BF, "update_b", below=below_b)
    came = {}
    for ks, pieces in zip(halves_out(shards), (pieces_a, pieces_b), strict=True):
        for k, piece in zip(ks, pieces, strict=True):
            came[k] = hop_y(piece, k) if k else piece
    return join_columns([came[k] for k in distances(shards)])


def solution(mesh):
    layers = mesh.shape["layer"]
    fine = Mesh(np.asarray(mesh.devices).reshape(layers, 4, -1), ("layer", "y", "z"))
    rows = P("layer", ("y", "z"), None)
    table = P("layer", None, None, None)
    return jax.shard_map(
        local,
        mesh=fine,
        in_specs=(rows, rows, rows, rows, table, table),
        out_specs=rows,
        check_vma=False,
    )
```

```python
import jax
import jax.numpy as jnp
import numpy as np
from jax import lax
from jax.experimental import pallas as pl
from jax.experimental.pallas import tpu as pltpu
from jax.sharding import Mesh, PartitionSpec as P

BF = jnp.bfloat16
F32 = jnp.float32
HALF = jnp.float16
BLK = 128
CODE = 8
VMEM = pl.BlockSpec(memory_space=pltpu.VMEM)
HBM = pl.BlockSpec(memory_space=pltpu.HBM)


def call(kernel, out, name, operands, scratch=(), mib=16, flops=0, far=()):
    moved = sum(x.size * x.dtype.itemsize for x in operands) + sum(x.size * x.dtype.itemsize for x in jax.tree.leaves(out))
    return pl.pallas_call(
        kernel,
        out_shape=out,
        in_specs=[HBM if i in far else VMEM for i in range(len(operands))],
        out_specs=jax.tree.map(lambda _: VMEM, out),
        scratch_shapes=list(scratch),
        compiler_params=pltpu.CompilerParams(vmem_limit_bytes=mib << 20),
        cost_estimate=pl.CostEstimate(flops=flops, bytes_accessed=moved, transcendentals=0),
        name=name,
    )(*operands)


def like(rows, cols, dtype):
    return jax.ShapeDtypeStruct((rows, cols), dtype)


def hop_layer(x, by):
    size = lax.axis_size("layer")
    return lax.ppermute(x, "layer", [(i, i + by) for i in range(size) if 0 <= i + by < size])


def chunks_of(width):
    return [(at, min(256, width - at)) for at in range(0, width, 256)]


def store_scaled(out_ref, parts, owners, at):
    rows, width = parts[0].shape
    cols = pl.ds(at, width)
    line = lax.broadcasted_iota(jnp.int32, (CODE, width), 0)
    codes = jnp.full((CODE, width), 1.0, F32)
    for part, owner in zip(parts, owners, strict=True):
        top = jnp.max(jnp.abs(part), axis=0, keepdims=True)
        scale = jnp.ones_like(top)
        code = jnp.full_like(top, 128.0)
        for bits in (64, 32, 16, 8):
            small = top < 2.0 ** (15 - bits)
            grow = jnp.where(small, 2.0**bits, 1.0)
            top = top * grow
            scale = scale * grow
            code = code * jnp.where(small, 2.0 ** (-(bits // 8)), 1.0)
        out_ref[rows_of(owner, rows), cols] = (part * scale).astype(BF)
        codes = jnp.where(line == owner, code, codes)
    out_ref[pl.ds(len(parts) * rows, CODE), cols] = codes.astype(BF)


def rows_of(owner, rows):
    return pl.ds(owner * rows if isinstance(owner, int) else pl.multiple_of(owner * rows, 16), rows)


def blocks_of(values, count):
    rows = values.shape[0] // count
    return [values[k * rows : (k + 1) * rows] for k in range(count)]


def owners_of(shards):
    y = lax.axis_index("y")
    return [lax.rem(y + (shards - k), shards) for k in distances(shards)]


def joined(pieces, rows, last=None):
    firsts = [piece.shape[0] - last if last else 0 for piece in pieces]
    return jnp.concatenate([piece[pl.ds(first, rows), :] for first, piece in zip(firsts, pieces, strict=True)], axis=0)


def load_scaled(in_ref, panel_ref, at, width, shards, rows):
    cols = pl.ds(at, width)
    count = in_ref.shape[0]
    for j in range(count):
        codes = in_ref[j, pl.ds(shards * rows, CODE), cols].astype(F32) * (1.0 / 128.0)
        codes = codes * codes
        codes = codes * codes
        codes = codes * codes
        for k in range(shards):
            undo = jnp.broadcast_to(codes[k : k + 1], (rows, width)).astype(BF)
            panel_ref[pl.ds((k * count + j) * rows, rows), cols] = in_ref[j, pl.ds(k * rows, rows), cols] * undo


def near_tile(halves, table, shards):
    part, width = halves[0].shape
    tile = part * len(halves)
    rows = tile // shards

    def kernel(*refs):
        above_refs, (table_ref, out_ref) = refs[: len(halves)], refs[len(halves) :]
        owners = owners_of(shards)
        for b in range(width // BLK):
            parts = []
            for ref in above_refs:
                near = lax.dot_general(
                    ref[:, pl.ds(b * BLK, BLK)], table_ref[b], (((1,), (1,)), ((), ())), preferred_element_type=F32
                )
                parts += blocks_of(near.astype(BF).astype(F32), part // rows)
            store_scaled(out_ref, parts, owners, b * BLK)

    return call(kernel, like(tile + CODE, width, BF), "near", [*halves, table], flops=2 * tile * width * BLK)


def reduced_tile(panel, factor, halves, shards):
    part, width = halves[0].shape
    tile = part * len(halves)
    depth, rows = factor[0].shape[1], tile // shards

    def kernel(panel_in, *refs):
        pieces, grad_refs, (out_ref, panel_ref) = refs[:shards], refs[shards:-2], refs[-2:]
        owners = owners_of(shards)
        for at, w in chunks_of(width):
            cols = pl.ds(at, w)
            load_scaled(panel_in, panel_ref, at, w, shards, rows)
            coupled = jnp.dot(joined(pieces, rows), panel_ref[:, cols], preferred_element_type=F32)
            grads = [ref[pl.ds(at_row, rows), cols] for ref in grad_refs for at_row in range(0, part, rows)]
            parts = [
                (grad.astype(F32) - block).astype(BF).astype(F32)
                for grad, block in zip(grads, blocks_of(coupled, shards), strict=True)
            ]
            store_scaled(out_ref, parts, owners, at)

    return call(
        kernel,
        like(tile + CODE, width, BF),
        "reduced",
        [panel, *factor, *halves],
        [pltpu.VMEM((depth, width), BF)],
        flops=2 * tile * depth * width,
    )


def halves_out(shards):
    order = distances(shards)
    order = order[1:] + order[:1]
    return order[: shards // 2], order[shards // 2 :]


def halves_of(factors):
    shards = len(factors)
    order = distances(shards)
    return [[factors[order.index((shards - k) % shards)] for k in ks] for ks in halves_out(shards)]


def product_rows(panel, pieces, tables, rows, last, kind, name, shards=0, below=None):
    depth, width = pieces[0].shape[1], panel.shape[-1]
    tile, count = len(pieces) * rows, len(pieces)
    operands_in = [panel, *pieces, *tables] + ([] if below is None else [below])

    def kernel(*refs):
        panel_in, piece_refs, table_refs = refs[0], refs[1 : 1 + count], refs[1 + count : 1 + count + len(tables)]
        out_refs = refs[len(operands_in) :]
        panel_ref = out_refs[-1] if shards else panel_in
        values = []
        for at, w in chunks_of(width):
            if shards:
                load_scaled(panel_in, panel_ref, at, w, shards, rows)
            both = jnp.dot(
                joined(piece_refs, rows, last * rows), panel_ref[:, pl.ds(at, w)], preferred_element_type=F32
            )
            values += [both[:, i : i + BLK] for i in range(0, w, BLK)]
        for table_ref in table_refs:
            values = [
                jnp.dot(x.astype(BF), table_ref[b], preferred_element_type=F32) for b, x in enumerate(values)
            ]
        for b, x in enumerate(values):
            cols = pl.ds(b * BLK, BLK)
            if below is None:
                out_refs[0][:, cols] = x.astype(kind)
            else:
                x = (x - refs[len(operands_in) - 1][:, cols].astype(F32)).astype(kind)
                for out_ref, part in zip(out_refs, blocks_of(x, count), strict=True):
                    out_ref[:, cols] = part

    out = like(tile, width, kind)
    if shards:
        out = (out, like(depth, width, BF))
    if below is not None:
        out = (like(rows, width, kind),) * count
    return call(kernel, out, name, operands_in, flops=2 * tile * depth * width)


def update_pieces(local_term, pushed, count, name):
    rows, width = pushed.shape[0] // count, pushed.shape[1]

    def kernel(local_ref, pushed_ref, *out_refs):
        for i, out_ref in enumerate(out_refs):
            here = pl.ds(i * rows, rows)
            out_ref[...] = (local_ref[here, :] - pushed_ref[here, :].astype(F32)).astype(BF)

    return call(kernel, tuple(like(rows, width, BF) for _ in range(count)), name, [local_term, pushed])


def copies(kernel, out, name, operands, count, near=HBM, far=VMEM):
    def body(*refs):
        sems = refs[-1]
        started = []
        for i, (source, target) in enumerate(kernel(*refs[:-1])):
            copy = pltpu.make_async_copy(source, target, sems.at[i])
            copy.start()
            started.append(copy)
        for copy in started:
            copy.wait()

    moved = 2 * sum(x.size * x.dtype.itemsize for x in jax.tree.leaves(out))
    return pl.pallas_call(
        body,
        out_shape=out,
        in_specs=[near] * len(operands),
        out_specs=jax.tree.map(lambda _: far, out),
        scratch_shapes=[pltpu.SemaphoreType.DMA((count,))],
        compiler_params=pltpu.CompilerParams(vmem_limit_bytes=16 << 20),
        cost_estimate=pl.CostEstimate(flops=0, bytes_accessed=moved, transcendentals=0),
        name=name,
    )(*[pltpu.with_memory_space_constraint(x, pltpu.HBM) if near is HBM else x for x in operands])


def column_blocks(gradient, shards):
    _, rows, width = gradient.shape
    width //= shards

    def kernel(grad_ref, *out_refs):
        y = lax.axis_index("y")
        for k, out_ref in zip(distances(shards), out_refs, strict=True):
            at = pl.multiple_of(lax.rem(y + k, shards) * width, BLK)
            yield grad_ref.at[0, :, pl.ds(at, width)], out_ref

    return copies(kernel, (like(rows, width, BF),) * shards, "blocks", [gradient], shards)


def operands(in_coupling, in_inverse, in_carry, out_inverse, out_coupling, shards):
    _, rows, width = in_inverse.shape
    blocks = out_inverse.shape[1] // shards
    table = jax.ShapeDtypeStruct((blocks, BLK, BLK), BF)

    def kernel(rows_ref, first_ref, second_ref, inverse_ref, coupling_ref, pair_ref, trio_ref, inv_ref, psi_ref):
        mine = pl.ds(lax.axis_index("y") * blocks, blocks)
        for i, ref in enumerate((rows_ref, first_ref, second_ref)):
            yield ref.at[0], trio_ref.at[pl.ds(i * rows, rows), :]
            if i:
                yield ref.at[0], pair_ref.at[pl.ds((i - 1) * rows, rows), :]
        yield coupling_ref.at[0, mine], psi_ref
        yield inverse_ref.at[0, mine], inv_ref

    out = (like(2 * rows, width, BF), like(3 * rows, width, BF), table, table)
    return copies(kernel, out, "operands", [in_coupling, in_inverse, in_carry, out_inverse, out_coupling], 7)


def stacked(pieces, name):
    rows, width = pieces[0].shape
    count = len(pieces)

    def kernel(*refs):
        for i in range(count):
            refs[count][pl.ds(i * rows, rows), :] = refs[i][...]

    return call(kernel, like(count * rows, width, BF), name, pieces)


def hop_y(x, by):
    size = lax.axis_size("y")
    return lax.ppermute(x, "y", [(i, (i + by) % size) for i in range(size)])


def distances(shards):
    return [0] + sorted(range(1, shards), key=lambda k: -min(k, shards - k))


def exchange(pieces):
    return [hop_y(piece, k) if k else piece for piece, k in zip(pieces, distances(len(pieces)), strict=True)]


def after(x, *others):
    return lax.optimization_barrier((x, *others))[0]


def join_columns(pieces):
    rows, width = pieces[0].shape
    shards = len(pieces)

    def kernel(*refs):
        for k, owner in enumerate(owners_of(shards)):
            yield refs[k], refs[shards].at[0, :, pl.ds(pl.multiple_of(owner * width, BLK), width)]

    out = jax.ShapeDtypeStruct((1, rows, shards * width), BF)
    return copies(kernel, out, "join", pieces, shards, near=VMEM, far=HBM)


def gather_panel(tile):
    return lax.all_gather(tile.astype(HALF), "z", axis=0).astype(BF)


def local(gradient, in_inverse, in_coupling, in_carry, out_inverse, out_coupling):
    shards = lax.axis_size("y")
    slices = column_blocks(gradient, shards)
    pieces = exchange(slices)
    first = after(in_coupling, slices[0])
    pair, trio, inv, psi = operands(first, in_inverse, in_carry, out_inverse, out_coupling, shards)
    grads = [stacked(lax.optimization_barrier((*pieces, pair))[:shards], "stacked")]
    above = [hop_layer(grad, -1) for grad in grads]
    pair, trio, own = lax.optimization_barrier((pair, trio, in_coupling[0], *grads))[:3]
    ahead, behind = hop_y(trio, 1), hop_y(trio, -1)
    coupling = [own, hop_y(own, 2), ahead, behind]
    near = near_tile(above, psi, shards)
    reduced = reduced_tile(gather_panel(near), coupling, grads, shards)
    factors = [pair, hop_y(behind, -1), ahead, behind]
    early, late = halves_of(factors)
    rows = own.shape[0]
    pushed_a, panel = product_rows(gather_panel(reduced), early, [inv, psi], rows, 1, BF, "pushed_a", shards)
    pushed_b = product_rows(panel, late, [inv, psi], rows, 1, BF, "pushed_b")
    below_a, below_b = hop_layer(pushed_a, 1), hop_layer(pushed_b, 1)
    local_a = product_rows(panel, early, [inv], rows, 2, F32, "local_a")
    pieces_a = update_pieces(local_a, below_a, len(early), "update_a")
    pieces_b = product_rows(panel, late, [inv], rows, 2, BF, "update_b", below=below_b)
    came = {}
    for ks, pieces in zip(halves_out(shards), (pieces_a, pieces_b), strict=True):
        for k, piece in zip(ks, pieces, strict=True):
            came[k] = hop_y(piece, k) if k else piece
    return join_columns([came[k] for k in distances(shards)])


def solution(mesh):
    layers = mesh.shape["layer"]
    fine = Mesh(np.asarray(mesh.devices).reshape(layers, 4, -1), ("layer", "y", "z"))
    rows = P("layer", ("y", "z"), None)
    table = P("layer", None, None, None)
    return jax.shard_map(
        local,
        mesh=fine,
        in_specs=(rows, rows, rows, rows, table, table),
        out_specs=rows,
        check_vma=False,
    )
```

```python
import jax
import jax.numpy as jnp
import numpy as np
from jax import lax
from jax.experimental import pallas as pl
from jax.experimental.pallas import tpu as pltpu
from jax.sharding import Mesh, PartitionSpec as P

BF = jnp.bfloat16
F32 = jnp.float32
HALF = jnp.float16
BLK = 128
CODE = 8
VMEM = pl.BlockSpec(memory_space=pltpu.VMEM)
HBM = pl.BlockSpec(memory_space=pltpu.HBM)


def call(kernel, out, name, operands, scratch=(), mib=16, flops=0, far=()):
    moved = sum(x.size * x.dtype.itemsize for x in operands) + sum(x.size * x.dtype.itemsize for x in jax.tree.leaves(out))
    return pl.pallas_call(
        kernel,
        out_shape=out,
        in_specs=[HBM if i in far else VMEM for i in range(len(operands))],
        out_specs=jax.tree.map(lambda _: VMEM, out),
        scratch_shapes=list(scratch),
        compiler_params=pltpu.CompilerParams(vmem_limit_bytes=mib << 20),
        cost_estimate=pl.CostEstimate(flops=flops, bytes_accessed=moved, transcendentals=0),
        name=name,
    )(*operands)


def like(rows, cols, dtype):
    return jax.ShapeDtypeStruct((rows, cols), dtype)


def hop_layer(x, by):
    size = lax.axis_size("layer")
    return lax.ppermute(x, "layer", [(i, i + by) for i in range(size) if 0 <= i + by < size])


def chunks_of(width):
    return [(at, min(256, width - at)) for at in range(0, width, 256)]


def store_scaled(out_ref, parts, owners, at):
    rows, width = parts[0].shape
    cols = pl.ds(at, width)
    line = lax.broadcasted_iota(jnp.int32, (CODE, width), 0)
    codes = jnp.full((CODE, width), 1.0, F32)
    for part, owner in zip(parts, owners, strict=True):
        top = jnp.max(jnp.abs(part), axis=0, keepdims=True)
        scale = jnp.ones_like(top)
        code = jnp.full_like(top, 128.0)
        for bits in (64, 32, 16, 8):
            small = top < 2.0 ** (15 - bits)
            grow = jnp.where(small, 2.0**bits, 1.0)
            top = top * grow
            scale = scale * grow
            code = code * jnp.where(small, 2.0 ** (-(bits // 8)), 1.0)
        out_ref[rows_of(owner, rows), cols] = (part * scale).astype(BF)
        codes = jnp.where(line == owner, code, codes)
    out_ref[pl.ds(len(parts) * rows, CODE), cols] = codes.astype(BF)


def rows_of(owner, rows):
    return pl.ds(owner * rows if isinstance(owner, int) else pl.multiple_of(owner * rows, 16), rows)


def blocks_of(values, count):
    rows = values.shape[0] // count
    return [values[k * rows : (k + 1) * rows] for k in range(count)]


def owners_of(shards):
    y = lax.axis_index("y")
    return [lax.rem(y + (shards - k), shards) for k in distances(shards)]


def joined(pieces, rows, last=None):
    firsts = [piece.shape[0] - last if last else 0 for piece in pieces]
    return jnp.concatenate([piece[pl.ds(first, rows), :] for first, piece in zip(firsts, pieces, strict=True)], axis=0)


def load_scaled(in_ref, panel_ref, at, width, shards, rows):
    cols = pl.ds(at, width)
    count = in_ref.shape[0]
    for j in range(count):
        codes = in_ref[j, pl.ds(shards * rows, CODE), cols].astype(F32) * (1.0 / 128.0)
        codes = codes * codes
        codes = codes * codes
        codes = codes * codes
        for k in range(shards):
            undo = jnp.broadcast_to(codes[k : k + 1], (rows, width)).astype(BF)
            panel_ref[pl.ds((k * count + j) * rows, rows), cols] = in_ref[j, pl.ds(k * rows, rows), cols] * undo


def near_tile(halves, table, shards):
    part, width = halves[0].shape
    tile = part * len(halves)
    rows = tile // shards

    def kernel(*refs):
        above_refs, (table_ref, out_ref) = refs[: len(halves)], refs[len(halves) :]
        owners = owners_of(shards)
        for b in range(width // BLK):
            parts = []
            for ref in above_refs:
                near = lax.dot_general(
                    ref[:, pl.ds(b * BLK, BLK)], table_ref[b], (((1,), (1,)), ((), ())), preferred_element_type=F32
                )
                parts += blocks_of(near.astype(BF).astype(F32), part // rows)
            store_scaled(out_ref, parts, owners, b * BLK)

    return call(kernel, like(tile + CODE, width, BF), "near", [*halves, table], flops=2 * tile * width * BLK)


def reduced_tile(panel, factor, halves, shards):
    part, width = halves[0].shape
    tile = part * len(halves)
    depth, rows = factor[0].shape[1], tile // shards

    def kernel(panel_in, *refs):
        pieces, grad_refs, (out_ref, panel_ref) = refs[:shards], refs[shards:-2], refs[-2:]
        owners = owners_of(shards)
        for at, w in chunks_of(width):
            cols = pl.ds(at, w)
            load_scaled(panel_in, panel_ref, at, w, shards, rows)
            coupled = jnp.dot(joined(pieces, rows), panel_ref[:, cols], preferred_element_type=F32)
            grads = [ref[pl.ds(at_row, rows), cols] for ref in grad_refs for at_row in range(0, part, rows)]
            parts = [
                (grad.astype(F32) - block).astype(BF).astype(F32)
                for grad, block in zip(grads, blocks_of(coupled, shards), strict=True)
            ]
            store_scaled(out_ref, parts, owners, at)

    return call(
        kernel,
        like(tile + CODE, width, BF),
        "reduced",
        [panel, *factor, *halves],
        [pltpu.VMEM((depth, width), BF)],
        flops=2 * tile * depth * width,
    )


def halves_out(shards):
    order = distances(shards)
    order = order[1:] + order[:1]
    return order[: shards // 2], order[shards // 2 :]


def halves_of(factors):
    shards = len(factors)
    order = distances(shards)
    return [[factors[order.index((shards - k) % shards)] for k in ks] for ks in halves_out(shards)]


def product_rows(panel, pieces, tables, rows, last, kind, name, shards=0, below=None):
    depth, width = pieces[0].shape[1], panel.shape[-1]
    tile, count = len(pieces) * rows, len(pieces)
    operands_in = [panel, *pieces, *tables] + ([] if below is None else [below])

    def kernel(*refs):
        panel_in, piece_refs, table_refs = refs[0], refs[1 : 1 + count], refs[1 + count : 1 + count + len(tables)]
        out_refs = refs[len(operands_in) :]
        panel_ref = out_refs[-1] if shards else panel_in
        values = []
        for at, w in chunks_of(width):
            if shards:
                load_scaled(panel_in, panel_ref, at, w, shards, rows)
            both = jnp.dot(
                joined(piece_refs, rows, last * rows), panel_ref[:, pl.ds(at, w)], preferred_element_type=F32
            )
            values += [both[:, i : i + BLK] for i in range(0, w, BLK)]
        for table_ref in table_refs:
            values = [
                jnp.dot(x.astype(BF), table_ref[b], preferred_element_type=F32) for b, x in enumerate(values)
            ]
        for b, x in enumerate(values):
            cols = pl.ds(b * BLK, BLK)
            if below is None:
                out_refs[0][:, cols] = x.astype(kind)
            else:
                x = (x - refs[len(operands_in) - 1][:, cols].astype(F32)).astype(kind)
                for out_ref, part in zip(out_refs, blocks_of(x, count), strict=True):
                    out_ref[:, cols] = part

    out = like(tile, width, kind)
    if shards:
        out = (out, like(depth, width, BF))
    if below is not None:
        out = (like(rows, width, kind),) * count
    return call(kernel, out, name, operands_in, flops=2 * tile * depth * width)


def update_pieces(local_term, pushed, count, name):
    rows, width = pushed.shape[0] // count, pushed.shape[1]

    def kernel(local_ref, pushed_ref, *out_refs):
        for i, out_ref in enumerate(out_refs):
            here = pl.ds(i * rows, rows)
            out_ref[...] = (local_ref[here, :] - pushed_ref[here, :].astype(F32)).astype(BF)

    return call(kernel, tuple(like(rows, width, BF) for _ in range(count)), name, [local_term, pushed])


def copies(kernel, out, name, operands, count, near=HBM, far=VMEM):
    def body(*refs):
        sems = refs[-1]
        started = []
        for i, (source, target) in enumerate(kernel(*refs[:-1])):
            copy = pltpu.make_async_copy(source, target, sems.at[i])
            copy.start()
            started.append(copy)
        for copy in started:
            copy.wait()

    moved = 2 * sum(x.size * x.dtype.itemsize for x in jax.tree.leaves(out))
    return pl.pallas_call(
        body,
        out_shape=out,
        in_specs=[near] * len(operands),
        out_specs=jax.tree.map(lambda _: far, out),
        scratch_shapes=[pltpu.SemaphoreType.DMA((count,))],
        compiler_params=pltpu.CompilerParams(vmem_limit_bytes=16 << 20),
        cost_estimate=pl.CostEstimate(flops=0, bytes_accessed=moved, transcendentals=0),
        name=name,
    )(*[pltpu.with_memory_space_constraint(x, pltpu.HBM) if near is HBM else x for x in operands])


def column_blocks(gradient, shards):
    _, rows, width = gradient.shape
    width //= shards

    def kernel(grad_ref, *out_refs):
        y = lax.axis_index("y")
        for k, out_ref in zip(distances(shards), out_refs, strict=True):
            at = pl.multiple_of(lax.rem(y + k, shards) * width, BLK)
            yield grad_ref.at[0, :, pl.ds(at, width)], out_ref

    return copies(kernel, (like(rows, width, BF),) * shards, "blocks", [gradient], shards)


def operands(in_coupling, in_inverse, in_carry, out_inverse, out_coupling, shards):
    _, rows, width = in_inverse.shape
    blocks = out_inverse.shape[1] // shards
    table = jax.ShapeDtypeStruct((blocks, BLK, BLK), BF)

    def kernel(rows_ref, first_ref, second_ref, inverse_ref, coupling_ref, pair_ref, trio_ref, inv_ref, psi_ref):
        mine = pl.ds(lax.axis_index("y") * blocks, blocks)
        for i, ref in enumerate((rows_ref, first_ref, second_ref)):
            yield ref.at[0], trio_ref.at[pl.ds(i * rows, rows), :]
            if i:
                yield ref.at[0], pair_ref.at[pl.ds((i - 1) * rows, rows), :]
        yield coupling_ref.at[0, mine], psi_ref
        yield inverse_ref.at[0, mine], inv_ref

    out = (like(2 * rows, width, BF), like(3 * rows, width, BF), table, table)
    return copies(kernel, out, "operands", [in_coupling, in_inverse, in_carry, out_inverse, out_coupling], 7)


def stacked(pieces, name):
    rows, width = pieces[0].shape
    count = len(pieces)

    def kernel(*refs):
        for i in range(count):
            refs[count][pl.ds(i * rows, rows), :] = refs[i][...]

    return call(kernel, like(count * rows, width, BF), name, pieces)


def hop_y(x, by):
    size = lax.axis_size("y")
    return lax.ppermute(x, "y", [(i, (i + by) % size) for i in range(size)])


def distances(shards):
    return [0] + sorted(range(1, shards), key=lambda k: -min(k, shards - k))


def exchange(pieces):
    return [hop_y(piece, k) if k else piece for piece, k in zip(pieces, distances(len(pieces)), strict=True)]


def after(x, *others):
    return lax.optimization_barrier((x, *others))[0]


def join_columns(pieces):
    rows, width = pieces[0].shape
    shards = len(pieces)

    def kernel(*refs):
        for k, owner in enumerate(owners_of(shards)):
            yield refs[k], refs[shards].at[0, :, pl.ds(pl.multiple_of(owner * width, BLK), width)]

    out = jax.ShapeDtypeStruct((1, rows, shards * width), BF)
    return copies(kernel, out, "join", pieces, shards, near=VMEM, far=HBM)


def gather_panel(tile):
    return lax.all_gather(tile.astype(HALF), "z", axis=0).astype(BF)


def local(gradient, in_inverse, in_coupling, in_carry, out_inverse, out_coupling):
    shards = lax.axis_size("y")
    slices = column_blocks(gradient, shards)
    pieces = exchange(slices)
    first = after(in_coupling, slices[0])
    pair, trio, inv, psi = operands(first, in_inverse, in_carry, out_inverse, out_coupling, shards)
    grads = [stacked(lax.optimization_barrier((*pieces, pair))[:shards], "stacked")]
    above = [hop_layer(grad, -1) for grad in grads]
    pair, trio, own = lax.optimization_barrier((pair, trio, in_coupling[0], *grads))[:3]
    ahead, behind = hop_y(trio, 1), hop_y(trio, -1)
    coupling = [own, hop_y(own, 2), ahead, behind]
    near = near_tile(above, psi, shards)
    reduced = reduced_tile(gather_panel(near), coupling, grads, shards)
    factors = [pair, hop_y(pair, 2), ahead, behind]
    early, late = halves_of(factors)
    rows = own.shape[0]
    pushed_a, panel = product_rows(gather_panel(reduced), early, [inv, psi], rows, 1, BF, "pushed_a", shards)
    pushed_b = product_rows(panel, late, [inv, psi], rows, 1, BF, "pushed_b")
    below_a, below_b = hop_layer(pushed_a, 1), hop_layer(pushed_b, 1)
    local_a = product_rows(panel, early, [inv], rows, 2, F32, "local_a")
    pieces_a = update_pieces(local_a, below_a, len(early), "update_a")
    pieces_b = product_rows(panel, late, [inv], rows, 2, BF, "update_b", below=below_b)
    came = {}
    for ks, pieces in zip(halves_out(shards), (pieces_a, pieces_b), strict=True):
        for k, piece in zip(ks, pieces, strict=True):
            came[k] = hop_y(piece, k) if k else piece
    return join_columns([came[k] for k in distances(shards)])


def solution(mesh):
    layers = mesh.shape["layer"]
    fine = Mesh(np.asarray(mesh.devices).reshape(layers, 4, -1), ("layer", "y", "z"))
    rows = P("layer", ("y", "z"), None)
    table = P("layer", None, None, None)
    return jax.shard_map(
        local,
        mesh=fine,
        in_specs=(rows, rows, rows, rows, table, table),
        out_specs=rows,
        check_vma=False,
    )
```

```python
import jax
import jax.numpy as jnp
import numpy as np
from jax import lax
from jax.experimental import pallas as pl
from jax.experimental.pallas import tpu as pltpu
from jax.sharding import Mesh, PartitionSpec as P

BF = jnp.bfloat16
F32 = jnp.float32
HALF = jnp.float16
BLK = 128
CODE = 8
VMEM = pl.BlockSpec(memory_space=pltpu.VMEM)
HBM = pl.BlockSpec(memory_space=pltpu.HBM)


def call(kernel, out, name, operands, scratch=(), mib=16, flops=0, far=()):
    moved = sum(x.size * x.dtype.itemsize for x in operands) + sum(x.size * x.dtype.itemsize for x in jax.tree.leaves(out))
    return pl.pallas_call(
        kernel,
        out_shape=out,
        in_specs=[HBM if i in far else VMEM for i in range(len(operands))],
        out_specs=jax.tree.map(lambda _: VMEM, out),
        scratch_shapes=list(scratch),
        compiler_params=pltpu.CompilerParams(vmem_limit_bytes=mib << 20),
        cost_estimate=pl.CostEstimate(flops=flops, bytes_accessed=moved, transcendentals=0),
        name=name,
    )(*operands)


def like(rows, cols, dtype):
    return jax.ShapeDtypeStruct((rows, cols), dtype)


def hop_layer(x, by):
    size = lax.axis_size("layer")
    return lax.ppermute(x, "layer", [(i, i + by) for i in range(size) if 0 <= i + by < size])


def chunks_of(width):
    return [(at, min(256, width - at)) for at in range(0, width, 256)]


def store_scaled(out_ref, parts, owners, at):
    rows, width = parts[0].shape
    cols = pl.ds(at, width)
    line = lax.broadcasted_iota(jnp.int32, (CODE, width), 0)
    codes = jnp.full((CODE, width), 1.0, F32)
    for part, owner in zip(parts, owners, strict=True):
        top = jnp.max(jnp.abs(part), axis=0, keepdims=True)
        scale = jnp.ones_like(top)
        code = jnp.full_like(top, 128.0)
        for bits in (64, 32, 16, 8):
            small = top < 2.0 ** (15 - bits)
            grow = jnp.where(small, 2.0**bits, 1.0)
            top = top * grow
            scale = scale * grow
            code = code * jnp.where(small, 2.0 ** (-(bits // 8)), 1.0)
        out_ref[rows_of(owner, rows), cols] = (part * scale).astype(BF)
        codes = jnp.where(line == owner, code, codes)
    out_ref[pl.ds(len(parts) * rows, CODE), cols] = codes.astype(BF)


def rows_of(owner, rows):
    return pl.ds(owner * rows if isinstance(owner, int) else pl.multiple_of(owner * rows, 16), rows)


def blocks_of(values, count):
    rows = values.shape[0] // count
    return [values[k * rows : (k + 1) * rows] for k in range(count)]


def owners_of(shards):
    y = lax.axis_index("y")
    return [lax.rem(y + (shards - k), shards) for k in distances(shards)]


def joined(pieces, rows, last=None):
    firsts = [piece.shape[0] - last if last else 0 for piece in pieces]
    return jnp.concatenate([piece[pl.ds(first, rows), :] for first, piece in zip(firsts, pieces, strict=True)], axis=0)


def load_scaled(in_ref, panel_ref, at, width, shards, rows):
    cols = pl.ds(at, width)
    count = in_ref.shape[0]
    for j in range(count):
        codes = in_ref[j, pl.ds(shards * rows, CODE), cols].astype(F32) * (1.0 / 128.0)
        codes = codes * codes
        codes = codes * codes
        codes = codes * codes
        for k in range(shards):
            undo = jnp.broadcast_to(codes[k : k + 1], (rows, width)).astype(BF)
            panel_ref[pl.ds((k * count + j) * rows, rows), cols] = in_ref[j, pl.ds(k * rows, rows), cols] * undo


def near_tile(halves, table, shards):
    part, width = halves[0].shape
    tile = part * len(halves)
    rows = tile // shards

    def kernel(*refs):
        above_refs, (table_ref, out_ref) = refs[: len(halves)], refs[len(halves) :]
        owners = owners_of(shards)
        for b in range(width // BLK):
            parts = []
            for ref in above_refs:
                near = lax.dot_general(
                    ref[:, pl.ds(b * BLK, BLK)], table_ref[b], (((1,), (1,)), ((), ())), preferred_element_type=F32
                )
                parts += blocks_of(near.astype(BF).astype(F32), part // rows)
            store_scaled(out_ref, parts, owners, b * BLK)

    return call(kernel, like(tile + CODE, width, BF), "near", [*halves, table], flops=2 * tile * width * BLK)


def reduced_tile(panel, factor, halves, shards):
    part, width = halves[0].shape
    tile = part * len(halves)
    depth, rows = factor[0].shape[1], tile // shards

    def kernel(panel_in, *refs):
        pieces, grad_refs, (out_ref, panel_ref) = refs[:shards], refs[shards:-2], refs[-2:]
        owners = owners_of(shards)
        for at, w in chunks_of(width):
            cols = pl.ds(at, w)
            load_scaled(panel_in, panel_ref, at, w, shards, rows)
            coupled = jnp.dot(joined(pieces, rows), panel_ref[:, cols], preferred_element_type=F32)
            grads = [ref[pl.ds(at_row, rows), cols] for ref in grad_refs for at_row in range(0, part, rows)]
            parts = [
                (grad.astype(F32) - block).astype(BF).astype(F32)
                for grad, block in zip(grads, blocks_of(coupled, shards), strict=True)
            ]
            store_scaled(out_ref, parts, owners, at)

    return call(
        kernel,
        like(tile + CODE, width, BF),
        "reduced",
        [panel, *factor, *halves],
        [pltpu.VMEM((depth, width), BF)],
        flops=2 * tile * depth * width,
    )


def halves_out(shards):
    order = distances(shards)
    order = order[1:] + order[:1]
    return order[: shards // 2], order[shards // 2 :]


def halves_of(factors):
    shards = len(factors)
    order = distances(shards)
    return [[factors[order.index((shards - k) % shards)] for k in ks] for ks in halves_out(shards)]


def product_rows(panel, pieces, tables, rows, last, kind, name, shards=0, below=None):
    depth, width = pieces[0].shape[1], panel.shape[-1]
    tile, count = len(pieces) * rows, len(pieces)
    operands_in = [panel, *pieces, *tables] + ([] if below is None else [below])

    def kernel(*refs):
        panel_in, piece_refs, table_refs = refs[0], refs[1 : 1 + count], refs[1 + count : 1 + count + len(tables)]
        out_refs = refs[len(operands_in) :]
        panel_ref = out_refs[-1] if shards else panel_in
        values = []
        for at, w in chunks_of(width):
            if shards:
                load_scaled(panel_in, panel_ref, at, w, shards, rows)
            both = jnp.dot(
                joined(piece_refs, rows, last * rows), panel_ref[:, pl.ds(at, w)], preferred_element_type=F32
            )
            values += [both[:, i : i + BLK] for i in range(0, w, BLK)]
        for table_ref in table_refs:
            values = [
                jnp.dot(x.astype(BF), table_ref[b], preferred_element_type=F32) for b, x in enumerate(values)
            ]
        for b, x in enumerate(values):
            cols = pl.ds(b * BLK, BLK)
            if below is None:
                out_refs[0][:, cols] = x.astype(kind)
            else:
                x = (x - refs[len(operands_in) - 1][:, cols].astype(F32)).astype(kind)
                for out_ref, part in zip(out_refs, blocks_of(x, count), strict=True):
                    out_ref[:, cols] = part

    out = like(tile, width, kind)
    if shards:
        out = (out, like(depth, width, BF))
    if below is not None:
        out = (like(rows, width, kind),) * count
    return call(kernel, out, name, operands_in, flops=2 * tile * depth * width)


def update_pieces(local_term, pushed, count, name):
    rows, width = pushed.shape[0] // count, pushed.shape[1]

    def kernel(local_ref, pushed_ref, *out_refs):
        for i, out_ref in enumerate(out_refs):
            here = pl.ds(i * rows, rows)
            out_ref[...] = (local_ref[here, :] - pushed_ref[here, :].astype(F32)).astype(BF)

    return call(kernel, tuple(like(rows, width, BF) for _ in range(count)), name, [local_term, pushed])


def copies(kernel, out, name, operands, count, near=HBM, far=VMEM):
    def body(*refs):
        sems = refs[-1]
        started = []
        for i, (source, target) in enumerate(kernel(*refs[:-1])):
            copy = pltpu.make_async_copy(source, target, sems.at[i])
            copy.start()
            started.append(copy)
        for copy in started:
            copy.wait()

    moved = 2 * sum(x.size * x.dtype.itemsize for x in jax.tree.leaves(out))
    return pl.pallas_call(
        body,
        out_shape=out,
        in_specs=[near] * len(operands),
        out_specs=jax.tree.map(lambda _: far, out),
        scratch_shapes=[pltpu.SemaphoreType.DMA((count,))],
        compiler_params=pltpu.CompilerParams(vmem_limit_bytes=16 << 20),
        cost_estimate=pl.CostEstimate(flops=0, bytes_accessed=moved, transcendentals=0),
        name=name,
    )(*[pltpu.with_memory_space_constraint(x, pltpu.HBM) if near is HBM else x for x in operands])


def column_blocks(gradient, shards):
    _, rows, width = gradient.shape
    width //= shards

    def kernel(grad_ref, *out_refs):
        y = lax.axis_index("y")
        for k, out_ref in zip(distances(shards), out_refs, strict=True):
            at = pl.multiple_of(lax.rem(y + k, shards) * width, BLK)
            yield grad_ref.at[0, :, pl.ds(at, width)], out_ref

    return copies(kernel, (like(rows, width, BF),) * shards, "blocks", [gradient], shards)


def operands(in_coupling, in_inverse, in_carry, out_inverse, out_coupling, shards):
    _, rows, width = in_inverse.shape
    blocks = out_inverse.shape[1] // shards
    table = jax.ShapeDtypeStruct((blocks, BLK, BLK), BF)

    def kernel(rows_ref, first_ref, second_ref, inverse_ref, coupling_ref, pair_ref, trio_ref, inv_ref, psi_ref):
        mine = pl.ds(lax.axis_index("y") * blocks, blocks)
        for i, ref in enumerate((rows_ref, first_ref, second_ref)):
            yield ref.at[0], trio_ref.at[pl.ds(i * rows, rows), :]
            if i:
                yield ref.at[0], pair_ref.at[pl.ds((i - 1) * rows, rows), :]
        yield coupling_ref.at[0, mine], psi_ref
        yield inverse_ref.at[0, mine], inv_ref

    out = (like(2 * rows, width, BF), like(3 * rows, width, BF), table, table)
    return copies(kernel, out, "operands", [in_coupling, in_inverse, in_carry, out_inverse, out_coupling], 7)


def stacked(pieces, name):
    rows, width = pieces[0].shape
    count = len(pieces)

    def kernel(*refs):
        for i in range(count):
            refs[count][pl.ds(i * rows, rows), :] = refs[i][...]

    return call(kernel, like(count * rows, width, BF), name, pieces)


def hop_y(x, by):
    size = lax.axis_size("y")
    return lax.ppermute(x, "y", [(i, (i + by) % size) for i in range(size)])


def distances(shards):
    return [0] + sorted(range(1, shards), key=lambda k: -min(k, shards - k))


def exchange(pieces):
    return [hop_y(piece, k) if k else piece for piece, k in zip(pieces, distances(len(pieces)), strict=True)]


def after(x, *others):
    return lax.optimization_barrier((x, *others))[0]


def join_columns(pieces):
    rows, width = pieces[0].shape
    shards = len(pieces)

    def kernel(*refs):
        for k, owner in enumerate(owners_of(shards)):
            yield refs[k], refs[shards].at[0, :, pl.ds(pl.multiple_of(owner * width, BLK), width)]

    out = jax.ShapeDtypeStruct((1, rows, shards * width), BF)
    return copies(kernel, out, "join", pieces, shards, near=VMEM, far=HBM)


def gather_panel(tile):
    return lax.all_gather(tile.astype(HALF), "z", axis=0).astype(BF)


def local(gradient, in_inverse, in_coupling, in_carry, out_inverse, out_coupling):
    shards = lax.axis_size("y")
    slices = column_blocks(gradient, shards)
    pieces = exchange(slices)
    first = after(in_coupling, slices[0])
    pair, trio, inv, psi = operands(first, in_inverse, in_carry, out_inverse, out_coupling, shards)
    half = shards // 2
    grads = [stacked(lax.optimization_barrier((*pieces[:half], pair))[:half], "early"), stacked(pieces[half:], "late")]
    above = [hop_layer(grad, -1) for grad in grads]
    pair, trio, own = lax.optimization_barrier((pair, trio, in_coupling[0], *grads))[:3]
    ahead, behind = hop_y(trio, 1), hop_y(trio, -1)
    coupling = [own, hop_y(own, 2), ahead, behind]
    near = near_tile(above, psi, shards)
    reduced = reduced_tile(gather_panel(near), coupling, grads, shards)
    factors = [pair, hop_y(behind, -1), ahead, behind]
    early, late = halves_of(factors)
    rows = own.shape[0]
    pushed_a, panel = product_rows(gather_panel(reduced), early, [inv, psi], rows, 1, BF, "pushed_a", shards)
    pushed_b = product_rows(panel, late, [inv, psi], rows, 1, BF, "pushed_b")
    below_a, below_b = hop_layer(pushed_a, 1), hop_layer(pushed_b, 1)
    local_a = product_rows(panel, early, [inv], rows, 2, F32, "local_a")
    pieces_a = update_pieces(local_a, below_a, len(early), "update_a")
    pieces_b = product_rows(panel, late, [inv], rows, 2, BF, "update_b", below=below_b)
    came = {}
    for ks, pieces in zip(halves_out(shards), (pieces_a, pieces_b), strict=True):
        for k, piece in zip(ks, pieces, strict=True):
            came[k] = hop_y(piece, k) if k else piece
    return join_columns([came[k] for k in distances(shards)])


def solution(mesh):
    layers = mesh.shape["layer"]
    fine = Mesh(np.asarray(mesh.devices).reshape(layers, 4, -1), ("layer", "y", "z"))
    rows = P("layer", ("y", "z"), None)
    table = P("layer", None, None, None)
    return jax.shard_map(
        local,
        mesh=fine,
        in_specs=(rows, rows, rows, rows, table, table),
        out_specs=rows,
        check_vma=False,
    )
```

```python
import jax
import jax.numpy as jnp
import numpy as np
from jax import lax
from jax.experimental import pallas as pl
from jax.experimental.pallas import tpu as pltpu
from jax.sharding import Mesh, PartitionSpec as P

BF = jnp.bfloat16
F32 = jnp.float32
HALF = jnp.float16
BLK = 128
CODE = 8
VMEM = pl.BlockSpec(memory_space=pltpu.VMEM)
HBM = pl.BlockSpec(memory_space=pltpu.HBM)


def call(kernel, out, name, operands, scratch=(), mib=16, flops=0, far=()):
    moved = sum(x.size * x.dtype.itemsize for x in operands) + sum(x.size * x.dtype.itemsize for x in jax.tree.leaves(out))
    return pl.pallas_call(
        kernel,
        out_shape=out,
        in_specs=[HBM if i in far else VMEM for i in range(len(operands))],
        out_specs=jax.tree.map(lambda _: VMEM, out),
        scratch_shapes=list(scratch),
        compiler_params=pltpu.CompilerParams(vmem_limit_bytes=mib << 20),
        cost_estimate=pl.CostEstimate(flops=flops, bytes_accessed=moved, transcendentals=0),
        name=name,
    )(*operands)


def like(rows, cols, dtype):
    return jax.ShapeDtypeStruct((rows, cols), dtype)


def hop_layer(x, by):
    size = lax.axis_size("layer")
    return lax.ppermute(x, "layer", [(i, i + by) for i in range(size) if 0 <= i + by < size])


def chunks_of(width):
    return [(at, min(256, width - at)) for at in range(0, width, 256)]


def store_scaled(out_ref, parts, owners, at):
    rows, width = parts[0].shape
    cols = pl.ds(at, width)
    line = lax.broadcasted_iota(jnp.int32, (CODE, width), 0)
    codes = jnp.full((CODE, width), 1.0, F32)
    for part, owner in zip(parts, owners, strict=True):
        top = jnp.max(jnp.abs(part), axis=0, keepdims=True)
        scale = jnp.ones_like(top)
        code = jnp.full_like(top, 128.0)
        for bits in (64, 32, 16, 8):
            small = top < 2.0 ** (15 - bits)
            grow = jnp.where(small, 2.0**bits, 1.0)
            top = top * grow
            scale = scale * grow
            code = code * jnp.where(small, 2.0 ** (-(bits // 8)), 1.0)
        out_ref[rows_of(owner, rows), cols] = (part * scale).astype(BF)
        codes = jnp.where(line == owner, code, codes)
    out_ref[pl.ds(len(parts) * rows, CODE), cols] = codes.astype(BF)


def rows_of(owner, rows):
    return pl.ds(owner * rows if isinstance(owner, int) else pl.multiple_of(owner * rows, 16), rows)


def blocks_of(values, count):
    rows = values.shape[0] // count
    return [values[k * rows : (k + 1) * rows] for k in range(count)]


def owners_of(shards):
    y = lax.axis_index("y")
    return [lax.rem(y + (shards - k), shards) for k in distances(shards)]


def joined(pieces, rows, last=None):
    firsts = [piece.shape[0] - last if last else 0 for piece in pieces]
    return jnp.concatenate([piece[pl.ds(first, rows), :] for first, piece in zip(firsts, pieces, strict=True)], axis=0)


def load_scaled(in_ref, panel_ref, at, width, shards, rows):
    cols = pl.ds(at, width)
    count = in_ref.shape[0]
    for j in range(count):
        codes = in_ref[j, pl.ds(shards * rows, CODE), cols].astype(F32) * (1.0 / 128.0)
        codes = codes * codes
        codes = codes * codes
        codes = codes * codes
        for k in range(shards):
            undo = jnp.broadcast_to(codes[k : k + 1], (rows, width)).astype(BF)
            panel_ref[pl.ds((k * count + j) * rows, rows), cols] = in_ref[j, pl.ds(k * rows, rows), cols] * undo


def near_tile(halves, table, shards):
    part, width = halves[0].shape
    tile = part * len(halves)
    rows = tile // shards

    def kernel(*refs):
        above_refs, (table_ref, out_ref) = refs[: len(halves)], refs[len(halves) :]
        owners = owners_of(shards)
        for b in range(width // BLK):
            parts = []
            for ref in above_refs:
                near = lax.dot_general(
                    ref[:, pl.ds(b * BLK, BLK)], table_ref[b], (((1,), (1,)), ((), ())), preferred_element_type=F32
                )
                parts += blocks_of(near.astype(BF).astype(F32), part // rows)
            store_scaled(out_ref, parts, owners, b * BLK)

    return call(kernel, like(tile + CODE, width, BF), "near", [*halves, table], flops=2 * tile * width * BLK)


def reduced_tile(panel, factor, halves, shards):
    part, width = halves[0].shape
    tile = part * len(halves)
    depth, rows = factor[0].shape[1], tile // shards

    def kernel(panel_in, *refs):
        pieces, grad_refs, (out_ref, panel_ref) = refs[:shards], refs[shards:-2], refs[-2:]
        owners = owners_of(shards)
        for at, w in chunks_of(width):
            cols = pl.ds(at, w)
            load_scaled(panel_in, panel_ref, at, w, shards, rows)
            coupled = jnp.dot(joined(pieces, rows), panel_ref[:, cols], preferred_element_type=F32)
            grads = [ref[pl.ds(at_row, rows), cols] for ref in grad_refs for at_row in range(0, part, rows)]
            parts = [
                (grad.astype(F32) - block).astype(BF).astype(F32)
                for grad, block in zip(grads, blocks_of(coupled, shards), strict=True)
            ]
            store_scaled(out_ref, parts, owners, at)

    return call(
        kernel,
        like(tile + CODE, width, BF),
        "reduced",
        [panel, *factor, *halves],
        [pltpu.VMEM((depth, width), BF)],
        flops=2 * tile * depth * width,
    )


def halves_out(shards):
    order = distances(shards)
    order = order[1:] + order[:1]
    return order[: shards // 2], order[shards // 2 :]


def halves_of(factors):
    shards = len(factors)
    order = distances(shards)
    return [[factors[order.index((shards - k) % shards)] for k in ks] for ks in halves_out(shards)]


def product_rows(panel, pieces, tables, rows, last, kind, name, shards=0, below=None):
    depth, width = pieces[0].shape[1], panel.shape[-1]
    tile, count = len(pieces) * rows, len(pieces)
    operands_in = [panel, *pieces, *tables] + ([] if below is None else [below])

    def kernel(*refs):
        panel_in, piece_refs, table_refs = refs[0], refs[1 : 1 + count], refs[1 + count : 1 + count + len(tables)]
        out_refs = refs[len(operands_in) :]
        panel_ref = out_refs[-1] if shards else panel_in
        values = []
        for at, w in chunks_of(width):
            if shards:
                load_scaled(panel_in, panel_ref, at, w, shards, rows)
            both = jnp.dot(
                joined(piece_refs, rows, last * rows), panel_ref[:, pl.ds(at, w)], preferred_element_type=F32
            )
            values += [both[:, i : i + BLK] for i in range(0, w, BLK)]
        for table_ref in table_refs:
            values = [
                jnp.dot(x.astype(BF), table_ref[b], preferred_element_type=F32) for b, x in enumerate(values)
            ]
        for b, x in enumerate(values):
            cols = pl.ds(b * BLK, BLK)
            if below is None:
                out_refs[0][:, cols] = x.astype(kind)
            else:
                x = (x - refs[len(operands_in) - 1][:, cols].astype(F32)).astype(kind)
                for out_ref, part in zip(out_refs, blocks_of(x, count), strict=True):
                    out_ref[:, cols] = part

    out = like(tile, width, kind)
    if shards:
        out = (out, like(depth, width, BF))
    if below is not None:
        out = (like(rows, width, kind),) * count
    return call(kernel, out, name, operands_in, flops=2 * tile * depth * width)


def update_pieces(local_term, pushed, count, name):
    rows, width = pushed.shape[0] // count, pushed.shape[1]

    def kernel(local_ref, pushed_ref, *out_refs):
        for i, out_ref in enumerate(out_refs):
            here = pl.ds(i * rows, rows)
            out_ref[...] = (local_ref[here, :] - pushed_ref[here, :].astype(F32)).astype(BF)

    return call(kernel, tuple(like(rows, width, BF) for _ in range(count)), name, [local_term, pushed])


def copies(kernel, out, name, operands, count, near=HBM, far=VMEM):
    def body(*refs):
        sems = refs[-1]
        started = []
        for i, (source, target) in enumerate(kernel(*refs[:-1])):
            copy = pltpu.make_async_copy(source, target, sems.at[i])
            copy.start()
            started.append(copy)
        for copy in started:
            copy.wait()

    moved = 2 * sum(x.size * x.dtype.itemsize for x in jax.tree.leaves(out))
    return pl.pallas_call(
        body,
        out_shape=out,
        in_specs=[near] * len(operands),
        out_specs=jax.tree.map(lambda _: far, out),
        scratch_shapes=[pltpu.SemaphoreType.DMA((count,))],
        compiler_params=pltpu.CompilerParams(vmem_limit_bytes=16 << 20),
        cost_estimate=pl.CostEstimate(flops=0, bytes_accessed=moved, transcendentals=0),
        name=name,
    )(*[pltpu.with_memory_space_constraint(x, pltpu.HBM) if near is HBM else x for x in operands])


def column_blocks(gradient, shards):
    _, rows, width = gradient.shape
    width //= shards

    def kernel(grad_ref, *out_refs):
        y = lax.axis_index("y")
        for k, out_ref in zip(distances(shards), out_refs, strict=True):
            at = pl.multiple_of(lax.rem(y + k, shards) * width, BLK)
            yield grad_ref.at[0, :, pl.ds(at, width)], out_ref

    return copies(kernel, (like(rows, width, BF),) * shards, "blocks", [gradient], shards)


def operands(in_coupling, in_inverse, in_carry, out_inverse, out_coupling, shards):
    _, rows, width = in_inverse.shape
    blocks = out_inverse.shape[1] // shards
    table = jax.ShapeDtypeStruct((blocks, BLK, BLK), BF)

    def kernel(*refs):
        row_refs, (inverse_ref, coupling_ref, trio_ref, inv_ref, psi_ref) = refs[:3], refs[3:]
        mine = pl.ds(lax.axis_index("y") * blocks, blocks)
        for i, ref in enumerate(row_refs):
            yield ref.at[0], trio_ref.at[pl.ds(i * rows, rows), :]
        yield coupling_ref.at[0, mine], psi_ref
        yield inverse_ref.at[0, mine], inv_ref

    out = (like(3 * rows, width, BF), table, table)
    return copies(kernel, out, "operands", [in_coupling, in_inverse, in_carry, out_inverse, out_coupling], 5)


def stacked(pieces, name):
    rows, width = pieces[0].shape
    count = len(pieces)

    def kernel(*refs):
        for i in range(count):
            refs[count][pl.ds(i * rows, rows), :] = refs[i][...]

    return call(kernel, like(count * rows, width, BF), name, pieces)


def hop_y(x, by):
    size = lax.axis_size("y")
    return lax.ppermute(x, "y", [(i, (i + by) % size) for i in range(size)])


def distances(shards):
    return [0] + sorted(range(1, shards), key=lambda k: -min(k, shards - k))


def exchange(pieces):
    return [hop_y(piece, k) if k else piece for piece, k in zip(pieces, distances(len(pieces)), strict=True)]


def after(x, *others):
    return lax.optimization_barrier((x, *others))[0]


def join_columns(pieces):
    rows, width = pieces[0].shape
    shards = len(pieces)

    def kernel(*refs):
        for k, owner in enumerate(owners_of(shards)):
            yield refs[k], refs[shards].at[0, :, pl.ds(pl.multiple_of(owner * width, BLK), width)]

    out = jax.ShapeDtypeStruct((1, rows, shards * width), BF)
    return copies(kernel, out, "join", pieces, shards, near=VMEM, far=HBM)


def gather_panel(tile):
    return lax.all_gather(tile.astype(HALF), "z", axis=0).astype(BF)


def local(gradient, in_inverse, in_coupling, in_carry, out_inverse, out_coupling):
    shards = lax.axis_size("y")
    slices = column_blocks(gradient, shards)
    pieces = exchange(slices)
    first = after(in_coupling, slices[0])
    trio, inv, psi = operands(first, in_inverse, in_carry, out_inverse, out_coupling, shards)
    half = shards // 2
    grads = [stacked(lax.optimization_barrier((*pieces[:half], trio))[:half], "early"), stacked(pieces[half:], "late")]
    above = [hop_layer(grad, -1) for grad in grads]
    trio, own = lax.optimization_barrier((trio, in_coupling[0], *grads))[:2]
    ahead, behind = hop_y(trio, 1), hop_y(trio, -1)
    coupling = [trio, hop_y(own, 2), ahead, behind]
    near = near_tile(above, psi, shards)
    reduced = reduced_tile(gather_panel(near), coupling, grads, shards)
    factors = [trio, hop_y(behind, -1), ahead, behind]
    early, late = halves_of(factors)
    rows = own.shape[0]
    pushed_a, panel = product_rows(gather_panel(reduced), early, [inv, psi], rows, 1, BF, "pushed_a", shards)
    pushed_b = product_rows(panel, late, [inv, psi], rows, 1, BF, "pushed_b")
    below_a, below_b = hop_layer(pushed_a, 1), hop_layer(pushed_b, 1)
    local_a = product_rows(panel, early, [inv], rows, 2, F32, "local_a")
    pieces_a = update_pieces(local_a, below_a, len(early), "update_a")
    pieces_b = product_rows(panel, late, [inv], rows, 2, BF, "update_b", below=below_b)
    came = {}
    for ks, pieces in zip(halves_out(shards), (pieces_a, pieces_b), strict=True):
        for k, piece in zip(ks, pieces, strict=True):
            came[k] = hop_y(piece, k) if k else piece
    return join_columns([came[k] for k in distances(shards)])


def solution(mesh):
    layers = mesh.shape["layer"]
    fine = Mesh(np.asarray(mesh.devices).reshape(layers, 4, -1), ("layer", "y", "z"))
    rows = P("layer", ("y", "z"), None)
    table = P("layer", None, None, None)
    return jax.shard_map(
        local,
        mesh=fine,
        in_specs=(rows, rows, rows, rows, table, table),
        out_specs=rows,
        check_vma=False,
    )
```

```python
import jax
import jax.numpy as jnp
import numpy as np
from jax import lax
from jax.experimental import pallas as pl
from jax.experimental.pallas import tpu as pltpu
from jax.sharding import Mesh, PartitionSpec as P

BF = jnp.bfloat16
F32 = jnp.float32
HALF = jnp.float16
BLK = 128
CODE = 8
VMEM = pl.BlockSpec(memory_space=pltpu.VMEM)
HBM = pl.BlockSpec(memory_space=pltpu.HBM)


def call(kernel, out, name, operands, scratch=(), mib=16, flops=0, far=()):
    moved = sum(x.size * x.dtype.itemsize for x in operands) + sum(x.size * x.dtype.itemsize for x in jax.tree.leaves(out))
    return pl.pallas_call(
        kernel,
        out_shape=out,
        in_specs=[HBM if i in far else VMEM for i in range(len(operands))],
        out_specs=jax.tree.map(lambda _: VMEM, out),
        scratch_shapes=list(scratch),
        compiler_params=pltpu.CompilerParams(vmem_limit_bytes=mib << 20),
        cost_estimate=pl.CostEstimate(flops=flops, bytes_accessed=moved, transcendentals=0),
        name=name,
    )(*operands)


def like(rows, cols, dtype):
    return jax.ShapeDtypeStruct((rows, cols), dtype)


def hop_layer(x, by):
    size = lax.axis_size("layer")
    return lax.ppermute(x, "layer", [(i, i + by) for i in range(size) if 0 <= i + by < size])


def chunks_of(width):
    return [(at, min(256, width - at)) for at in range(0, width, 256)]


def store_scaled(out_ref, parts, owners, at):
    rows, width = parts[0].shape
    cols = pl.ds(at, width)
    line = lax.broadcasted_iota(jnp.int32, (CODE, width), 0)
    codes = jnp.full((CODE, width), 1.0, F32)
    for part, owner in zip(parts, owners, strict=True):
        top = jnp.max(jnp.abs(part), axis=0, keepdims=True)
        scale = jnp.ones_like(top)
        code = jnp.full_like(top, 128.0)
        for bits in (64, 32, 16, 8):
            small = top < 2.0 ** (15 - bits)
            grow = jnp.where(small, 2.0**bits, 1.0)
            top = top * grow
            scale = scale * grow
            code = code * jnp.where(small, 2.0 ** (-(bits // 8)), 1.0)
        out_ref[rows_of(owner, rows), cols] = (part * scale).astype(BF)
        codes = jnp.where(line == owner, code, codes)
    out_ref[pl.ds(len(parts) * rows, CODE), cols] = codes.astype(BF)


def rows_of(owner, rows):
    return pl.ds(owner * rows if isinstance(owner, int) else pl.multiple_of(owner * rows, 16), rows)


def blocks_of(values, count):
    rows = values.shape[0] // count
    return [values[k * rows : (k + 1) * rows] for k in range(count)]


def owners_of(shards):
    y = lax.axis_index("y")
    return [lax.rem(y + (shards - k), shards) for k in distances(shards)]


def joined(pieces, rows, last=None):
    firsts = [piece.shape[0] - last if last else 0 for piece in pieces]
    return jnp.concatenate([piece[pl.ds(first, rows), :] for first, piece in zip(firsts, pieces, strict=True)], axis=0)


def load_scaled(in_ref, panel_ref, at, width, shards, rows):
    cols = pl.ds(at, width)
    count = in_ref.shape[0]
    for j in range(count):
        codes = in_ref[j, pl.ds(shards * rows, CODE), cols].astype(F32) * (1.0 / 128.0)
        codes = codes * codes
        codes = codes * codes
        codes = codes * codes
        for k in range(shards):
            undo = jnp.broadcast_to(codes[k : k + 1], (rows, width)).astype(BF)
            panel_ref[pl.ds((k * count + j) * rows, rows), cols] = in_ref[j, pl.ds(k * rows, rows), cols] * undo


def near_tile(halves, table, shards):
    part, width = halves[0].shape
    tile = part * len(halves)
    rows = tile // shards

    def kernel(*refs):
        above_refs, (table_ref, out_ref) = refs[: len(halves)], refs[len(halves) :]
        owners = owners_of(shards)
        for b in range(width // BLK):
            parts = []
            for ref in above_refs:
                near = lax.dot_general(
                    ref[:, pl.ds(b * BLK, BLK)], table_ref[b], (((1,), (1,)), ((), ())), preferred_element_type=F32
                )
                parts += blocks_of(near.astype(BF).astype(F32), part // rows)
            store_scaled(out_ref, parts, owners, b * BLK)

    return call(kernel, like(tile + CODE, width, BF), "near", [*halves, table], flops=2 * tile * width * BLK)


def reduced_tile(panel, factor, halves, shards):
    part, width = halves[0].shape
    tile = part * len(halves)
    depth, rows = factor[0].shape[1], tile // shards

    def kernel(panel_in, *refs):
        pieces, grad_refs, (out_ref, panel_ref) = refs[:shards], refs[shards:-2], refs[-2:]
        owners = owners_of(shards)
        for at, w in chunks_of(width):
            cols = pl.ds(at, w)
            load_scaled(panel_in, panel_ref, at, w, shards, rows)
            coupled = jnp.dot(joined(pieces, rows), panel_ref[:, cols], preferred_element_type=F32)
            grads = [ref[pl.ds(at_row, rows), cols] for ref in grad_refs for at_row in range(0, part, rows)]
            parts = [
                (grad.astype(F32) - block).astype(BF).astype(F32)
                for grad, block in zip(grads, blocks_of(coupled, shards), strict=True)
            ]
            store_scaled(out_ref, parts, owners, at)

    return call(
        kernel,
        like(tile + CODE, width, BF),
        "reduced",
        [panel, *factor, *halves],
        [pltpu.VMEM((depth, width), BF)],
        flops=2 * tile * depth * width,
    )


def halves_out(shards):
    order = distances(shards)
    order = order[1:] + order[:1]
    return order[: shards // 2], order[shards // 2 :]


def halves_of(factors):
    shards = len(factors)
    order = distances(shards)
    return [[factors[order.index((shards - k) % shards)] for k in ks] for ks in halves_out(shards)]


def product_rows(panel, pieces, tables, rows, last, kind, name, shards=0, below=None):
    depth, width = pieces[0].shape[1], panel.shape[-1]
    tile, count = len(pieces) * rows, len(pieces)
    operands_in = [panel, *pieces, *tables] + ([] if below is None else [below])

    def kernel(*refs):
        panel_in, piece_refs, table_refs = refs[0], refs[1 : 1 + count], refs[1 + count : 1 + count + len(tables)]
        out_refs = refs[len(operands_in) :]
        panel_ref = out_refs[-1] if shards else panel_in
        values = []
        for at, w in chunks_of(width):
            if shards:
                load_scaled(panel_in, panel_ref, at, w, shards, rows)
            both = jnp.dot(
                joined(piece_refs, rows, last * rows), panel_ref[:, pl.ds(at, w)], preferred_element_type=F32
            )
            values += [both[:, i : i + BLK] for i in range(0, w, BLK)]
        for table_ref in table_refs:
            values = [
                jnp.dot(x.astype(BF), table_ref[b], preferred_element_type=F32) for b, x in enumerate(values)
            ]
        for b, x in enumerate(values):
            cols = pl.ds(b * BLK, BLK)
            if below is None:
                out_refs[0][:, cols] = x.astype(kind)
            else:
                x = (x - refs[len(operands_in) - 1][:, cols].astype(F32)).astype(kind)
                for out_ref, part in zip(out_refs, blocks_of(x, count), strict=True):
                    out_ref[:, cols] = part

    out = like(tile, width, kind)
    if shards:
        out = (out, like(depth, width, BF))
    if below is not None:
        out = (like(rows, width, kind),) * count
    return call(kernel, out, name, operands_in, flops=2 * tile * depth * width)


def update_pieces(local_term, pushed, count, name):
    rows, width = pushed.shape[0] // count, pushed.shape[1]

    def kernel(local_ref, pushed_ref, *out_refs):
        for i, out_ref in enumerate(out_refs):
            here = pl.ds(i * rows, rows)
            out_ref[...] = (local_ref[here, :] - pushed_ref[here, :].astype(F32)).astype(BF)

    return call(kernel, tuple(like(rows, width, BF) for _ in range(count)), name, [local_term, pushed])


def copies(kernel, out, name, operands, count, near=HBM, far=VMEM):
    def body(*refs):
        sems = refs[-1]
        started = []
        for i, (source, target) in enumerate(kernel(*refs[:-1])):
            copy = pltpu.make_async_copy(source, target, sems.at[i])
            copy.start()
            started.append(copy)
        for copy in started:
            copy.wait()

    moved = 2 * sum(x.size * x.dtype.itemsize for x in jax.tree.leaves(out))
    return pl.pallas_call(
        body,
        out_shape=out,
        in_specs=[near] * len(operands),
        out_specs=jax.tree.map(lambda _: far, out),
        scratch_shapes=[pltpu.SemaphoreType.DMA((count,))],
        compiler_params=pltpu.CompilerParams(vmem_limit_bytes=16 << 20),
        cost_estimate=pl.CostEstimate(flops=0, bytes_accessed=moved, transcendentals=0),
        name=name,
    )(*[pltpu.with_memory_space_constraint(x, pltpu.HBM) if near is HBM else x for x in operands])


def column_blocks(gradient, shards):
    _, rows, width = gradient.shape
    width //= shards

    def kernel(grad_ref, *out_refs):
        y = lax.axis_index("y")
        for k, out_ref in zip(distances(shards), out_refs, strict=True):
            at = pl.multiple_of(lax.rem(y + k, shards) * width, BLK)
            yield grad_ref.at[0, :, pl.ds(at, width)], out_ref

    return copies(kernel, (like(rows, width, BF),) * shards, "blocks", [gradient], shards)


def operands(in_coupling, in_inverse, in_carry, out_inverse, out_coupling, shards):
    _, rows, width = in_inverse.shape
    blocks = out_inverse.shape[1] // shards
    table = jax.ShapeDtypeStruct((blocks, BLK, BLK), BF)

    def kernel(*refs):
        row_refs, (inverse_ref, coupling_ref, trio_ref, inv_ref, psi_ref) = refs[:3], refs[3:]
        mine = pl.ds(lax.axis_index("y") * blocks, blocks)
        for i, ref in enumerate(row_refs):
            yield ref.at[0], trio_ref.at[pl.ds(i * rows, rows), :]
        yield coupling_ref.at[0, mine], psi_ref
        yield inverse_ref.at[0, mine], inv_ref

    out = (like(3 * rows, width, BF), table, table)
    return copies(kernel, out, "operands", [in_coupling, in_inverse, in_carry, out_inverse, out_coupling], 5)


def stacked(pieces, name):
    rows, width = pieces[0].shape
    count = len(pieces)

    def kernel(*refs):
        for i in range(count):
            refs[count][pl.ds(i * rows, rows), :] = refs[i][...]

    return call(kernel, like(count * rows, width, BF), name, pieces)


def hop_y(x, by):
    size = lax.axis_size("y")
    return lax.ppermute(x, "y", [(i, (i + by) % size) for i in range(size)])


def distances(shards):
    return [0] + sorted(range(1, shards), key=lambda k: -min(k, shards - k))


def exchange(pieces):
    return [hop_y(piece, k) if k else piece for piece, k in zip(pieces, distances(len(pieces)), strict=True)]


def after(x, *others):
    return lax.optimization_barrier((x, *others))[0]


def join_columns(pieces):
    rows, width = pieces[0].shape
    shards = len(pieces)

    def kernel(*refs):
        for k, owner in enumerate(owners_of(shards)):
            yield refs[k], refs[shards].at[0, :, pl.ds(pl.multiple_of(owner * width, BLK), width)]

    out = jax.ShapeDtypeStruct((1, rows, shards * width), BF)
    return copies(kernel, out, "join", pieces, shards, near=VMEM, far=HBM)


def gather_panel(tile):
    return lax.all_gather(tile.astype(HALF), "z", axis=0).astype(BF)


def local(gradient, in_inverse, in_coupling, in_carry, out_inverse, out_coupling):
    shards = lax.axis_size("y")
    slices = column_blocks(gradient, shards)
    pieces = exchange(slices)
    first = after(in_coupling, slices[0])
    trio, inv, psi = operands(first, in_inverse, in_carry, out_inverse, out_coupling, shards)
    half = shards // 2
    grads = [stacked(lax.optimization_barrier((*pieces[:half], trio))[:half], "early"), stacked(pieces[half:], "late")]
    above = [hop_layer(grad, -1) for grad in grads]
    trio = after(trio, *grads)
    own = trio[: in_coupling.shape[1]]
    ahead, behind = hop_y(trio, 1), hop_y(trio, -1)
    coupling = [trio, hop_y(own, 2), ahead, behind]
    near = near_tile(above, psi, shards)
    reduced = reduced_tile(gather_panel(near), coupling, grads, shards)
    factors = [trio, hop_y(behind, -1), ahead, behind]
    early, late = halves_of(factors)
    rows = own.shape[0]
    pushed_a, panel = product_rows(gather_panel(reduced), early, [inv, psi], rows, 1, BF, "pushed_a", shards)
    pushed_b = product_rows(panel, late, [inv, psi], rows, 1, BF, "pushed_b")
    below_a, below_b = hop_layer(pushed_a, 1), hop_layer(pushed_b, 1)
    local_a = product_rows(panel, early, [inv], rows, 2, F32, "local_a")
    pieces_a = update_pieces(local_a, below_a, len(early), "update_a")
    pieces_b = product_rows(panel, late, [inv], rows, 2, BF, "update_b", below=below_b)
    came = {}
    for ks, pieces in zip(halves_out(shards), (pieces_a, pieces_b), strict=True):
        for k, piece in zip(ks, pieces, strict=True):
            came[k] = hop_y(piece, k) if k else piece
    return join_columns([came[k] for k in distances(shards)])


def solution(mesh):
    layers = mesh.shape["layer"]
    fine = Mesh(np.asarray(mesh.devices).reshape(layers, 4, -1), ("layer", "y", "z"))
    rows = P("layer", ("y", "z"), None)
    table = P("layer", None, None, None)
    return jax.shard_map(
        local,
        mesh=fine,
        in_specs=(rows, rows, rows, rows, table, table),
        out_specs=rows,
        check_vma=False,
    )
```
